256 devices in a mesh: gz: 16 (over x, z_hi), gy: 4 (over z_lo, core), gx: 4 (over y).
Axes of the slice: x: 4, y: 4, z: 8 (z_hi: 4, z_lo: 2; z = z_hi * 2 + z_lo), core: 2. Of those that a mesh axis runs over, the one named last changes fastest.
Arguments:
- grid_input: bfloat16 [128, 64, 8192], P('gz', 'gy', 'gx'), may hold values from -6 to 6
- pre_one: bfloat16 [128, 64, 8192], P('gz', 'gy', 'gx'), may hold values from -5.875 to 4.125
- pre_two: bfloat16 [128, 64, 8192], P('gz', 'gy', 'gx'), may hold values from -8 to 8
- grad_output: bfloat16 [128, 64, 8192], P('gz', 'gy', 'gx'), may hold values from -6 to 6
- spectral_one: bfloat16 [16, 16, 16, 4096], P('gz', 'gy', 'gx'), may hold values from -1.5 to 1.5
- spectral_two: bfloat16 [16, 16, 16, 4096], P('gz', 'gy', 'gx'), may hold values from -1.5 to 1.5
- point_one: bfloat16 [64, 64], replicated, may hold values from -0.75 to 0.75
- point_two: bfloat16 [64, 64], replicated, may hold values from -0.75 to 0.75
Outputs:
- input_grad: bfloat16 [128, 64, 8192], P('gz', 'gy', 'gx')
- spectral_grad_one: float32 [16, 16, 16, 4096], P('gz', 'gy', 'gx')
- spectral_grad_two: float32 [16, 16, 16, 4096], P('gz', 'gy', 'gx')
- point_grad_one: float32 [64, 64], replicated
- point_grad_two: float32 [64, 64], replicated
The draws below stay inside these ranges and needn't reach their ends.
All inputs are finite; a program needn't handle non-finite values.
Results may differ from the reference program's by a relative error of at most 0.012.
Values sent between devices are 32-bit elements; how exact they have to be, the bound alone decides.
No kernel may reach another device: no remote copies, remote signals or barrier semaphores. Data moves between devices by JAX's collectives and lax.ppermute only.
A program may use at most 64 MiB of HBM per device.

```python
import math
import jax
import jax.numpy as jnp
from jax import lax

C = 64
MX = 16
MY = 16
MZ = 16
CX = 8
CY = 16
CZ = 32
NX = 128
NY = 64
NZ = 128


def draw_pre_one(key, part):
    values = jax.random.normal(key, (NX, NY, NZ * C), jnp.float32)
    return (jnp.clip(values, -5.0, 5.0) - 0.875).astype(jnp.bfloat16)


def block_levels(rng, shape, pieces, least, top_value):
    def one(dim, shards_of):
        heights = jax.random.uniform(jax.random.fold_in(jax.random.fold_in(rng, 6), dim), (shards_of,), jnp.float32, least / len(pieces), top_value / len(pieces))
        return jnp.repeat(jnp.exp(heights), shape[dim] // shards_of).reshape((-1,) + (1,) * (len(shape) - dim - 1))

    gain = one(*pieces[0])
    for cut in pieces[1:]:
        gain = gain * one(*cut)
    return gain


def noise(key, shape, width, limit, cuts=(), kind=jnp.bfloat16):
    loudness = block_levels(key, shape, cuts, -0.22, 0.18) if cuts else 1.0
    values = jax.random.normal(key, shape, jnp.float32) * width * loudness
    return jnp.minimum(jnp.maximum(values, -limit), limit).astype(kind)


def setup_inputs(seed: int = 0) -> dict:
    streams_of = jax.random.split(jax.random.key(seed), 9)
    return {
        "grid_input": noise(streams_of[0], (NX, NY, NZ * C), 1.0, 6.0, ((0, 16), (1, 4), (2, 4))),
        "pre_one": draw_pre_one(jax.random.fold_in(streams_of[8], 71), 0),
        "pre_two": noise(streams_of[2], (NX, NY, NZ * C), 1.5, 8.0, ((0, 16), (1, 4), (2, 4))),
        "grad_output": noise(streams_of[3], (NX, NY, NZ * C), 1.0, 6.0, ((0, 16), (1, 4), (2, 4))),
        "spectral_one": noise(streams_of[4], (MX, MY, MZ, C * C), (C // 4) ** -0.5, 1.5, ((0, 16), (1, 4), (2, 4))),
        "spectral_two": noise(streams_of[5], (MX, MY, MZ, C * C), (C // 4) ** -0.5, 1.5, ((0, 16), (1, 4), (2, 4))),
        "point_one": noise(streams_of[6], (C, C), C ** -0.5, 0.75),
        "point_two": noise(streams_of[7], (C, C), C ** -0.5, 0.75),
    }


highest = lax.Precision.HIGHEST
inv_root_two = 0.7071067811865476
inv_root_tau = 0.3989422804014327


def frequency_list(mode_count, length):
    position = jnp.arange(mode_count, dtype=jnp.int32)
    return jnp.where(position < mode_count // 2, position, length - mode_count + position).astype(jnp.int32)


def cell_positions(cell_count, device_count):
    rows = jnp.arange(cell_count * device_count, dtype=jnp.int32)
    return ((rows % cell_count) * device_count + rows // cell_count).astype(jnp.int32)


def cas_table(mode_count, length, positions):
    frequency = frequency_list(mode_count, length)
    product = (frequency[:, None] * positions[None, :]) % length
    phase = product.astype(jnp.float32) * (2.0 * math.pi / length)
    return (jnp.cos(phase) + jnp.sin(phase)).astype(jnp.bfloat16)


def gelu_value(pre_value):
    return pre_value * 0.5 * (1.0 + jax.scipy.special.erf(pre_value * inv_root_two))


def gelu_slope(pre_value):
    normal_cdf = 0.5 * (1.0 + jax.scipy.special.erf(pre_value * inv_root_two))
    return normal_cdf + pre_value * jnp.exp(-0.5 * pre_value * pre_value) * inv_root_tau


def analyse(values, tables):
    table_x, table_y, table_z = [t.astype(jnp.float32) for t in tables]
    along_z = jnp.einsum('xyzc,kz->xykc', values.astype(jnp.float32), table_z, precision=highest)
    along_y = jnp.einsum('xykc,jy->xjkc', along_z, table_y, precision=highest)
    return jnp.einsum('xjkc,ix->ijkc', along_y, table_x, precision=highest)


def synthesise(spectra, tables):
    table_x, table_y, table_z = [t.astype(jnp.float32) for t in tables]
    along_z = jnp.einsum('ijkc,kz->ijzc', spectra, table_z, precision=highest)
    along_y = jnp.einsum('ijzc,jy->iyzc', along_z, table_y, precision=highest)
    return jnp.einsum('iyzc,ix->xyzc', along_y, table_x, precision=highest)


def layer_back(layer_in, pre_act, upstream, spectral, point, tables, scales):
    analysis, synthesis, cell_scale = scales
    channels = point.shape[0]
    pre_grad = (upstream * gelu_slope(pre_act.astype(jnp.float32))).astype(jnp.bfloat16)
    hat_in = analysis * analyse(layer_in, tables)
    hat_grad = synthesis * analyse(pre_grad, tables)
    weights = spectral.astype(jnp.float32).reshape(hat_in.shape + (channels,))
    spec_grad = (hat_in[..., :, None] * hat_grad[..., None, :]).reshape(spectral.shape)
    hat_back = jnp.einsum('ijkao,ijko->ijka', weights, hat_grad, precision=highest)
    flat_in = layer_in.reshape(-1, channels)
    flat_grad = pre_grad.reshape(-1, channels)
    point_grad = cell_scale * jnp.dot(flat_in.T, flat_grad, preferred_element_type=jnp.float32)
    local_term = jnp.dot(flat_grad, point.T, preferred_element_type=jnp.float32).reshape(layer_in.shape)
    down = analysis * synthesise(hat_back, tables) + local_term
    return down, spec_grad, point_grad


def reference(grid_input, pre_one, pre_two, grad_output, spectral_one, spectral_two, point_one, point_two):
    shape_four = (NX, NY, NZ, C)
    tables = (cas_table(MX, NX, cell_positions(CX, NX // CX)),
              cas_table(MY, NY, cell_positions(CY, NY // CY)),
              cas_table(MZ, NZ, cell_positions(CZ, NZ // CZ)))
    total_cells = NX * NY * NZ
    total_modes = MX * MY * MZ
    scales = ((total_cells * total_modes) ** -0.25, total_cells ** -0.5, total_cells ** -0.5)
    first_in = grid_input.reshape(shape_four)
    first_pre = pre_one.reshape(shape_four)
    second_pre = pre_two.reshape(shape_four)
    upstream = grad_output.reshape(shape_four).astype(jnp.float32)
    middle = gelu_value(first_pre.astype(jnp.float32)).astype(jnp.bfloat16)
    down_two, spec_two, grad_two = layer_back(middle, second_pre, upstream, spectral_two, point_two, tables, scales)
    down_one, spec_one, grad_one = layer_back(first_in, first_pre, down_two, spectral_one, point_one, tables, scales)
    input_grad = down_one.astype(jnp.bfloat16).reshape(NX, NY, NZ * C)
    return (input_grad, spec_one, spec_two, grad_one, grad_two)
```

```python
import jax
import jax.numpy as jnp
import numpy as np
from jax import lax
from jax.experimental import pallas as pl
from jax.experimental.pallas import tpu as pltpu
from jax.sharding import PartitionSpec as P

INTERPRET = False

C = 64
CELLS_X, CELLS_Y, CELLS_Z = 8, 16, 32
DEV_X, DEV_Y, DEV_Z = 16, 4, 4
ROWS = CELLS_X * CELLS_Y
WIDE = CELLS_Z * C
TOTAL_CELLS = CELLS_X * DEV_X * CELLS_Y * DEV_Y * CELLS_Z * DEV_Z
TOTAL_MODES = 16**3
SCALE_A = (TOTAL_CELLS * TOTAL_MODES) ** (-0.25)
SCALE_B = TOTAL_CELLS ** (-0.5)

inv_root_two = 0.7071067811865476
inv_root_tau = 0.3989422804014327
bf16 = jnp.bfloat16
f32 = jnp.float32


def cas(mode, length, position):
    mode = np.asarray(mode)
    freq = np.where(mode < 8, mode, length - 16 + mode)
    phase = (freq * position % length) * (2.0 * np.pi / length)
    return (np.cos(phase) + np.sin(phase)).astype(np.float32)


def build_tables():
    four = np.arange(4)
    z = np.arange(CELLS_Z)
    tz = np.zeros((DEV_Z, CELLS_Z, 16), np.float32)
    for d in range(DEV_Z):
        modes = (((d + four) % 4)[:, None] * 4 + four[None, :]).reshape(-1)
        tz[d] = cas(modes[None, :], CELLS_Z * DEV_Z, z[:, None] * DEV_Z + d)
    tz = np.repeat(tz, C, axis=2)
    y = np.arange(CELLS_Y)
    ty = np.zeros((DEV_Y, 4, CELLS_X, 4, CELLS_X, CELLS_Y), np.float32)
    for d in range(DEV_Y):
        modes = ((d + four) % 4)[:, None] * 4 + four[None, :]
        small = cas(modes[:, :, None], CELLS_Y * DEV_Y, y * DEV_Y + d)
        for x in range(CELLS_X):
            ty[d, :, x, :, x, :] = small
    ty = ty.reshape(DEV_Y, ROWS, ROWS)
    x = np.arange(CELLS_X)
    tx = np.zeros((DEV_X, 4, 4, 4, CELLS_X, 4), np.float32)
    turn = np.zeros((DEV_X, 4, 4, 4, 64), np.float32)
    for d in range(DEV_X):
        modes = ((d // 4 + four) % 4)[:, None] * 4 + (d % 4 + four[None, :]) % 4
        small = cas(modes[:, :, None], CELLS_X * DEV_X, x * DEV_X + d)
        for l in range(4):
            tx[d, :, :, l, :, l] = small
            for i in range(4):
                for j in range(4):
                    turn[d, i, j, l, modes[i, j] * 4 + l] = 1.0
    tx = tx.reshape(DEV_X, 64, CELLS_X * 4)
    turn = turn.reshape(DEV_X, 64, 64)
    fold = (np.arange(C * C)[:, None] // C == np.arange(C)[None, :]).astype(np.float32)
    return tuple(t.astype(bf16) for t in (tz, ty, tx, turn, fold))


def dot(left, right):
    return jnp.dot(left, right, preferred_element_type=f32)


def dot_nt(left, right):
    return lax.dot_general(left, right, (((1,), (1,)), ((), ())), preferred_element_type=f32)


def dot_tn(left, right):
    return lax.dot_general(left, right, (((0,), (0,)), ((), ())), preferred_element_type=f32)


def split(v):
    high = v.astype(bf16)
    return high, (v - high.astype(f32)).astype(bf16)


def table_dot(table, v):
    high, low = split(v)
    return dot(table, high) + dot(table, low)


def table_dot_tn(table, v):
    high, low = split(v)
    return dot_tn(table, high) + dot_tn(table, low)


def slope_of(v, cdf):
    return cdf + v * jnp.exp(-0.5 * v * v) * inv_root_tau


def cdf_of(v):
    return 0.5 * (1.0 + lax.erf(v * inv_root_two))


def call(body, outs, *args, smem=0):
    specs = [
        pl.BlockSpec(memory_space=pltpu.SMEM if i < smem else pltpu.VMEM) for i in range(len(args))
    ]
    return pl.pallas_call(
        body,
        out_shape=[jax.ShapeDtypeStruct(s, d) for s, d in outs],
        in_specs=specs,
        out_specs=[pl.BlockSpec(memory_space=pltpu.VMEM)] * len(outs),
        interpret=INTERPRET,
        name=body.__name__,
    )(*args)


def store_parts(v, refs, width):
    for j, ref in enumerate(refs):
        ref[...] = v[:, j * width : (j + 1) * width]


def start_kernel(at, pre, grad, tz, dz, ka, *parts):
    lane = lax.broadcasted_iota(jnp.int32, (C, 16 * C), 1) & (C - 1)
    row = lax.broadcasted_iota(jnp.int32, (C, 16 * C), 0)
    eye = jnp.where(lane == row, 1.0, 0.0).astype(bf16)
    mine = tz[at[0]]
    for z in range(CELLS_Z):
        ka[z * C : (z + 1) * C, :] = eye * mine[z : z + 1, :]
    for b in range(8):
        cut = slice(b * 256, (b + 1) * 256)
        v = pre[:, cut].astype(f32)
        dz[:, cut] = (grad[:, cut].astype(f32) * slope_of(v, cdf_of(v))).astype(bf16)
    store_parts(dot(dz[...], ka[...]), parts, 256)


def weight_grad(left, right):
    total = dot_tn(left[:, :256], right[:, :256])
    for b in range(1, 8):
        cut = slice(b * 256, (b + 1) * 256)
        total = total + dot_tn(left[:, cut], right[:, cut])
    return sum(total[i * C : (i + 1) * C, i * C : (i + 1) * C] for i in range(4))


def side_kernel(pre, first, dz, ka, point, slope, local, weight, mid, *parts):
    for b in range(8):
        cut = slice(b * 256, (b + 1) * 256)
        v = pre[:, cut].astype(f32)
        cdf = cdf_of(v)
        slope[:, cut] = slope_of(v, cdf)
        mid[:, cut] = (v * cdf).astype(bf16)
        local[:, cut] = dot(dz[:, cut], point[...])
    weight[...] = weight_grad(mid, dz)
    table = ka[...]
    mids = dot(mid[...], table)
    firsts = dot(first[...], table)
    for j, ref in enumerate(parts):
        ref[:, :256] = mids[:, j * 256 : (j + 1) * 256]
        ref[:, 256:] = firsts[:, j * 256 : (j + 1) * 256]


def side_one_kernel(first, dz, point, weight_two, turn, local, sent):
    for b in range(8):
        cut = slice(b * 256, (b + 1) * 256)
        local[:, cut] = dot(dz[:, cut], point[...])
    both = jnp.concatenate([weight_two[...], weight_grad(first, dz)], axis=1) * SCALE_B
    turned = table_dot(turn[...], both)
    sent[...] = jnp.concatenate([turned[:32], turned[32:]], axis=1)


def total_of(refs):
    return (refs[0][...] + refs[1][...]) + (refs[2][...] + refs[3][...])


def along_y_kernel(a, b, c, d, ty, *parts):
    out = table_dot(ty[...], total_of((a, b, c, d)))
    for j, ref in enumerate(parts):
        ref[...] = out[j * 32 : (j + 1) * 32]


def along_y_join_kernel(a, b, c, d, ty, ins0, ins1, ins2, ins3, sent, *parts):
    out = table_dot(ty[...], total_of((a, b, c, d)))
    ins = (ins0, ins1, ins2, ins3)
    for j, ref in enumerate(parts):
        ref[:, :256] = out[j * 32 : (j + 1) * 32]
        ref[:, 256:768] = ins[j][...]
        ref[:, 768:] = sent[...]


def along_x_kernel(a, b, c, d, tx, *parts):
    v = total_of((a, b, c, d))
    if v.shape[1] == 1024:
        weight = jnp.concatenate([v[:, 768:896], v[:, 896:]], axis=0)
        v = v[:, :768]
    else:
        weight = None
    out = table_dot(tx[...], v)
    for j, ref in enumerate(parts):
        if weight is None:
            ref[...] = out[j * 16 : (j + 1) * 16]
        else:
            ref[:, :768] = out[j * 16 : (j + 1) * 16]
            ref[:, 768:] = weight[j * 16 : (j + 1) * 16]


def halves_kernel(a, b, c, d, *parts):
    v = total_of((a, b, c, d))
    for j, ref in enumerate(parts):
        ref[...] = v[j * 4 : (j + 1) * 4]


def mixed(hat, weights, fold):
    pieces = []
    for k in range(4):
        h = hat[:, k * C : (k + 1) * C]
        pieces.append(jnp.concatenate([h, h], axis=1))
    tall = jnp.concatenate(pieces, axis=0)
    product = weights[...] * jnp.concatenate([tall] * 32, axis=1)
    high, low = split(product)
    out = dot(jnp.concatenate([high, low], axis=0), fold[...])
    out = (out[:16] + out[16:]) * SCALE_A
    return jnp.concatenate([out[k * 4 : (k + 1) * 4] for k in range(4)], axis=1)


def mix_two_kernel(a, b, c, d, weights, fold, back, hat_out):
    hat = total_of((a, b, c, d)) * SCALE_B
    hat_out[...] = hat
    back[...] = mixed(hat, weights, fold)


def mix_one_kernel(a, b, c, d, weights, fold, back, hat_out, mid_out, first_out):
    v = total_of((a, b, c, d))
    hat = v[:, :256] * SCALE_B
    hat_out[...] = hat
    mid_out[...] = v[:, 256:512] * SCALE_A
    first_out[...] = v[:, 512:768] * SCALE_A
    back[:, :256] = mixed(hat, weights, fold)
    back[:, 256:] = v[:, 768:]


def outer_kernel(left, right, fold, out):
    lefts = []
    rights = []
    for k in range(4):
        cut = slice(k * C, (k + 1) * C)
        h = right[:, cut]
        lefts.append(left[:, cut])
        rights.append(jnp.concatenate([h, h], axis=1))
    v = jnp.concatenate(lefts, axis=0)
    high, rest = v.astype(bf16), v - v.astype(bf16).astype(f32)
    low, last = split(rest)
    spread_left = dot_nt(jnp.concatenate([high, low, last], axis=0), fold[...])
    tall = jnp.concatenate(rights, axis=0)
    whole = (spread_left[:16] + spread_left[16:32]) + spread_left[32:]
    out[...] = whole * jnp.concatenate([tall] * 32, axis=1)


def stack_kernel(a, b, c, d, out):
    for j, ref in enumerate((a, b, c, d)):
        out[j * 4 : (j + 1) * 4] = ref[...]


def back_x_kernel(a, b, c, d, tx, out):
    v = jnp.concatenate([a[...], b[...], c[...], d[...]], axis=0)
    out[...] = table_dot_tn(tx[...], v)


def back_x_one_kernel(a, b, c, d, tx, out, weight):
    v = jnp.concatenate([a[...], b[...], c[...], d[...]], axis=0)
    out[...] = table_dot_tn(tx[...], v[:, :256])
    weight[...] = jnp.concatenate([v[:32, 256:], v[32:, 256:]], axis=1)


def back_y_kernel(a, b, c, d, ty, out):
    v = jnp.concatenate([a[...], b[...], c[...], d[...]], axis=0)
    out[...] = table_dot_tn(ty[...], v)


def back_y_one_kernel(a, b, c, d, ty, weight, out):
    v = jnp.concatenate([a[...], b[...], c[...], d[...]], axis=0)
    out[:ROWS] = table_dot_tn(ty[...], v)
    out[ROWS:] = weight[...]


def down_of(refs, ka, local):
    v = jnp.concatenate([r[:ROWS] for r in refs], axis=1)
    high, low = split(v)
    table = ka[...]
    return (dot_nt(high, table) + dot_nt(low, table)) + local[...]


def middle_kernel(a, b, c, d, ka, local, slope, dz, *parts):
    down = down_of((a, b, c, d), ka, local)
    dz[...] = (down * slope[...]).astype(bf16)
    store_parts(dot(dz[...], ka[...]), parts, 256)


def end_kernel(a, b, c, d, ka, local, turn, out, weight):
    out[...] = down_of((a, b, c, d), ka, local).astype(bf16)
    w = (a[ROWS:] + b[ROWS:]) + (c[ROWS:] + d[ROWS:])
    w = jnp.concatenate([w[:, :128], w[:, 128:]], axis=0)
    weight[...] = table_dot_tn(turn[...], w)


def shift_pairs(kind, s):
    if kind == "x":
        return "gz", [(i, (i // 4 + s) % 4 * 4 + i % 4) for i in range(16)]
    if kind == "z":
        return "gz", [(i, i // 4 * 4 + (i % 4 + s) % 4) for i in range(16)]
    return kind, [(i, (i + s) % 4) for i in range(4)]


def shifted(v, kind, s):
    axis, pairs = shift_pairs(kind, s)
    return lax.ppermute(v, axis, pairs)


def exchange(parts, kind):
    with jax.named_scope("reduce_" + kind):
        return [parts[0]] + [shifted(parts[s], kind, s) for s in (1, 2, 3)]


def spread(v, kind):
    with jax.named_scope("spread_" + kind):
        return [v] + [shifted(v, kind, s) for s in (3, 2, 1)]


def by_kz(weights):
    w = weights.reshape(4, 4, C * C).transpose(1, 0, 2).reshape(16, C * C)
    return w.astype(f32)


def by_ky(values):
    return values.reshape(4, 4, C * C).transpose(1, 0, 2).reshape(1, 4, 4, C * C)


def on_device(
    grid_input, pre_one, pre_two, grad_output, spectral_one, spectral_two, point_one, point_two
):
    tz, ty, tx, turn, fold = [jnp.asarray(t) for t in build_tables()]
    ix, iy, iz = (lax.axis_index(n) for n in ("gz", "gy", "gx"))
    ty, tx, turn = [
        lax.dynamic_index_in_dim(t, i, 0, keepdims=False) for t, i in ((ty, iy), (tx, ix), (turn, ix))
    ]
    first, pre_one, pre_two, upstream = [
        t.reshape(ROWS, WIDE) for t in (grid_input, pre_one, pre_two, grad_output)
    ]
    eye = jnp.eye(4, dtype=bf16)
    point_one, point_two = [
        (eye[:, None, :, None] * p.T[None, :, None, :]).reshape(256, 256)
        for p in (point_one, point_two)
    ]
    big = (ROWS, WIDE)
    dz_two, ka, *parts = call(
        start_kernel,
        [(big, bf16), ((WIDE, 16 * C), bf16)] + [((ROWS, 256), f32)] * 4,
        iz.reshape(1),
        pre_two,
        upstream,
        tz,
        smem=1,
    )
    slope, local_two, weight_two, _, *ins = call(
        side_kernel,
        [(big, f32), (big, f32), ((C, C), f32), (big, bf16)] + [((ROWS, 512), f32)] * 4,
        pre_one,
        first,
        dz_two,
        ka,
        point_two,
    )
    got = exchange(parts, "gx")
    parts = call(along_y_kernel, [((32, 256), f32)] * 4, *got, ty)
    got = exchange(parts, "gy")
    got_in = exchange(ins, "gx")
    parts = call(along_x_kernel, [((16, 256), f32)] * 4, *got, tx)
    got = exchange(parts, "x")
    ins = call(along_y_kernel, [((32, 512), f32)] * 4, *got_in, ty)
    parts = call(halves_kernel, [((4, 256), f32)] * 4, *got)
    got = exchange(parts, "z")
    back, hat_two = call(
        mix_two_kernel, [((4, 256), f32)] * 2, *got, by_kz(spectral_two), fold
    )
    (tall,) = call(stack_kernel, [((16, 256), f32)], *spread(back, "z"))
    (tall,) = call(back_x_kernel, [((32, 256), f32)], *spread(tall, "x"), tx)
    (tall,) = call(back_y_kernel, [((ROWS, 256), f32)], *spread(tall, "gy"), ty)
    dz_one, *parts = call(
        middle_kernel,
        [(big, bf16)] + [((ROWS, 256), f32)] * 4,
        *spread(tall, "gx"),
        ka,
        local_two,
        slope,
    )
    local_one, sent = call(
        side_one_kernel,
        [(big, f32), ((32, 256), f32)],
        first,
        dz_one,
        point_one,
        weight_two,
        turn,
    )
    got = exchange(parts, "gx")
    parts = call(along_y_join_kernel, [((32, 1024), f32)] * 4, *got, ty, *ins, sent)
    got = exchange(parts, "gy")
    parts = call(along_x_kernel, [((16, 896), f32)] * 4, *got, tx)
    got = exchange(parts, "x")
    parts = call(halves_kernel, [((4, 896), f32)] * 4, *got)
    got = exchange(parts, "z")
    back, hat_one, mid_hat, first_hat = call(
        mix_one_kernel,
        [((4, 384), f32)] + [((4, 256), f32)] * 3,
        *got,
        by_kz(spectral_one),
        fold,
    )
    (spec_two,) = call(outer_kernel, [((16, C * C), f32)], mid_hat, hat_two, fold)
    (spec_one,) = call(outer_kernel, [((16, C * C), f32)], first_hat, hat_one, fold)
    (tall,) = call(stack_kernel, [((16, 384), f32)], *spread(back, "z"))
    tall, weight = call(
        back_x_one_kernel, [((32, 256), f32)] * 2, *spread(tall, "x"), tx
    )
    (tall,) = call(back_y_one_kernel, [((ROWS + 32, 256), f32)], *spread(tall, "gy"), ty, weight)
    input_grad, weight = call(
        end_kernel,
        [(big, bf16), ((C, 128), f32)],
        *spread(tall, "gx"),
        ka,
        local_one,
        turn,
    )
    return (
        input_grad.reshape(CELLS_X, CELLS_Y, WIDE),
        by_ky(spec_one),
        by_ky(spec_two),
        weight[:, C:],
        weight[:, :C],
    )


def solution(mesh):
    grid = P("gz", "gy", "gx")
    modes = P("gz", "gy", "gx", None)
    return jax.shard_map(
        on_device,
        mesh=mesh,
        in_specs=(grid, grid, grid, grid, modes, modes, P(), P()),
        out_specs=(grid, modes, modes, P(), P()),
        check_vma=False,
    )
```

```python
import jax
import jax.numpy as jnp
import numpy as np
from jax import lax
from jax.experimental import pallas as pl
from jax.experimental.pallas import tpu as pltpu
from jax.sharding import PartitionSpec as P


INTERPRET = False

C = 64
CELLS_X, CELLS_Y, CELLS_Z = 8, 16, 32
DEV_X, DEV_Y, DEV_Z = 16, 4, 4
ROWS = CELLS_X * CELLS_Y
WIDE = CELLS_Z * C
TOTAL_CELLS = CELLS_X * DEV_X * CELLS_Y * DEV_Y * CELLS_Z * DEV_Z
TOTAL_MODES = 16**3
SCALE_A = (TOTAL_CELLS * TOTAL_MODES) ** (-0.25)
SCALE_B = TOTAL_CELLS ** (-0.5)

inv_root_two = 0.7071067811865476
inv_root_tau = 0.3989422804014327
bf16 = jnp.bfloat16
f32 = jnp.float32


def cas(mode, length, position):
    mode = np.asarray(mode)
    freq = np.where(mode < 8, mode, length - 16 + mode)
    phase = (freq * position % length) * (2.0 * np.pi / length)
    return (np.cos(phase) + np.sin(phase)).astype(np.float32)


def build_tables():
    four = np.arange(4)
    z = np.arange(CELLS_Z)
    tz = np.zeros((DEV_Z, CELLS_Z, 16), np.float32)
    for d in range(DEV_Z):
        modes = (((d + four) % 4)[:, None] * 4 + four[None, :]).reshape(-1)
        tz[d] = cas(modes[None, :], CELLS_Z * DEV_Z, z[:, None] * DEV_Z + d)
    tz = np.repeat(tz, C, axis=2).astype(np.float32)
    y = np.arange(CELLS_Y)
    ty = np.zeros((DEV_Y, 4, CELLS_X, 4, CELLS_X, CELLS_Y), np.float32)
    for d in range(DEV_Y):
        modes = ((d + four) % 4)[:, None] * 4 + four[None, :]
        small = cas(modes[:, :, None], CELLS_Y * DEV_Y, y * DEV_Y + d)
        for x in range(CELLS_X):
            ty[d, :, x, :, x, :] = small
    ty = ty.reshape(DEV_Y, ROWS, ROWS)
    x = np.arange(CELLS_X)
    tx = np.zeros((DEV_X, 4, 4, 4, CELLS_X, 4), np.float32)
    wide = np.zeros((DEV_X, 4, 4, 4, 4, CELLS_X, 4), np.float32)
    turn = np.zeros((4, 4, 16, 64), np.float32)
    for d in range(4):
        for j in range(4):
            for i in range(16):
                turn[d, j, i, (d + j) % 4 * 16 + i] = 1.0
    for d in range(DEV_X):
        modes = ((d // 4 + four) % 4)[:, None] * 4 + (d % 4 + four[None, :]) % 4
        small = cas(modes[:, :, None], CELLS_X * DEV_X, x * DEV_X + d)
        for l in range(4):
            tx[d, :, :, l, :, l] = small
            for j in range(4):
                there = (d // 4 + j) % 4 * 4 + d % 4
                far = cas(modes[:, :, None], CELLS_X * DEV_X, x * DEV_X + there)
                wide[d, :, :, l, j, :, l] = far.transpose(1, 0, 2)
    tx = tx.reshape(DEV_X, 64, CELLS_X * 4)
    turn = turn.reshape(4, 64, 64)
    fold = (np.arange(C * C)[:, None] // C == np.arange(C)[None, :]).astype(np.float32)
    wide = wide.reshape(DEV_X, 64, 4 * CELLS_X * 4)
    tz = tz.astype(bf16).astype(np.float32)
    return (tz,) + tuple(t.astype(bf16) for t in (ty, tx, wide, turn, fold))


def dot(left, right):
    return jnp.dot(left, right, preferred_element_type=f32)


def dot_nt(left, right):
    return lax.dot_general(left, right, (((1,), (1,)), ((), ())), preferred_element_type=f32)


def dot_tn(left, right):
    return lax.dot_general(left, right, (((0,), (0,)), ((), ())), preferred_element_type=f32)


def split(v):
    high = v.astype(bf16)
    return high, (v - high.astype(f32)).astype(bf16)


def table_dot(table, v):
    high, low = split(v)
    return dot(table, high) + dot(table, low)


def table_dot_tn(table, v):
    high, low = split(v)
    return dot_tn(table, high) + dot_tn(table, low)


def slope_of(v, cdf):
    return cdf + v * jnp.exp(-0.5 * v * v) * inv_root_tau


def cdf_of(v):
    return 0.5 * (1.0 + lax.erf(v * inv_root_two))


def call(body, outs, *args, scratch=(), limit=8):
    rest = args[1:]
    shapes = [pltpu.VMEM(*o[:2]) if len(o) == 2 else jax.ShapeDtypeStruct(*o[:2]) for o in outs]
    if INTERPRET:
        shapes = [jax.ShapeDtypeStruct(*o[:2]) for o in outs]
    else:
        rest = [pltpu.with_memory_space_constraint(a, pltpu.VMEM) for a in rest]
    return pl.pallas_call(
        body,
        out_shape=shapes,
        in_specs=[pl.BlockSpec(memory_space=pltpu.SMEM)]
        + [pl.BlockSpec(memory_space=pltpu.VMEM)] * len(rest),
        out_specs=[pl.BlockSpec(memory_space=pltpu.VMEM)] * len(outs),
        scratch_shapes=[pltpu.VMEM(s, d) for s, d in scratch],
        interpret=INTERPRET,
        compiler_params=pltpu.CompilerParams(vmem_limit_bytes=limit << 20),
    )(args[0], *rest)


def at_x(at):
    return at[0] >> 4


def at_y(at):
    return (at[0] >> 2) & 3


def at_z(at):
    return at[0] & 3


def block(b):
    return pl.ds(pl.multiple_of(b * 256, 256), 256)


def store_parts(v, refs):
    for j, ref in enumerate(refs):
        ref[...] = v[:, j * 256 : (j + 1) * 256]


def fill_table(ka, tz, place, b):
    lane = lax.broadcasted_iota(jnp.int32, (C, 16 * C), 1) & (C - 1)
    row = lax.broadcasted_iota(jnp.int32, (C, 16 * C), 0)
    eye = jnp.where(lane == row, 1.0, 0.0)
    for q in range(4):
        z = b * 4 + q
        here = pl.ds(pl.multiple_of(z * C, C), C)
        ka[here, :] = (eye * tz[place, pl.ds(z, 1), :]).astype(bf16)


def start_kernel(at, pre, grad, tz, dz, p0, p1, p2, p3, ka, total):
    place = at_z(at)

    def fill(b):
        cut = block(b)
        v = pre[:, cut].astype(f32)
        dz[:, cut] = (grad[:, cut].astype(f32) * slope_of(v, cdf_of(v))).astype(bf16)
        fill_table(ka, tz, place, b)

    def step(b, _):
        fill(b)
        total[...] += dot(dz[:, block(b - 1)], ka[block(b - 1), :])
        return 0

    total[...] = jnp.zeros_like(total)
    fill(0)
    lax.fori_loop(1, 8, step, 0)
    store_parts(total[...] + dot(dz[:, 7 * 256 :], ka[7 * 256 :, :]), (p0, p1, p2, p3))


def diagonal_sum(total):
    return sum(total[i * C : (i + 1) * C, i * C : (i + 1) * C] for i in range(4))


def side_kernel(
    at, pre, first, dz, tz, point, slope, local, weight, p0, p1, p2, p3, ka, total, squares
):
    place = at_z(at)

    def step(b, _):
        cut = block(b)
        v = pre[:, cut].astype(f32)
        cdf = cdf_of(v)
        slope[:, cut] = slope_of(v, cdf)
        mid = (v * cdf).astype(bf16)
        here = dz[:, cut]
        local[:, cut] = dot(here, point[...])
        squares[...] += dot_tn(mid, here)
        fill_table(ka, tz, place, b)
        total[...] += dot(jnp.concatenate([mid, first[:, cut]], axis=0), ka[cut, :])
        return 0

    total[...] = jnp.zeros_like(total)
    squares[...] = jnp.zeros_like(squares)
    lax.fori_loop(0, 8, step, 0)
    weight[...] = diagonal_sum(squares[...])
    for j, ref in enumerate((p0, p1, p2, p3)):
        ref[:, :256] = total[:ROWS, j * 256 : (j + 1) * 256]
        ref[:, 256:] = total[ROWS:, j * 256 : (j + 1) * 256]


def side_one_kernel(at, first, dz, point, weight_two, turn, local, sent, squares):
    def step(b, _):
        cut = block(b)
        here = dz[:, cut]
        local[:, cut] = dot(here, point[...])
        squares[...] += dot_tn(first[:, cut], here)
        return 0

    squares[...] = jnp.zeros_like(squares)
    lax.fori_loop(0, 8, step, 0)
    both = jnp.concatenate([weight_two[...], diagonal_sum(squares[...])], axis=1) * SCALE_B
    turned = table_dot(turn[at_x(at) & 3], both)
    sent[...] = jnp.concatenate([turned[:32], turned[32:]], axis=1)


def total_of(refs):
    return (refs[0][...] + refs[1][...]) + (refs[2][...] + refs[3][...])


def along_y_kernel(at, a, b, c, d, ty, *parts):
    out = table_dot(ty[at_y(at)], total_of((a, b, c, d)))
    for j, ref in enumerate(parts):
        ref[...] = out[j * 32 : (j + 1) * 32]


def along_y_join_kernel(at, a, b, c, d, ty, ins0, ins1, ins2, ins3, sent, *parts):
    out = table_dot(ty[at_y(at)], total_of((a, b, c, d)))
    ins = (ins0, ins1, ins2, ins3)
    for j, ref in enumerate(parts):
        ref[:, :256] = out[j * 32 : (j + 1) * 32]
        ref[:, 256:768] = ins[j][...]
        ref[:, 768:] = sent[...]


def total_kernel(at, a, b, c, d, out):
    out[...] = total_of((a, b, c, d))


def before_x_kernel(at, a, b, c, d, tx, *parts):
    v = total_of((a, b, c, d))
    ins = table_dot(tx[at_x(at)], v[:, 256:768])
    weight = jnp.concatenate([v[:, 768:896], v[:, 896:]], axis=0)
    for j, ref in enumerate(parts):
        ref[:, :256] = v[:16, :256]
        ref[:, 256:512] = v[16:, :256]
        ref[:, 512:1024] = ins[j * 16 : (j + 1) * 16]
        for k in range(4):
            ref[:, 1024 + 128 * k : 1152 + 128 * k] = weight[k * 16 : (k + 1) * 16]


def along_x_kernel(at, a, b, c, d, wide, *parts):
    v = jnp.concatenate([a[...], b[...], c[...], d[...]], axis=0)
    out = table_dot(wide[at_x(at)], v)
    for j, ref in enumerate(parts):
        ref[...] = out[j * 16 : (j + 1) * 16]


def along_x_join_kernel(at, a, b, c, d, wide, *parts):
    order = (a, d, c, b)
    v = jnp.concatenate([r[:, k : k + 256] for r in order for k in (0, 256)], axis=0)
    out = table_dot(wide[at_x(at)], v)
    side = total_of([r[:, 512:] for r in order])
    for j, ref in enumerate(parts):
        here = side[j * 4 : (j + 1) * 4]
        ref[:16, :256] = out[j * 16 : (j + 1) * 16]
        ref[:16, 256:] = side[:, 512 + 128 * j : 640 + 128 * j]
        ref[16:20, :256] = here[:, :256]
        ref[20:24, :256] = here[:, 256:512]
        ref[16:, 256:] = jnp.zeros((8, 128), f32)


def mixed(hat, weights, fold):
    pieces = []
    for j in range(4):
        tall = []
        for k in range(4):
            h = hat[j * 4 : (j + 1) * 4, k * C : (k + 1) * C]
            tall.append(jnp.concatenate([h, h], axis=1))
        product = weights[j][...] * jnp.concatenate([jnp.concatenate(tall, axis=0)] * 32, axis=1)
        pieces.extend(split(product))
    out = dot(jnp.concatenate(pieces, axis=0), fold[...])
    rows = []
    for j in range(4):
        here = (out[j * 32 : j * 32 + 16] + out[j * 32 + 16 : j * 32 + 32]) * SCALE_A
        rows.append(jnp.concatenate([here[k * 4 : (k + 1) * 4] for k in range(4)], axis=1))
    return jnp.concatenate(rows, axis=0)


def mix_two_kernel(at, a, b, c, d, w0, w1, w2, w3, fold, back, hat_out):
    hat = total_of((a, b, c, d)) * SCALE_B
    hat_out[...] = hat[:4]
    back[...] = mixed(hat, (w0, w1, w2, w3), fold)


def mix_one_kernel(
    at, a, b, c, d, w0, w1, w2, w3, fold, back, hat_out, mid_out, first_out
):
    v = total_of((a, b, c, d))
    hat = v[:16, :256] * SCALE_B
    hat_out[...] = hat[:4]
    mid_out[...] = v[16:20, :256] * SCALE_A
    first_out[...] = v[20:24, :256] * SCALE_A
    back[:, :256] = mixed(hat, (w0, w1, w2, w3), fold)
    back[:, 256:] = v[:16, 256:]


def outer_kernel(at, left, right, fold, out):
    lefts = []
    rights = []
    for k in range(4):
        cut = slice(k * C, (k + 1) * C)
        h = right[:, cut]
        lefts.append(left[:, cut])
        rights.append(jnp.concatenate([h, h], axis=1))
    v = jnp.concatenate(lefts, axis=0)
    high, rest = v.astype(bf16), v - v.astype(bf16).astype(f32)
    low, last = split(rest)
    spread_left = dot_nt(jnp.concatenate([high, low, last], axis=0), fold[...])
    tall = jnp.concatenate(rights, axis=0)
    whole = (spread_left[:16] + spread_left[16:32]) + spread_left[32:]
    whole = whole * jnp.concatenate([tall] * 32, axis=1)
    for k in range(4):
        out[:, k, :] = whole[k * 4 : (k + 1) * 4]


def back_x_kernel(at, a, b, c, d, wide, out):
    v = jnp.concatenate([a[...], b[...], c[...], d[...]], axis=0)
    out[...] = table_dot_tn(wide[at_x(at)], v)[:32]


def back_x_one_kernel(at, a, b, c, d, wide, out, weight):
    v = jnp.concatenate([a[...], b[...], c[...], d[...]], axis=0)
    out[...] = table_dot_tn(wide[at_x(at)], v[:, :256])[:32]
    weight[...] = jnp.concatenate([v[:32, 256:], v[32:, 256:]], axis=1)


def back_y_kernel(at, a, b, c, d, ty, out):
    v = jnp.concatenate([a[...], b[...], c[...], d[...]], axis=0)
    out[...] = table_dot_tn(ty[at_y(at)], v)


def back_y_one_kernel(at, a, b, c, d, ty, weight, out):
    v = jnp.concatenate([a[...], b[...], c[...], d[...]], axis=0)
    out[:ROWS] = table_dot_tn(ty[at_y(at)], v)
    out[ROWS:] = weight[...]


def stack_halves(refs, halves):
    for j, ref in enumerate(refs):
        high, low = split(ref[:ROWS])
        halves[:ROWS, j * 256 : (j + 1) * 256] = high
        halves[ROWS:, j * 256 : (j + 1) * 256] = low


def down_of(halves, rows, local):
    out = dot_nt(halves[...], rows)
    return (out[:ROWS] + out[ROWS:]) + local


def middle_kernel(
    at, a, b, c, d, tz, local, slope, dz, p0, p1, p2, p3, ka, halves, total
):
    place = at_z(at)
    stack_halves((a, b, c, d), halves)

    def fill(i):
        cut = block(i)
        fill_table(ka, tz, place, i)
        down = down_of(halves, ka[cut, :], local[:, cut])
        dz[:, cut] = (down * slope[:, cut]).astype(bf16)

    def step(i, _):
        fill(i)
        total[...] += dot(dz[:, block(i - 1)], ka[block(i - 1), :])
        return 0

    total[...] = jnp.zeros_like(total)
    fill(0)
    lax.fori_loop(1, 8, step, 0)
    store_parts(total[...] + dot(dz[:, 7 * 256 :], ka[7 * 256 :, :]), (p0, p1, p2, p3))


def end_kernel(at, a, b, c, d, tz, local, turn, out, weight_two, weight_one, ka, halves):
    place = at_z(at)
    stack_halves((a, b, c, d), halves)

    def step(i, _):
        cut = block(i)
        fill_table(ka, tz, place, i)
        out[:, cut] = down_of(halves, ka[cut, :], local[:, cut]).astype(bf16)
        return 0

    lax.fori_loop(0, 8, step, 0)
    w = (a[ROWS:] + b[ROWS:]) + (c[ROWS:] + d[ROWS:])
    w = jnp.concatenate([w[:, :128], w[:, 128:]], axis=0)
    w = table_dot_tn(turn[at_x(at) & 3], w)
    weight_two[...] = w[:, :C]
    weight_one[...] = w[:, C:]


def shift_pairs(kind, s):
    if kind == "x":
        return "gz", [(i, (i // 4 + s) % 4 * 4 + i % 4) for i in range(16)]
    if kind == "z":
        return "gz", [(i, i // 4 * 4 + (i % 4 + s) % 4) for i in range(16)]
    return kind, [(i, (i + s) % 4) for i in range(4)]


def shifted(v, kind, s):
    axis, pairs = shift_pairs(kind, s)
    return lax.ppermute(v, axis, pairs)


def exchange(parts, kind):
    return [parts[0]] + [shifted(parts[s], kind, s) for s in (1, 2, 3)]


def spread(v, kind):
    return [v] + [shifted(v, kind, s) for s in (3, 2, 1)]


def by_kz(weights):
    w = weights.reshape(4, 4, C * C).transpose(1, 0, 2).reshape(16, C * C)
    return w.astype(f32)


def on_device(
    grid_input, pre_one, pre_two, grad_output, spectral_one, spectral_two, point_one, point_two
):
    tz, ty, tx, wide, turn, fold = [jnp.asarray(t) for t in build_tables()]
    at = lax.axis_index(("gz", "gy", "gx")).reshape(1)
    first, pre_one, pre_two, upstream = [
        t.reshape(ROWS, WIDE) for t in (grid_input, pre_one, pre_two, grad_output)
    ]
    eye = jnp.eye(4, dtype=bf16)
    point_one, point_two = [
        (eye[:, None, :, None] * p.T[None, :, None, :]).reshape(256, 256)
        for p in (point_one, point_two)
    ]
    big = (ROWS, WIDE)
    parts_of = [((ROWS, 256), f32)] * 4
    table = ((WIDE, 16 * C), bf16)
    weights_two = spread(by_kz(spectral_two), "x")
    weights_one = spread(by_kz(spectral_one), "x")

    dz_two, *parts = call(
        start_kernel,
        [(big, bf16)] + parts_of,
        at,
        pre_two,
        upstream,
        tz,
        scratch=[table, ((ROWS, 16 * C), f32)],
    )
    slope, local_two, weight_two, *ins = call(
        side_kernel,
        [(big, f32), (big, f32), ((C, C), f32)] + [((ROWS, 512), f32)] * 4,
        at,
        pre_one,
        first,
        dz_two,
        tz,
        point_two,
        scratch=[table, ((2 * ROWS, 16 * C), f32), ((256, 256), f32)],
    )
    got = exchange(parts, "gx")
    got, ins, slope, local_two, weight_two = lax.optimization_barrier(
        (got, ins, slope, local_two, weight_two)
    )
    parts = call(along_y_kernel, [((32, 256), f32)] * 4, at, *got, ty)
    got_in = exchange(ins, "gx")
    got = exchange(parts, "gy")
    (tall,) = call(total_kernel, [((32, 256), f32)], at, *got)
    got = spread(tall, "x")
    got, weights_two = lax.optimization_barrier((got, weights_two))
    parts = call(along_x_kernel, [((16, 256), f32)] * 4, at, *got, wide)
    got = exchange(parts, "z")
    ins = call(along_y_kernel, [((32, 512), f32)] * 4, at, *got_in, ty)
    got, ins = lax.optimization_barrier((got, ins))
    back, hat_two = call(
        mix_two_kernel,
        [((16, 256), f32), ((4, 256), f32)],
        at,
        *got,
        *weights_two,
        fold,
    )
    (tall,) = call(back_x_kernel, [((32, 256), f32)], at, *spread(back, "z"), wide)
    got = spread(tall, "gy")
    got, weights_one = lax.optimization_barrier((got, weights_one))
    (tall,) = call(back_y_kernel, [((ROWS, 256), f32)], at, *got, ty)
    dz_one, *parts = call(
        middle_kernel,
        [(big, bf16)] + parts_of,
        at,
        *spread(tall, "gx"),
        tz,
        local_two,
        slope,
        scratch=[table, ((2 * ROWS, 16 * C), bf16), ((ROWS, 16 * C), f32)],
    )
    local_one, sent = call(
        side_one_kernel,
        [(big, f32), ((32, 256), f32)],
        at,
        first,
        dz_one,
        point_one,
        weight_two,
        turn,
        scratch=[((256, 256), f32)],
    )
    got = exchange(parts, "gx")
    parts = call(along_y_join_kernel, [((32, 1024), f32)] * 4, at, *got, ty, *ins, sent)
    got = exchange(parts, "gy")
    parts = call(before_x_kernel, [((16, 1536), f32)] * 4, at, *got, tx)
    got = exchange(parts, "x")
    parts = call(along_x_join_kernel, [((24, 384), f32)] * 4, at, *got, wide)
    got = exchange(parts, "z")
    back, hat_one, mid_hat, first_hat = call(
        mix_one_kernel,
        [((16, 384), f32)] + [((4, 256), f32)] * 3,
        at,
        *got,
        *weights_one,
        fold,
    )
    (spec_two,) = call(outer_kernel, [((4, 4, C * C), f32, 0)], at, mid_hat, hat_two, fold)
    (spec_one,) = call(outer_kernel, [((4, 4, C * C), f32, 0)], at, first_hat, hat_one, fold)
    tall, weight = call(
        back_x_one_kernel,
        [((32, 256), f32), ((32, 256), f32)],
        at,
        *spread(back, "z"),
        wide,
    )
    (tall,) = call(
        back_y_one_kernel, [((ROWS + 32, 256), f32)], at, *spread(tall, "gy"), ty, weight
    )
    input_grad, weight_two, weight_one = call(
        end_kernel,
        [(big, bf16, 0), ((C, C), f32, 0), ((C, C), f32, 0)],
        at,
        *spread(tall, "gx"),
        tz,
        local_one,
        turn,
        scratch=[table, ((2 * ROWS, 16 * C), bf16)],
    )
    return (
        input_grad.reshape(CELLS_X, CELLS_Y, WIDE),
        spec_one[None],
        spec_two[None],
        weight_one,
        weight_two,
    )


def solution(mesh):
    grid = P("gz", "gy", "gx")
    modes = P("gz", "gy", "gx", None)
    return jax.shard_map(
        on_device,
        mesh=mesh,
        in_specs=(grid, grid, grid, grid, modes, modes, P(), P()),
        out_specs=(grid, modes, modes, P(), P()),
        check_vma=False,
    )
```

```python
import jax
import jax.numpy as jnp
import numpy as np
from jax import lax
from jax.experimental import pallas as pl
from jax.experimental.pallas import tpu as pltpu
from jax.sharding import PartitionSpec as P


INTERPRET = False

C = 64
CELLS_X, CELLS_Y, CELLS_Z = 8, 16, 32
DEV_X, DEV_Y, DEV_Z = 16, 4, 4
ROWS = CELLS_X * CELLS_Y
WIDE = CELLS_Z * C
TOTAL_CELLS = CELLS_X * DEV_X * CELLS_Y * DEV_Y * CELLS_Z * DEV_Z
TOTAL_MODES = 16**3
SCALE_A = (TOTAL_CELLS * TOTAL_MODES) ** (-0.25)
SCALE_B = TOTAL_CELLS ** (-0.5)

inv_root_two = 0.7071067811865476
inv_root_tau = 0.3989422804014327
bf16 = jnp.bfloat16
f32 = jnp.float32


def cas(mode, length, position):
    mode = np.asarray(mode)
    freq = np.where(mode < 8, mode, length - 16 + mode)
    phase = (freq * position % length) * (2.0 * np.pi / length)
    return (np.cos(phase) + np.sin(phase)).astype(np.float32)


def build_tables():
    four = np.arange(4)
    z = np.arange(CELLS_Z)
    tz = np.zeros((DEV_Z, CELLS_Z, 16), np.float32)
    for d in range(DEV_Z):
        modes = (((d + four) % 4)[:, None] * 4 + four[None, :]).reshape(-1)
        tz[d] = cas(modes[None, :], CELLS_Z * DEV_Z, z[:, None] * DEV_Z + d)
    tz = np.repeat(tz, C, axis=2).astype(np.float32)
    y = np.arange(CELLS_Y)
    ty = np.zeros((DEV_Y, 4, CELLS_X, 4, CELLS_X, CELLS_Y), np.float32)
    for d in range(DEV_Y):
        modes = (d ^ four)[:, None] * 4 + four[None, :]
        small = cas(modes[:, :, None], CELLS_Y * DEV_Y, y * DEV_Y + d)
        for x in range(CELLS_X):
            ty[d, :, x, :, x, :] = small
    ty = ty.reshape(DEV_Y, ROWS, ROWS)
    x = np.arange(CELLS_X)
    tx = np.zeros((DEV_X, 4, 4, 4, CELLS_X, 4), np.float32)
    wide = np.zeros((DEV_X, 4, 4, 4, 4, CELLS_X, 4), np.float32)
    turn = np.zeros((4, 4, 16, 64), np.float32)
    for d in range(4):
        for j in range(4):
            for i in range(16):
                turn[d, j, i, (d + j) % 4 * 16 + i] = 1.0
    for d in range(DEV_X):
        modes = ((d // 4 + four) % 4)[:, None] * 4 + (d % 4 + four[None, :]) % 4
        small = cas(modes[:, :, None], CELLS_X * DEV_X, x * DEV_X + d)
        for l in range(4):
            tx[d, :, :, l, :, l] = small
            for j in range(4):
                there = (d // 4 + j) % 4 * 4 + d % 4
                far = cas(modes[:, :, None], CELLS_X * DEV_X, x * DEV_X + there)
                wide[d, :, :, l, j, :, l] = far.transpose(1, 0, 2)
    tx = tx.reshape(DEV_X, 64, CELLS_X * 4)
    turn = turn.reshape(4, 64, 64)
    fold = (np.arange(C * C)[:, None] // C == np.arange(C)[None, :]).astype(np.float32)
    wide = wide.reshape(DEV_X, 64, 4 * CELLS_X * 4)
    tz = tz.astype(bf16).astype(np.float32)
    return (tz,) + tuple(t.astype(bf16) for t in (ty, tx, wide, turn, fold))


def dot(left, right):
    return jnp.dot(left, right, preferred_element_type=f32)


def dot_nt(left, right):
    return lax.dot_general(left, right, (((1,), (1,)), ((), ())), preferred_element_type=f32)


def dot_tn(left, right):
    return lax.dot_general(left, right, (((0,), (0,)), ((), ())), preferred_element_type=f32)


def split(v):
    high = v.astype(bf16)
    return high, (v - high.astype(f32)).astype(bf16)


def table_dot(table, v):
    high, low = split(v)
    return dot(table, high) + dot(table, low)


def table_dot_tn(table, v):
    high, low = split(v)
    return dot_tn(table, high) + dot_tn(table, low)


def slope_of(v, cdf):
    return cdf + v * jnp.exp(-0.5 * v * v) * inv_root_tau


def cdf_of(v):
    return 0.5 * (1.0 + lax.erf(v * inv_root_two))


def call(body, outs, *args, scratch=(), limit=8, raw=0):
    near = args[1 : 1 + raw]
    rest = args[1 + raw :]
    shapes = [pltpu.VMEM(*o[:2]) if len(o) == 2 else jax.ShapeDtypeStruct(*o[:2]) for o in outs]
    if INTERPRET:
        shapes = [jax.ShapeDtypeStruct(*o[:2]) for o in outs]
    else:
        near = [pltpu.with_memory_space_constraint(a, pltpu.HBM) for a in near]
        rest = [pltpu.with_memory_space_constraint(a, pltpu.VMEM) for a in rest]
    return pl.pallas_call(
        body,
        out_shape=shapes,
        in_specs=[pl.BlockSpec(memory_space=pltpu.SMEM)]
        + [pl.BlockSpec(memory_space=pl.ANY if INTERPRET else pltpu.HBM)] * raw
        + [pl.BlockSpec(memory_space=pltpu.VMEM)] * len(rest),
        out_specs=[
            pl.BlockSpec(memory_space=(pl.ANY if INTERPRET else pltpu.HBM) if "raw" in o else pltpu.VMEM)
            for o in outs
        ],
        scratch_shapes=[pltpu.VMEM(*s) if isinstance(s, tuple) else s for s in scratch],
        interpret=INTERPRET,
        compiler_params=pltpu.CompilerParams(vmem_limit_bytes=limit << 20),
    )(*args[:1], *near, *rest)


def at_x(at):
    return at[0] >> 4


def at_y(at):
    return (at[0] >> 2) & 3


def at_z(at):
    return at[0] & 3


def block(b):
    return pl.ds(pl.multiple_of(b * 256, 256), 256)


def store_parts(v, refs):
    for j, ref in enumerate(refs):
        ref[...] = v[:, j * 256 : (j + 1) * 256]


def fill_table(ka, mine, b):
    lane = lax.broadcasted_iota(jnp.int32, (C, 16 * C), 1) & (C - 1)
    row = lax.broadcasted_iota(jnp.int32, (C, 16 * C), 0)
    eye = jnp.where(lane == row, 1.0, 0.0)
    for q in range(4):
        z = b * 4 + q
        here = pl.ds(pl.multiple_of(z * C, C), C)
        ka[here, :] = (eye * mine[pl.ds(z, 1), :]).astype(bf16)


def start_kernel(
    at, pre_from, grad_from, tz, dz_to, p1, p2, p3, mine_out, ka, total, pre, grad, dz, mine, sems
):
    def copies(b):
        cut = block(b)
        return (
            pltpu.make_async_copy(pre_from.at[:, cut], pre.at[:, cut], sems.at[b]),
            pltpu.make_async_copy(grad_from.at[:, cut], grad.at[:, cut], sems.at[8 + b]),
        )

    def leave(b):
        return pltpu.make_async_copy(dz.at[:, block(b)], dz_to.at[:, block(b)], sems.at[17 + b])

    first = pltpu.make_async_copy(tz.at[at_z(at)], mine, sems.at[16])
    first.start()
    for b in range(8):
        for copy in copies(b):
            copy.start()
    first.wait()
    mine_out[...] = mine[...]

    def fill(b):
        fill_table(ka, mine, b)
        for copy in copies(b):
            copy.wait()
        cut = block(b)
        v = pre[:, cut].astype(f32)
        dz[:, cut] = (grad[:, cut].astype(f32) * slope_of(v, cdf_of(v))).astype(bf16)

    def step(b, _):
        fill(b)
        leave(b - 1).start()
        total[...] += dot(dz[:, block(b - 1)], ka[block(b - 1), 256:])
        return 0

    total[...] = jnp.zeros_like(total)
    fill(0)
    lax.fori_loop(1, 8, step, 0)
    leave(7).start()
    store_parts(total[...] + dot(dz[:, 7 * 256 :], ka[7 * 256 :, 256:]), (p1, p2, p3))
    for b in range(8):
        leave(b).wait()


def table_kernel(at, mine, dz, ka, p0):
    fill_table(ka, mine, 0)

    def step(b, total):
        fill_table(ka, mine, b)
        return total + dot(dz[:, block(b - 1)], ka[block(b - 1), :256])

    total = lax.fori_loop(1, 8, step, jnp.zeros((ROWS, 256), f32))
    p0[...] = total + dot(dz[:, 7 * 256 :], ka[7 * 256 :, :256])


def diagonal_sum(total):
    return sum(total[i * C : (i + 1) * C, i * C : (i + 1) * C] for i in range(4))


def side_kernel(
    at, pre, first, dz, ka, point, slope, local, weight, p0, p1, p2, p3, total, squares
):
    def step(b, _):
        cut = block(b)
        v = pre[:, cut].astype(f32)
        cdf = cdf_of(v)
        slope[:, cut] = slope_of(v, cdf)
        mid = (v * cdf).astype(bf16)
        here = dz[:, cut]
        local[:, cut] = dot(here, point[...])
        squares[...] += dot_tn(mid, here)
        total[...] += dot(jnp.concatenate([mid, first[:, cut]], axis=0), ka[cut, :])
        return 0

    total[...] = jnp.zeros_like(total)
    squares[...] = jnp.zeros_like(squares)
    lax.fori_loop(0, 8, step, 0)
    weight[...] = diagonal_sum(squares[...])
    for j, ref in enumerate((p0, p1, p2, p3)):
        ref[:, :256] = total[:ROWS, j * 256 : (j + 1) * 256]
        ref[:, 256:] = total[ROWS:, j * 256 : (j + 1) * 256]


def side_one_kernel(at, first, dz, ka, point, weight_two, turn, local, sent, p0, squares):
    def step(b, total):
        cut = block(b)
        here = dz[:, cut]
        local[:, cut] = dot(here, point[...])
        squares[...] += dot_tn(first[:, cut], here)
        return total + dot(here, ka[cut, :256])

    squares[...] = jnp.zeros_like(squares)
    p0[...] = lax.fori_loop(0, 8, step, jnp.zeros((ROWS, 256), f32))
    both = jnp.concatenate([weight_two[...], diagonal_sum(squares[...])], axis=1) * SCALE_B
    turned = table_dot(turn[at_x(at) & 3], both)
    sent[...] = jnp.concatenate([turned[:32], turned[32:]], axis=1)


def total_of(refs):
    return (refs[0][...] + refs[1][...]) + (refs[2][...] + refs[3][...])


def along_y_kernel(at, a, b, c, d, ty, near, far):
    out = table_dot(ty[at_y(at)], total_of((a, b, c, d)))
    near[...] = out[:64]
    far[...] = out[64:]


def along_y_join_kernel(at, a, b, c, d, ty, ins_near, ins_far, sent, near, far):
    out = table_dot(ty[at_y(at)], total_of((a, b, c, d)))
    for ref, ins, here in ((near, ins_near, out[:64]), (far, ins_far, out[64:])):
        ref[:, :256] = here
        ref[:, 256:768] = ins[...]
        ref[:32, 768:] = sent[...]
        ref[32:, 768:] = jnp.zeros((32, 256), f32)


def keep_kernel(at, near, got, keep, send):
    v = near[...] + got[...]
    keep[...] = v[:32]
    wide = min(v.shape[1], 768)
    send[:, :wide] = v[32:, :wide]
    if v.shape[1] > 768:
        send[:, 768:] = v[:32, 768:]


def pair_kernel(at, a, b, out):
    out[:32] = a[...]
    out[32:] = b[...]


def total_kernel(at, a, b, out):
    out[...] = a[...] + b[...]


def before_x_kernel(at, a, b, tx, *parts):
    v = a[...] + b[...]
    ins = table_dot(tx[at_x(at)], v[:, 256:768])
    weight = jnp.concatenate([v[:, 768:896], v[:, 896:]], axis=0)
    for j, ref in enumerate(parts):
        ref[:, :256] = v[:16, :256]
        ref[:, 256:512] = v[16:, :256]
        ref[:, 512:1024] = ins[j * 16 : (j + 1) * 16]
        for k in range(4):
            ref[:, 1024 + 128 * k : 1152 + 128 * k] = weight[k * 16 : (k + 1) * 16]


def along_x_kernel(at, a, b, c, d, wide, *parts):
    v = jnp.concatenate([a[...], b[...], c[...], d[...]], axis=0)
    out = table_dot(wide[at_x(at)], v)
    for j, ref in enumerate(parts):
        ref[...] = out[j * 16 : (j + 1) * 16]


def along_x_join_kernel(at, a, b, c, d, wide, *parts):
    order = (a, d, c, b)
    v = jnp.concatenate([r[:, k : k + 256] for r in order for k in (0, 256)], axis=0)
    out = table_dot(wide[at_x(at)], v)
    side = total_of([r[:, 512:] for r in order])
    for j, ref in enumerate(parts):
        here = side[j * 4 : (j + 1) * 4]
        ref[:16, :256] = out[j * 16 : (j + 1) * 16]
        ref[:16, 256:] = side[:, 512 + 128 * j : 640 + 128 * j]
        ref[16:20, :256] = here[:, :256]
        ref[20:24, :256] = here[:, 256:512]
        ref[16:, 256:] = jnp.zeros((8, 128), f32)


def mixed(hat, weights, rows_from, fold):
    pieces = []
    for j in range(4):
        tall = []
        for k in range(4):
            h = hat[j * 4 : (j + 1) * 4, k * C : (k + 1) * C]
            tall.append(jnp.concatenate([h, h], axis=1))
        product = weights[j][rows_from : rows_from + 16] * jnp.concatenate([jnp.concatenate(tall, axis=0)] * 32, axis=1)
        pieces.extend(split(product))
    out = dot(jnp.concatenate(pieces, axis=0), fold[...])
    rows = []
    for j in range(4):
        here = (out[j * 32 : j * 32 + 16] + out[j * 32 + 16 : j * 32 + 32]) * SCALE_A
        rows.append(jnp.concatenate([here[k * 4 : (k + 1) * 4] for k in range(4)], axis=1))
    return jnp.concatenate(rows, axis=0)


def mix_two_kernel(at, a, b, c, d, w0, w1, w2, w3, fold, back, hat_out):
    hat = total_of((a, b, c, d)) * SCALE_B
    hat_out[...] = hat[:4]
    back[...] = mixed(hat, (w0, w1, w2, w3), 0, fold)


def mix_one_kernel(
    at, a, b, c, d, w0, w1, w2, w3, fold, back, hat_out, mid_out, first_out
):
    v = total_of((a, b, c, d))
    hat = v[:16, :256] * SCALE_B
    hat_out[...] = hat[:4]
    mid_out[...] = v[16:20, :256] * SCALE_A
    first_out[...] = v[20:24, :256] * SCALE_A
    back[:, :256] = mixed(hat, (w0, w1, w2, w3), 16, fold)
    back[:, 256:] = v[:16, 256:]


def outer_kernel(at, left, right, fold, out):
    lefts = []
    rights = []
    for k in range(4):
        cut = slice(k * C, (k + 1) * C)
        h = right[:, cut]
        lefts.append(left[:, cut])
        rights.append(jnp.concatenate([h, h], axis=1))
    v = jnp.concatenate(lefts, axis=0)
    high, rest = v.astype(bf16), v - v.astype(bf16).astype(f32)
    low, last = split(rest)
    spread_left = dot_nt(jnp.concatenate([high, low, last], axis=0), fold[...])
    tall = jnp.concatenate(rights, axis=0)
    whole = (spread_left[:16] + spread_left[16:32]) + spread_left[32:]
    whole = whole * jnp.concatenate([tall] * 32, axis=1)
    for k in range(4):
        out[:, k, :] = whole[k * 4 : (k + 1) * 4]


def back_x_kernel(at, a, b, c, d, wide, out):
    v = jnp.concatenate([a[...], b[...], c[...], d[...]], axis=0)
    out[...] = table_dot_tn(wide[at_x(at)], v)[:32]


def back_x_one_kernel(at, a, b, c, d, wide, out, weight):
    v = jnp.concatenate([a[...], b[...], c[...], d[...]], axis=0)
    out[...] = table_dot_tn(wide[at_x(at)], v[:, :256])[:32]
    weight[...] = jnp.concatenate([v[:32, 256:], v[32:, 256:]], axis=1)


def back_y_kernel(at, a, b, ty, out):
    v = jnp.concatenate([a[...], b[...]], axis=0)
    out[...] = table_dot_tn(ty[at_y(at)], v)


def back_y_one_kernel(at, a, b, ty, weight, out):
    v = jnp.concatenate([a[...], b[...]], axis=0)
    out[:ROWS] = table_dot_tn(ty[at_y(at)], v)
    out[ROWS:] = weight[...]


def stack_modes(refs, modes):
    for j, ref in enumerate(refs):
        modes[:, j * 256 : (j + 1) * 256] = ref[:ROWS].astype(bf16)


def middle_kernel(
    at, a, b, c, d, ka, local, slope, dz_to, p1, p2, p3, modes, total, dz, sems
):
    stack_modes((a, b, c, d), modes)

    def leave(i):
        return pltpu.make_async_copy(dz.at[:, block(i)], dz_to.at[:, block(i)], sems.at[i])

    def fill(i):
        cut = block(i)
        down = dot_nt(modes[...], ka[cut, :]) + local[:, cut]
        dz[:, cut] = (down * slope[:, cut]).astype(bf16)

    def step(i, _):
        fill(i)
        leave(i - 1).start()
        total[...] += dot(dz[:, block(i - 1)], ka[block(i - 1), 256:])
        return 0

    total[...] = jnp.zeros_like(total)
    fill(0)
    lax.fori_loop(1, 8, step, 0)
    leave(7).start()
    store_parts(total[...] + dot(dz[:, 7 * 256 :], ka[7 * 256 :, 256:]), (p1, p2, p3))
    for i in range(8):
        leave(i).wait()


def end_kernel(
    at, a, b, c, d, ka, local, turn, out_to, weight_two, weight_one, modes, out, sems
):
    stack_modes((a, b, c, d), modes)

    def leave(i):
        return pltpu.make_async_copy(out.at[:, block(i)], out_to.at[:, block(i)], sems.at[i])

    def step(i, _):
        cut = block(i)
        out[:, cut] = (dot_nt(modes[...], ka[cut, :]) + local[:, cut]).astype(bf16)
        leave(i).start()
        return 0

    lax.fori_loop(0, 8, step, 0)
    w = (a[ROWS:] + b[ROWS:]) + (c[ROWS:] + d[ROWS:])
    w = jnp.concatenate([w[:, :128], w[:, 128:]], axis=0)
    w = table_dot_tn(turn[at_x(at) & 3], w)
    weight_two[...] = w[:, :C]
    weight_one[...] = w[:, C:]
    for i in range(8):
        leave(i).wait()


def shift_pairs(kind, s):
    if kind == "x":
        return "gz", [(i, (i // 4 + s) % 4 * 4 + i % 4) for i in range(16)]
    if kind == "z":
        return "gz", [(i, i // 4 * 4 + (i % 4 + s) % 4) for i in range(16)]
    if kind == "gy":
        return "gy", [(i, i ^ s) for i in range(4)]
    return kind, [(i, (i + s) % 4) for i in range(4)]


def shifted(v, kind, s):
    axis, pairs = shift_pairs(kind, s)
    return lax.ppermute(v, axis, pairs)


def exchange(parts, kind):
    return [parts[0]] + [shifted(parts[s], kind, s) for s in (1, 2, 3)]


def spread(v, kind):
    return [v] + [shifted(v, kind, s) for s in (3, 2, 1)]


def reduce_y(at, near, far, width):
    keep, send = call(
        keep_kernel, [((32, width), f32)] * 2, at, near, shifted(far, "gy", 2)
    )
    return keep, shifted(send, "gy", 1)


def spread_y(at, v):
    (pair,) = call(pair_kernel, [((64, 256), f32)], at, v, shifted(v, "gy", 1))
    return pair, shifted(pair, "gy", 2)


def by_kz(weights):
    w = weights.reshape(4, 4, C * C).transpose(1, 0, 2).reshape(16, C * C)
    return w.astype(f32)


def on_device(
    grid_input, pre_one, pre_two, grad_output, spectral_one, spectral_two, point_one, point_two
):
    tz, ty, tx, wide, turn, fold = [jnp.asarray(t) for t in build_tables()]
    at = lax.axis_index(("gz", "gy", "gx")).reshape(1)
    first, pre_one, pre_two, upstream = [
        t.reshape(ROWS, WIDE) for t in (grid_input, pre_one, pre_two, grad_output)
    ]
    eye = jnp.eye(4, dtype=bf16)
    point_one, point_two = [
        (eye[:, None, :, None] * p.T[None, :, None, :]).reshape(256, 256)
        for p in (point_one, point_two)
    ]
    big = (ROWS, WIDE)
    parts_of = [((ROWS, 256), f32)] * 3
    table = ((WIDE, 16 * C), bf16)

    dz_two, *parts, mine = call(
        start_kernel,
        [(big, bf16, "raw")] + parts_of + [((CELLS_Z, 16 * C), f32)],
        at,
        pre_two,
        upstream,
        tz,
        raw=3,
        scratch=[
            table,
            ((ROWS, 12 * C), f32),
            (big, bf16),
            (big, bf16),
            (big, bf16),
            ((CELLS_Z, 16 * C), f32),
            pltpu.SemaphoreType.DMA((25,)),
        ],
    )
    parts, mine, spectral_two, spectral_one = lax.optimization_barrier(
        (parts, mine, spectral_two, spectral_one)
    )
    ka, own = call(table_kernel, [(*table, 0), ((ROWS, 256), f32)], at, mine, dz_two)
    weights = jnp.concatenate([by_kz(spectral_two), by_kz(spectral_one)], axis=0)
    weights = spread(weights, "x")
    got = exchange([own] + parts, "gx")
    near, far = call(along_y_kernel, [((64, 256), f32)] * 2, at, *got, ty)
    got = reduce_y(at, near, far, 256)
    (tall,) = call(total_kernel, [((32, 256), f32)], at, *got)
    got = spread(tall, "x")
    parts = call(along_x_kernel, [((16, 256), f32)] * 4, at, *got, wide)
    parts, dz_side, pre_one, first = lax.optimization_barrier((parts, dz_two, pre_one, first))
    slope, local_two, weight_two, *ins = call(
        side_kernel,
        [(big, f32, 0), (big, f32, 0), ((C, C), f32, 0)] + [((ROWS, 512), f32)] * 4,
        at,
        pre_one,
        first,
        dz_side,
        ka,
        point_two,
        scratch=[((2 * ROWS, 16 * C), f32), ((256, 256), f32)],
    )
    got = exchange(parts, "z")
    got, ins, slope, local_two, weight_two = lax.optimization_barrier(
        (got, ins, slope, local_two, weight_two)
    )
    got_in = exchange(ins, "gx")
    back, hat_two = call(
        mix_two_kernel,
        [((16, 256), f32), ((4, 256), f32)],
        at,
        *got,
        *weights,
        fold,
    )
    (tall,) = call(back_x_kernel, [((32, 256), f32)], at, *spread(back, "z"), wide)
    ins = call(along_y_kernel, [((64, 512), f32)] * 2, at, *got_in, ty)
    got = spread_y(at, tall)
    got, ins = lax.optimization_barrier((got, ins))
    (tall,) = call(back_y_kernel, [((ROWS, 256), f32)], at, *got, ty)
    dz_one, *parts = call(
        middle_kernel,
        [(big, bf16, "raw")] + parts_of,
        at,
        *spread(tall, "gx"),
        ka,
        local_two,
        slope,
        scratch=[
            ((ROWS, 16 * C), bf16),
            ((ROWS, 12 * C), f32),
            (big, bf16),
            pltpu.SemaphoreType.DMA((8,)),
        ],
    )
    local_one, sent, own = call(
        side_one_kernel,
        [(big, f32, 0), ((32, 256), f32), ((ROWS, 256), f32)],
        at,
        first,
        dz_one,
        ka,
        point_one,
        weight_two,
        turn,
        scratch=[((256, 256), f32)],
    )
    got = exchange([own] + parts, "gx")
    near, far = call(along_y_join_kernel, [((64, 1024), f32)] * 2, at, *got, ty, *ins, sent)
    got = reduce_y(at, near, far, 1024)
    parts = call(before_x_kernel, [((16, 1536), f32)] * 4, at, *got, tx)
    got = exchange(parts, "x")
    parts = call(along_x_join_kernel, [((24, 384), f32)] * 4, at, *got, wide)
    got = exchange(parts, "z")
    back, hat_one, mid_hat, first_hat = call(
        mix_one_kernel,
        [((16, 384), f32)] + [((4, 256), f32)] * 3,
        at,
        *got,
        *weights,
        fold,
    )
    (spec_two,) = call(outer_kernel, [((4, 4, C * C), f32, 0)], at, mid_hat, hat_two, fold)
    (spec_one,) = call(outer_kernel, [((4, 4, C * C), f32, 0)], at, first_hat, hat_one, fold)
    tall, weight = call(
        back_x_one_kernel,
        [((32, 256), f32), ((32, 256), f32)],
        at,
        *spread(back, "z"),
        wide,
    )
    (tall,) = call(
        back_y_one_kernel,
        [((ROWS + 32, 256), f32)],
        at,
        *spread_y(at, tall),
        ty,
        weight,
    )
    input_grad, weight_two, weight_one = call(
        end_kernel,
        [(big, bf16, "raw"), ((C, C), f32, 0), ((C, C), f32, 0)],
        at,
        *spread(tall, "gx"),
        ka,
        local_one,
        turn,
        scratch=[((ROWS, 16 * C), bf16), (big, bf16), pltpu.SemaphoreType.DMA((8,))],
    )
    return (
        input_grad.reshape(CELLS_X, CELLS_Y, WIDE),
        spec_one[None],
        spec_two[None],
        weight_one,
        weight_two,
    )


def solution(mesh):
    grid = P("gz", "gy", "gx")
    modes = P("gz", "gy", "gx", None)
    return jax.shard_map(
        on_device,
        mesh=mesh,
        in_specs=(grid, grid, grid, grid, modes, modes, P(), P()),
        out_specs=(grid, modes, modes, P(), P()),
        check_vma=False,
    )
```

```python
import jax
import jax.numpy as jnp
import numpy as np
from jax import lax
from jax.experimental import pallas as pl
from jax.experimental.pallas import tpu as pltpu
from jax.sharding import PartitionSpec as P


INTERPRET = False

C = 64
CELLS_X, CELLS_Y, CELLS_Z = 8, 16, 32
DEV_X, DEV_Y, DEV_Z = 16, 4, 4
ROWS = CELLS_X * CELLS_Y
WIDE = CELLS_Z * C
TOTAL_CELLS = CELLS_X * DEV_X * CELLS_Y * DEV_Y * CELLS_Z * DEV_Z
TOTAL_MODES = 16**3
SCALE_A = (TOTAL_CELLS * TOTAL_MODES) ** (-0.25)
SCALE_B = TOTAL_CELLS ** (-0.5)

inv_root_two = 0.7071067811865476
inv_root_tau = 0.3989422804014327
bf16 = jnp.bfloat16
f32 = jnp.float32


def cas(mode, length, position):
    mode = np.asarray(mode)
    freq = np.where(mode < 8, mode, length - 16 + mode)
    phase = (freq * position % length) * (2.0 * np.pi / length)
    return (np.cos(phase) + np.sin(phase)).astype(np.float32)


def build_tables():
    four = np.arange(4)
    z = np.arange(CELLS_Z)
    tz = np.zeros((DEV_Z, CELLS_Z, 16), np.float32)
    for d in range(DEV_Z):
        modes = (((d + four) % 4)[:, None] * 4 + four[None, :]).reshape(-1)
        tz[d] = cas(modes[None, :], CELLS_Z * DEV_Z, z[:, None] * DEV_Z + d)
    tz = np.repeat(tz, C, axis=2).astype(np.float32)
    y = np.arange(CELLS_Y)
    ty = np.zeros((DEV_Y, 4, CELLS_X, 4, CELLS_X, CELLS_Y), np.float32)
    for d in range(DEV_Y):
        modes = (d ^ np.array([0, 2, 1, 3]))[:, None] * 4 + four[None, :]
        small = cas(modes[:, :, None], CELLS_Y * DEV_Y, y * DEV_Y + d)
        for x in range(CELLS_X):
            ty[d, :, x, :, x, :] = small
    ty = ty.reshape(DEV_Y, ROWS, ROWS)
    x = np.arange(CELLS_X)
    tx = np.zeros((DEV_X, 16, 4, CELLS_X, 4), np.float32)
    for d in range(DEV_X):
        small = cas(np.arange(16)[:, None], CELLS_X * DEV_X, x * DEV_X + d)
        for l in range(4):
            tx[d, :, l, :, l] = small
    tx = tx.reshape(DEV_X, 64, CELLS_X * 4)
    return tuple(t.astype(bf16) for t in (tz, ty, tx))


def dot(left, right):
    return jnp.dot(left, right, preferred_element_type=f32)


def dot_nt(left, right):
    return lax.dot_general(left, right, (((1,), (1,)), ((), ())), preferred_element_type=f32)


def dot_tn(left, right):
    return lax.dot_general(left, right, (((0,), (0,)), ((), ())), preferred_element_type=f32)


def split(v):
    high = v.astype(bf16)
    return high, (v - high.astype(f32)).astype(bf16)


def table_dot(table, v):
    high, low = split(v)
    return dot(table, high) + dot(table, low)


def table_dot_tn(table, v):
    high, low = split(v)
    return dot_tn(table, high) + dot_tn(table, low)


def slope_of(v, cdf):
    return cdf + v * jnp.exp(-0.5 * v * v) * inv_root_tau


def cdf_of(v):
    return 0.5 * (1.0 + lax.erf(v * inv_root_two))


def call(body, outs, *args, scratch=(), limit=8, raw=0):
    near = args[1 : 1 + raw]
    rest = args[1 + raw :]
    shapes = [pltpu.VMEM(*o[:2]) if len(o) == 2 else jax.ShapeDtypeStruct(*o[:2]) for o in outs]
    if INTERPRET:
        shapes = [jax.ShapeDtypeStruct(*o[:2]) for o in outs]
    else:
        near = [pltpu.with_memory_space_constraint(a, pltpu.HBM) for a in near]
        rest = [pltpu.with_memory_space_constraint(a, pltpu.VMEM) for a in rest]
    return pl.pallas_call(
        body,
        out_shape=shapes,
        in_specs=[pl.BlockSpec(memory_space=pltpu.SMEM)]
        + [pl.BlockSpec(memory_space=pl.ANY if INTERPRET else pltpu.HBM)] * raw
        + [pl.BlockSpec(memory_space=pltpu.VMEM)] * len(rest),
        out_specs=[
            pl.BlockSpec(memory_space=(pl.ANY if INTERPRET else pltpu.HBM) if "raw" in o else pltpu.VMEM)
            for o in outs
        ],
        scratch_shapes=[pltpu.VMEM(*s) if isinstance(s, tuple) else s for s in scratch],
        interpret=INTERPRET,
        compiler_params=pltpu.CompilerParams(vmem_limit_bytes=limit << 20),
    )(*args[:1], *near, *rest)


def at_x(at):
    return at[0] >> 4


def at_y(at):
    return (at[0] >> 2) & 3


def at_z(at):
    return at[0] & 3


def block(b):
    return pl.ds(pl.multiple_of(b * 256, 256), 256)


def store_parts(v, refs):
    for j, ref in enumerate(refs):
        ref[...] = v[:, j * 256 : (j + 1) * 256]


def fill_table(ka, mine, b, wide=16 * C):
    lane = lax.broadcasted_iota(jnp.int32, (C, wide), 1) & (C - 1)
    row = lax.broadcasted_iota(jnp.int32, (C, wide), 0)
    eye = jnp.where(lane == row, 1.0, 0.0)
    for q in range(4):
        z = b * 4 + q
        here = pl.ds(pl.multiple_of(z * C, C), C) if wide > 256 else slice(q * C, (q + 1) * C)
        ka[here, :] = (eye * mine[pl.ds(z, 1), :wide]).astype(bf16)


def start_kernel(
    at, pre_from, grad_from, tz, dz_to, p1, p2, p3, mine_out, ka, total, pre, grad, dz, short, mine, sems
):
    def copies(b):
        cut = block(b)
        return (
            pltpu.make_async_copy(pre_from.at[:, cut], pre.at[:, cut], sems.at[b]),
            pltpu.make_async_copy(grad_from.at[:, cut], grad.at[:, cut], sems.at[8 + b]),
        )

    def leave(b):
        return pltpu.make_async_copy(dz.at[:, block(b)], dz_to.at[:, block(b)], sems.at[17 + b])

    first = pltpu.make_async_copy(tz.at[at_z(at)], short, sems.at[16])
    first.start()
    for b in range(8):
        for copy in copies(b):
            copy.start()
    first.wait()
    mine[...] = short[...].astype(f32)
    mine_out[...] = mine[...]

    def fill(b):
        fill_table(ka, mine, b)
        for copy in copies(b):
            copy.wait()
        cut = block(b)
        v = pre[:, cut].astype(f32)
        dz[:, cut] = (grad[:, cut].astype(f32) * slope_of(v, cdf_of(v))).astype(bf16)

    def step(b, _):
        fill(b)
        leave(b - 1).start()
        total[...] += dot(dz[:, block(b - 1)], ka[block(b - 1), 256:])
        return 0

    total[...] = jnp.zeros_like(total)
    fill(0)
    lax.fori_loop(1, 8, step, 0)
    leave(7).start()
    store_parts(total[...] + dot(dz[:, 7 * 256 :], ka[7 * 256 :, 256:]), (p1, p2, p3))
    for b in range(8):
        leave(b).wait()


def fill_point(square, point):
    square[...] = jnp.zeros_like(square)
    for i in range(4):
        square[i * C : (i + 1) * C, i * C : (i + 1) * C] = point[...]


def diagonal_sum(total):
    return sum(total[i * C : (i + 1) * C, i * C : (i + 1) * C] for i in range(4))


def side_kernel(
    at, pre, first, dz, mine, point, slope_to, local_to, weight, p0, q0, q1, q2, q3,
    ka, total, own, squares, square, slope, local, sems,
):
    fill_point(square, point)

    def leave(b):
        cut = block(b)
        return (
            pltpu.make_async_copy(slope.at[:, cut], slope_to.at[:, cut], sems.at[b]),
            pltpu.make_async_copy(local.at[:, cut], local_to.at[:, cut], sems.at[8 + b]),
        )

    def fill(b):
        fill_table(ka, mine, b)
        cut = block(b)
        v = pre[:, cut].astype(f32)
        cdf = cdf_of(v)
        slope[:, cut] = slope_of(v, cdf)
        total[b, :ROWS] = (v * cdf).astype(bf16)
        total[b, ROWS:] = first[:, cut]

    def step(b, _):
        cut = block(b)
        fill(b)
        here = dz[:, cut]
        local[:, cut] = dot_nt(here, square[...])
        for copy in leave(b):
            copy.start()
        squares[...] += dot_tn(total[b, :ROWS], here)
        own[: 2 * ROWS] += dot(total[b], ka[cut, :])
        own[2 * ROWS :, :256] += dot(here, ka[cut, :256])
        return 0

    own[...] = jnp.zeros_like(own)
    squares[...] = jnp.zeros_like(squares)
    lax.fori_loop(0, 8, step, 0)
    weight[...] = diagonal_sum(squares[...])
    p0[...] = own[2 * ROWS :, :256]
    for j, ref in enumerate((q0, q1, q2, q3)):
        ref[:, :256] = own[:ROWS, j * 256 : (j + 1) * 256]
        ref[:, 256:] = own[ROWS : 2 * ROWS, j * 256 : (j + 1) * 256]
    for b in range(8):
        for copy in leave(b):
            copy.wait()


def side_one_kernel(
    at, first, dz, mine, point, weight_two, local_to, sent, p0, ka, squares, square, local, sems
):
    fill_point(square, point)

    def leave(b):
        cut = block(b)
        return pltpu.make_async_copy(local.at[:, cut], local_to.at[:, cut], sems.at[b])

    def step(b, total):
        cut = block(b)
        here = dz[:, cut]
        local[:, cut] = dot_nt(here, square[...])
        leave(b).start()
        squares[...] += dot_tn(first[:, cut], here)
        fill_table(ka, mine, b, 256)
        return total + dot(here, ka[...])

    squares[...] = jnp.zeros_like(squares)
    p0[...] = lax.fori_loop(0, 8, step, jnp.zeros((ROWS, 256), f32))
    both = jnp.concatenate([weight_two[...], diagonal_sum(squares[...])], axis=1) * SCALE_B
    sent[...] = jnp.concatenate([both[:32], both[32:]], axis=1)
    for b in range(8):
        leave(b).wait()


def total_of(refs):
    return (refs[0][...] + refs[1][...]) + (refs[2][...] + refs[3][...])


def along_y_kernel(at, a, b, c, d, ty, near, far):
    out = table_dot(ty[at_y(at)], total_of((a, b, c, d)))
    near[...] = out[:64]
    far[...] = out[64:]


def along_y_join_kernel(at, a, b, c, d, ty, ins_near, ins_far, sent, near, far):
    out = table_dot(ty[at_y(at)], total_of((a, b, c, d)))
    for ref, ins, here in ((near, ins_near, out[:64]), (far, ins_far, out[64:])):
        ref[:, :256] = here
        ref[:, 256:768] = ins[...]
        ref[:32, 768:] = sent[...]
        ref[32:, 768:] = jnp.zeros((32, 256), f32)


def keep_kernel(at, near, got, keep, send):
    v = near[...] + got[...]
    keep[...] = v[:32]
    wide = min(v.shape[1], 768)
    send[:, :wide] = v[32:, :wide]
    if v.shape[1] > 768:
        send[:, 768:] = v[:32, 768:]


def pair_kernel(at, a, b, out):
    out[:32] = a[...]
    out[32:] = b[...]


def along_x_kernel(at, a, b, tx, out):
    v = a[...] + b[...]
    modes = table_dot(tx[at_x(at)], v[:, : min(v.shape[1], 768)])
    for i in range(16):
        out[i, :, : modes.shape[1]] = modes[i * 4 : (i + 1) * 4]
    if v.shape[1] > 768:
        weight = jnp.concatenate([v[:, 768:896], v[:, 896:]], axis=0)
        for i in range(16):
            out[i, :, 768:] = weight[i * 4 : (i + 1) * 4]


def mixed(hat, spectral, wide, fold):
    wide[...] = spectral[0].astype(f32)
    products = []
    for k in range(4):
        h = hat[:, k * C : (k + 1) * C]
        h = jnp.concatenate([h, h], axis=1)
        products.append(wide[:, k, :] * jnp.concatenate([h] * 32, axis=1))
    high, low = split(jnp.concatenate(products, axis=0))
    out = dot(jnp.concatenate([high, low], axis=0), fold[...])
    out = (out[:16] + out[16:]) * SCALE_A
    return jnp.concatenate([out[k * 4 : (k + 1) * 4] for k in range(4)], axis=1)


def sixteen(got):
    v = [got[i] for i in range(16)]
    while len(v) > 1:
        v = [v[i] + v[i + 1] for i in range(0, len(v), 2)]
    return v[0]


def mix_two_kernel(at, got, spectral, fold, back, hat_out, wide):
    hat = sixteen(got) * SCALE_B
    hat_out[...] = hat
    out = mixed(hat, spectral, wide, fold)
    for i in range(16):
        back[i] = out


def mix_one_kernel(at, got, spectral, fold, back, hat_out, mid_out, first_out, wide):
    v = sixteen(got)
    hat = v[:, :256] * SCALE_B
    hat_out[...] = hat
    mid_out[...] = v[:, 256:512] * SCALE_A
    first_out[...] = v[:, 512:768] * SCALE_A
    out = mixed(hat, spectral, wide, fold)
    for i in range(16):
        back[i, :, :256] = out
        back[i, :, 256:] = v[:, 768:]


def outer_kernel(at, left, right, fold, out):
    lefts = []
    rights = []
    for k in range(4):
        cut = slice(k * C, (k + 1) * C)
        h = right[:, cut]
        lefts.append(left[:, cut])
        rights.append(jnp.concatenate([h, h], axis=1))
    v = jnp.concatenate(lefts, axis=0)
    high, rest = v.astype(bf16), v - v.astype(bf16).astype(f32)
    low, last = split(rest)
    spread_left = dot_nt(jnp.concatenate([high, low, last], axis=0), fold[...])
    tall = jnp.concatenate(rights, axis=0)
    whole = (spread_left[:16] + spread_left[16:32]) + spread_left[32:]
    whole = whole * jnp.concatenate([tall] * 32, axis=1)
    for k in range(4):
        out[:, k, :] = whole[k * 4 : (k + 1) * 4]


def back_x_kernel(at, got, tx, out):
    v = jnp.concatenate([got[i] for i in range(16)], axis=0)
    out[...] = table_dot_tn(tx[at_x(at)], v)


def back_x_one_kernel(at, got, tx, out, weight):
    v = jnp.concatenate([got[i] for i in range(16)], axis=0)
    out[...] = table_dot_tn(tx[at_x(at)], v[:, :256])
    weight[...] = jnp.concatenate([v[:32, 256:], v[32:, 256:]], axis=1)


def back_y_kernel(at, a, b, ty, out):
    v = jnp.concatenate([a[...], b[...]], axis=0)
    out[...] = table_dot_tn(ty[at_y(at)], v)


def back_y_one_kernel(at, a, b, ty, weight, out):
    v = jnp.concatenate([a[...], b[...]], axis=0)
    out[:ROWS] = table_dot_tn(ty[at_y(at)], v)
    out[ROWS:] = weight[...]


def stack_modes(refs, modes):
    for j, ref in enumerate(refs):
        modes[:, j * 256 : (j + 1) * 256] = ref[:ROWS].astype(bf16)


def middle_kernel(
    at, a, b, c, d, mine, local, slope, dz_to, p1, p2, p3, modes, total, dz, ka, sems
):
    stack_modes((a, b, c, d), modes)

    def leave(i):
        return pltpu.make_async_copy(dz.at[:, block(i)], dz_to.at[:, block(i)], sems.at[i])

    def fill(i):
        cut = block(i)
        fill_table(ka, mine, i)
        down = dot_nt(modes[...], ka[cut, :]) + local[:, cut]
        dz[:, cut] = (down * slope[:, cut]).astype(bf16)

    def step(i, _):
        fill(i)
        leave(i - 1).start()
        total[...] += dot(dz[:, block(i - 1)], ka[block(i - 1), 256:])
        return 0

    total[...] = jnp.zeros_like(total)
    fill(0)
    lax.fori_loop(1, 8, step, 0)
    leave(7).start()
    store_parts(total[...] + dot(dz[:, 7 * 256 :], ka[7 * 256 :, 256:]), (p1, p2, p3))
    for i in range(8):
        leave(i).wait()


def end_kernel(
    at, a, b, c, d, mine, local, out_to, weight_two, weight_one, modes, out, ka, sems
):
    stack_modes((a, b, c, d), modes)

    def leave(i):
        return pltpu.make_async_copy(out.at[:, block(i)], out_to.at[:, block(i)], sems.at[i])

    def step(i, _):
        cut = block(i)
        fill_table(ka, mine, i)
        out[:, cut] = (dot_nt(modes[...], ka[cut, :]) + local[:, cut]).astype(bf16)
        leave(i).start()
        return 0

    lax.fori_loop(0, 8, step, 0)
    w = (a[ROWS:] + b[ROWS:]) + (c[ROWS:] + d[ROWS:])
    w = jnp.concatenate([w[:, :128], w[:, 128:]], axis=0)
    weight_two[...] = w[:, :C]
    weight_one[...] = w[:, C:]
    for i in range(8):
        leave(i).wait()


def shift_pairs(kind, s):
    return kind, [(i, i ^ s if kind == "gy" else (i + s) % 4) for i in range(4)]


def shifted(v, kind, s):
    axis, pairs = shift_pairs(kind, s)
    return lax.ppermute(v, axis, pairs)


def exchange(parts, kind):
    return [parts[0]] + [shifted(parts[s], kind, s) for s in (1, 2, 3)]


def spread(v, kind):
    return [v] + [shifted(v, kind, s) for s in (3, 2, 1)]


def reduce_y(at, near, far, width):
    keep, send = call(
        keep_kernel, [((32, width), f32)] * 2, at, near, shifted(far, "gy", 1)
    )
    return keep, shifted(send, "gy", 2)


def spread_y(at, v):
    (pair,) = call(pair_kernel, [((64, 256), f32)], at, v, shifted(v, "gy", 2))
    return pair, shifted(pair, "gy", 1)


def over_x(v):
    return lax.all_to_all(v, "gz", 0, 0, tiled=True)


def on_device(
    grid_input, pre_one, pre_two, grad_output, spectral_one, spectral_two, point_one, point_two
):
    tz, ty, tx = [jnp.asarray(t) for t in build_tables()]
    row = lax.broadcasted_iota(jnp.int32, (C * C, C), 0)
    fold = (row // C == lax.broadcasted_iota(jnp.int32, (C * C, C), 1)).astype(bf16)
    at = lax.axis_index(("gz", "gy", "gx")).reshape(1)
    first, pre_one, pre_two, upstream = [
        t.reshape(ROWS, WIDE) for t in (grid_input, pre_one, pre_two, grad_output)
    ]
    big = (ROWS, WIDE)
    half = ((ROWS, 256), f32)
    table = ((WIDE, 16 * C), bf16)
    native = ((4, 4, C * C), f32)
    dma = pltpu.SemaphoreType.DMA

    dz_two, *parts, mine = call(
        start_kernel,
        [(big, bf16, "raw")] + [half] * 3 + [((CELLS_Z, 16 * C), f32)],
        at,
        pre_two,
        upstream,
        tz,
        raw=3,
        scratch=[
            table,
            ((ROWS, 12 * C), f32),
            (big, bf16),
            (big, bf16),
            (big, bf16),
            ((CELLS_Z, 16 * C), bf16),
            ((CELLS_Z, 16 * C), f32),
            dma((25,)),
        ],
    )
    slope, local_two, weight_two, own, *ins = call(
        side_kernel,
        [(big, f32, "raw")] * 2 + [((C, C), f32, 0), half] + [((ROWS, 512), f32)] * 4,
        at,
        pre_one,
        first,
        dz_two,
        mine,
        point_two,
        limit=14,
        scratch=[
            table,
            ((8, 2 * ROWS, 256), bf16),
            ((3 * ROWS, 16 * C), f32),
            ((256, 256), f32),
            ((256, 256), bf16),
            (big, f32),
            (big, f32),
            dma((16,)),
        ],
    )
    got = exchange([own] + parts, "gx")
    near, far = call(along_y_kernel, [((64, 256), f32)] * 2, at, *got, ty)
    got = reduce_y(at, near, far, 256)
    (modes,) = call(along_x_kernel, [((16, 4, 256), f32)], at, *got, tx)
    got_in = exchange(ins, "gx")
    modes, got_in[0] = lax.optimization_barrier((modes, got_in[0]))
    got = over_x(modes)
    back, hat_two = call(
        mix_two_kernel,
        [((16, 4, 256), f32), ((4, 256), f32)],
        at,
        got,
        spectral_two,
        fold,
        scratch=[native],
    )
    got = over_x(back)
    got, got_in = lax.optimization_barrier((got, got_in))
    (tall,) = call(back_x_kernel, [((32, 256), f32)], at, got, tx)
    got = spread_y(at, tall)
    (tall,) = call(back_y_kernel, [half], at, *got, ty)
    got = spread(tall, "gx")
    ins = call(along_y_kernel, [((64, 512), f32)] * 2, at, *got_in, ty)
    dz_one, *parts = call(
        middle_kernel,
        [(big, bf16, "raw")] + [half] * 3,
        at,
        *got,
        mine,
        local_two,
        slope,
        scratch=[((ROWS, 16 * C), bf16), ((ROWS, 12 * C), f32), (big, bf16), table, dma((8,))],
    )
    local_one, sent, own = call(
        side_one_kernel,
        [(big, f32, "raw"), ((32, 256), f32), half],
        at,
        first,
        dz_one,
        mine,
        point_one,
        weight_two,
        scratch=[
            ((256, 256), bf16),
            ((256, 256), f32),
            ((256, 256), bf16),
            (big, f32),
            dma((8,)),
        ],
    )
    got = exchange([own] + parts, "gx")
    near, far = call(along_y_join_kernel, [((64, 1024), f32)] * 2, at, *got, ty, *ins, sent)
    got = reduce_y(at, near, far, 1024)
    (modes,) = call(along_x_kernel, [((16, 4, 896), f32)], at, *got, tx)
    back, hat_one, mid_hat, first_hat = call(
        mix_one_kernel,
        [((16, 4, 384), f32)] + [((4, 256), f32)] * 3,
        at,
        over_x(modes),
        spectral_one,
        fold,
        scratch=[native],
    )
    (spec_two,) = call(outer_kernel, [(*native, 0)], at, mid_hat, hat_two, fold)
    (spec_one,) = call(outer_kernel, [(*native, 0)], at, first_hat, hat_one, fold)
    tall, weight = call(back_x_one_kernel, [((32, 256), f32)] * 2, at, over_x(back), tx)
    got = spread_y(at, tall)
    (tall,) = call(back_y_one_kernel, [((ROWS + 32, 256), f32)], at, *got, ty, weight)
    got = spread(tall, "gx")
    input_grad, weight_two, weight_one = call(
        end_kernel,
        [(big, bf16, "raw"), ((C, C), f32, 0), ((C, C), f32, 0)],
        at,
        *got,
        mine,
        local_one,
        scratch=[((ROWS, 16 * C), bf16), (big, bf16), table, dma((8,))],
    )
    return (
        input_grad.reshape(CELLS_X, CELLS_Y, WIDE),
        spec_one[None],
        spec_two[None],
        weight_one,
        weight_two,
    )


def solution(mesh):
    grid = P("gz", "gy", "gx")
    modes = P("gz", "gy", "gx", None)
    return jax.shard_map(
        on_device,
        mesh=mesh,
        in_specs=(grid, grid, grid, grid, modes, modes, P(), P()),
        out_specs=(grid, modes, modes, P(), P()),
        check_vma=False,
    )
```

```python
import jax
import jax.numpy as jnp
import numpy as np
from jax import lax
from jax.experimental import pallas as pl
from jax.experimental.pallas import tpu as pltpu
from jax.sharding import PartitionSpec as P


INTERPRET = False

C = 64
CELLS_X, CELLS_Y, CELLS_Z = 8, 16, 32
DEV_X, DEV_Y, DEV_Z = 16, 4, 4
ROWS = CELLS_X * CELLS_Y
WIDE = CELLS_Z * C
TOTAL_CELLS = CELLS_X * DEV_X * CELLS_Y * DEV_Y * CELLS_Z * DEV_Z
TOTAL_MODES = 16**3
SCALE_A = (TOTAL_CELLS * TOTAL_MODES) ** (-0.25)
SCALE_B = TOTAL_CELLS ** (-0.5)

inv_root_two = 0.7071067811865476
inv_root_tau = 0.3989422804014327
bf16 = jnp.bfloat16
f32 = jnp.float32


def cas(mode, length, position):
    mode = np.asarray(mode)
    freq = np.where(mode < 8, mode, length - 16 + mode)
    phase = (freq * position % length) * (2.0 * np.pi / length)
    return (np.cos(phase) + np.sin(phase)).astype(np.float32)


def build_tables():
    four = np.arange(4)
    z = np.arange(CELLS_Z)
    tz = np.zeros((DEV_Z, CELLS_Z, 16), np.float32)
    for d in range(DEV_Z):
        modes = (((d + four) % 4)[:, None] * 4 + four[None, :]).reshape(-1)
        tz[d] = cas(modes[None, :], CELLS_Z * DEV_Z, z[:, None] * DEV_Z + d)
    tz = np.repeat(tz, C, axis=2).astype(np.float32)
    y = np.arange(CELLS_Y)
    ty = np.zeros((DEV_Y, 4, CELLS_X, 4, CELLS_X, CELLS_Y), np.float32)
    for d in range(DEV_Y):
        modes = (d ^ np.array([0, 2, 1, 3]))[:, None] * 4 + four[None, :]
        small = cas(modes[:, :, None], CELLS_Y * DEV_Y, y * DEV_Y + d)
        for x in range(CELLS_X):
            ty[d, :, x, :, x, :] = small
    ty = ty.reshape(DEV_Y, ROWS, ROWS)
    x = np.arange(CELLS_X)
    tx = np.zeros((DEV_X, 16, 4, CELLS_X, 4), np.float32)
    for d in range(DEV_X):
        small = cas(np.arange(16)[:, None], CELLS_X * DEV_X, x * DEV_X + d)
        for l in range(4):
            tx[d, :, l, :, l] = small
    tx = tx.reshape(DEV_X, 64, CELLS_X * 4).transpose(0, 2, 1)
    return tuple(t.astype(bf16) for t in (tz, ty, tx))


def dot(left, right):
    return jnp.dot(left, right, preferred_element_type=f32)


def dot_nt(left, right):
    return lax.dot_general(left, right, (((1,), (1,)), ((), ())), preferred_element_type=f32)


def dot_tn(left, right):
    return lax.dot_general(left, right, (((0,), (0,)), ((), ())), preferred_element_type=f32)


def split(v):
    high = v.astype(bf16)
    return high, (v - high.astype(f32)).astype(bf16)


def table_dot(table, v):
    high, low = split(v)
    return dot(table, high) + dot(table, low)


def table_dot_tn(table, v):
    high, low = split(v)
    return dot_tn(table, high) + dot_tn(table, low)


def slope_of(v, cdf):
    return cdf + v * jnp.exp(-0.5 * v * v) * inv_root_tau


def cdf_of(v):
    return 0.5 * (1.0 + lax.erf(v * inv_root_two))


def call(body, outs, *args, scratch=(), limit=8, raw=0):
    near = args[1 : 1 + raw]
    rest = args[1 + raw :]
    shapes = [pltpu.VMEM(*o) if len(o) == 2 else jax.ShapeDtypeStruct(*o[:2]) for o in outs]
    shapes = [pltpu.HBM(*o[:2]) if "raw" in o else v for o, v in zip(outs, shapes)]
    if INTERPRET:
        shapes = [jax.ShapeDtypeStruct(*o[:2]) for o in outs]
    else:
        near = [pltpu.with_memory_space_constraint(a, pltpu.HBM) for a in near]
        rest = [pltpu.with_memory_space_constraint(a, pltpu.VMEM) for a in rest]
    return pl.pallas_call(
        body,
        out_shape=shapes,
        in_specs=[pl.BlockSpec(memory_space=pltpu.SMEM)]
        + [pl.BlockSpec(memory_space=pl.ANY if INTERPRET else pltpu.HBM)] * raw
        + [pl.BlockSpec(memory_space=pltpu.VMEM)] * len(rest),
        out_specs=[
            pl.BlockSpec(memory_space=(pl.ANY if INTERPRET else pltpu.HBM) if "raw" in o else pltpu.VMEM)
            for o in outs
        ],
        scratch_shapes=[pltpu.VMEM(*s) if isinstance(s, tuple) else s for s in scratch],
        interpret=INTERPRET,
        compiler_params=pltpu.CompilerParams(vmem_limit_bytes=limit << 20),
    )(*args[:1], *near, *rest)


def at_x(at):
    return at[0] >> 4


def at_y(at):
    return (at[0] >> 2) & 3


def at_z(at):
    return at[0] & 3


def block(b):
    return slice(b * 256, (b + 1) * 256)


def store_parts(v, refs):
    for j, ref in enumerate(refs):
        ref[...] = v[:, j * 256 : (j + 1) * 256]


def fill_table(ka, mine, b, wide=16 * C):
    lane = lax.broadcasted_iota(jnp.int32, (C, wide), 1) & (C - 1)
    row = lax.broadcasted_iota(jnp.int32, (C, wide), 0)
    eye = jnp.where(lane == row, 1.0, 0.0)
    for z in range(4 * b, 4 * b + 4):
        ka[z * C : (z + 1) * C, :] = (eye * mine[z : z + 1, :wide]).astype(bf16)


def start_kernel(
    at, pre_from, grad_from, tz, dz_to, p1, p2, p3, mine,
    ka, total, pre, grad, dz, short, sems,
):
    def copies(b):
        cut = block(b)
        return (
            pltpu.make_async_copy(pre_from.at[:, cut], pre.at[:, cut], sems.at[b]),
            pltpu.make_async_copy(grad_from.at[:, cut], grad.at[:, cut], sems.at[8 + b]),
        )

    def leave(b):
        return pltpu.make_async_copy(dz.at[:, block(b)], dz_to.at[:, block(b)], sems.at[17 + b])

    first = pltpu.make_async_copy(tz.at[at_z(at)], short, sems.at[16])
    first.start()
    for b in range(8):
        for copy in copies(b):
            copy.start()
    first.wait()
    mine[...] = short[...].astype(f32)
    total[...] = jnp.zeros_like(total)
    for b in range(9):
        if b < 8:
            fill_table(ka, mine, b)
            for copy in copies(b):
                copy.wait()
            v = pre[:, block(b)].astype(f32)
            slope = slope_of(v, cdf_of(v))
            dz[:, block(b)] = (grad[:, block(b)].astype(f32) * slope).astype(bf16)
            leave(b).start()
        if b > 0:
            total[...] += dot(dz[:, block(b - 1)], ka[block(b - 1), 256:])
    store_parts(total[...], (p1, p2, p3))
    for b in range(8):
        leave(b).wait()


def own_kernel(at, mine, dz, p0, fold, ka):
    for b in range(8):
        fill_table(ka, mine, b, 256)
    p0[...] = dot(dz[...], ka[...])
    row = lax.broadcasted_iota(jnp.int32, (256, C), 0) >> 6
    lane = lax.broadcasted_iota(jnp.int32, (256, C), 1)
    for r in range(16):
        fold[r * 256 : (r + 1) * 256, :] = jnp.where(lane == row + 4 * r, 1.0, 0.0).astype(bf16)


def fill_point(square, point):
    square[...] = jnp.zeros_like(square)
    for i in range(4):
        square[i * C : (i + 1) * C, i * C : (i + 1) * C] = point[...]


def diagonal_sum(total):
    return sum(total[i * C : (i + 1) * C, i * C : (i + 1) * C] for i in range(4))


def side_kernel(
    at, pre, first, dz, mine, point, slope_to, local_to, weight, q0, q1, q2, q3,
    ka, mid, own, squares, square, slope, local, sems,
):
    fill_point(square, point)

    def leave(b):
        cut = block(b)
        return (
            pltpu.make_async_copy(slope.at[:, cut], slope_to.at[:, cut], sems.at[b]),
            pltpu.make_async_copy(local.at[:, cut], local_to.at[:, cut], sems.at[8 + b]),
        )

    own[...] = jnp.zeros_like(own)
    squares[...] = jnp.zeros_like(squares)
    for b in range(9):
        if b < 8:
            cut = block(b)
            fill_table(ka, mine, b)
            v = pre[:, cut].astype(f32)
            cdf = cdf_of(v)
            slope[:, cut] = slope_of(v, cdf)
            mid[:ROWS, cut] = (v * cdf).astype(bf16)
            mid[ROWS:, cut] = first[:, cut]
            local[:, cut] = dot_nt(dz[:, cut], square[...])
            for copy in leave(b):
                copy.start()
        if b > 0:
            cut = block(b - 1)
            squares[...] += dot_tn(mid[:ROWS, cut], dz[:, cut])
            own[...] += dot(mid[:, cut], ka[cut, :])
    weight[...] = diagonal_sum(squares[...])
    for j, ref in enumerate((q0, q1, q2, q3)):
        ref[:, :256] = own[:ROWS, j * 256 : (j + 1) * 256]
        ref[:, 256:] = own[ROWS:, j * 256 : (j + 1) * 256]
    for b in range(8):
        for copy in leave(b):
            copy.wait()


def side_one_kernel(at, first, dz, mine, weight_two, sent, p0, ka):
    for b in range(8):
        fill_table(ka, mine, b, 256)
    squares = dot_tn(first[:, :256], dz[:, :256])
    for b in range(1, 8):
        squares = squares + dot_tn(first[:, block(b)], dz[:, block(b)])
    p0[...] = dot(dz[...], ka[...])
    both = jnp.concatenate([weight_two[...], diagonal_sum(squares)], axis=1) * SCALE_B
    sent[...] = jnp.concatenate([both[:32], both[32:]], axis=1)


def local_kernel(at, dz, point, local_to, square, local, sems):
    fill_point(square, point)

    def leave(b):
        return pltpu.make_async_copy(local.at[:, block(b)], local_to.at[:, block(b)], sems.at[b])

    for b in range(8):
        local[:, block(b)] = dot_nt(dz[:, block(b)], square[...])
        leave(b).start()
    for b in range(8):
        leave(b).wait()


def total_of(refs):
    return (refs[0][...] + refs[1][...]) + (refs[2][...] + refs[3][...])


def along_y_kernel(at, a, b, c, d, ty, near, far):
    out = table_dot(ty[at_y(at)], total_of((a, b, c, d)))
    near[...] = out[:64]
    far[...] = out[64:]


def along_y_join_kernel(at, a, b, c, d, ty, ins_near, ins_far, sent, near, far):
    out = table_dot(ty[at_y(at)], total_of((a, b, c, d)))
    for ref, ins, here in ((near, ins_near, out[:64]), (far, ins_far, out[64:])):
        ref[:, :256] = here
        ref[:, 256:768] = ins[...]
        ref[:32, 768:] = sent[...]
        ref[32:, 768:] = jnp.zeros((32, 256), f32)


def keep_kernel(at, near, got, keep, send):
    v = near[...] + got[...]
    keep[...] = v[:32]
    wide = min(v.shape[1], 768)
    send[:, :wide] = v[32:, :wide]
    if v.shape[1] > 768:
        send[:, 768:] = v[:32, 768:]


def pair_kernel(at, a, b, out):
    out[:32] = a[...]
    out[32:] = b[...]


def along_x_kernel(at, a, b, tx, out):
    v = a[...] + b[...]
    modes = table_dot_tn(tx[at_x(at)], v[:, : min(v.shape[1], 768)])
    for i in range(16):
        out[i, :, : modes.shape[1]] = modes[i * 4 : (i + 1) * 4]
    if v.shape[1] > 768:
        weight = jnp.concatenate([v[:, 768:896], v[:, 896:]], axis=0)
        for i in range(16):
            out[i, :, 768:] = weight[i * 4 : (i + 1) * 4]


def mixed(hat, spectral, wide, fold):
    wide[...] = spectral[0].astype(f32)
    products = []
    for k in range(4):
        h = hat[:, k * C : (k + 1) * C]
        h = jnp.concatenate([h, h], axis=1)
        products.append(wide[:, k, :] * jnp.concatenate([h] * 32, axis=1))
    high, low = split(jnp.concatenate(products, axis=0))
    out = dot(jnp.concatenate([high, low], axis=0), fold[...])
    out = (out[:16] + out[16:]) * SCALE_A
    return jnp.concatenate([out[k * 4 : (k + 1) * 4] for k in range(4)], axis=1)


def sixteen(got):
    v = [got[i] for i in range(16)]
    while len(v) > 1:
        v = [v[i] + v[i + 1] for i in range(0, len(v), 2)]
    return v[0]


def mix_two_kernel(at, got, spectral, fold, back, hat_out, wide):
    hat = sixteen(got) * SCALE_B
    hat_out[...] = hat
    out = mixed(hat, spectral, wide, fold)
    for i in range(16):
        back[i] = out


def mix_one_kernel(at, got, spectral, fold, back, hat_out, mid_out, first_out, wide):
    v = sixteen(got)
    hat = v[:, :256] * SCALE_B
    hat_out[...] = hat
    mid_out[...] = v[:, 256:512] * SCALE_A
    first_out[...] = v[:, 512:768] * SCALE_A
    out = mixed(hat, spectral, wide, fold)
    for i in range(16):
        back[i, :, :256] = out
        back[i, :, 256:] = v[:, 768:]


def outer_kernel(at, left, right, fold, out):
    lefts = []
    rights = []
    for k in range(4):
        cut = slice(k * C, (k + 1) * C)
        h = right[:, cut]
        lefts.append(left[:, cut])
        rights.append(jnp.concatenate([h, h], axis=1))
    v = jnp.concatenate(lefts, axis=0)
    high, rest = v.astype(bf16), v - v.astype(bf16).astype(f32)
    low, last = split(rest)
    spread_left = dot_nt(jnp.concatenate([high, low, last], axis=0), fold[...])
    tall = jnp.concatenate(rights, axis=0)
    whole = (spread_left[:16] + spread_left[16:32]) + spread_left[32:]
    whole = whole * jnp.concatenate([tall] * 32, axis=1)
    for k in range(4):
        out[:, k, :] = whole[k * 4 : (k + 1) * 4]


def back_x_kernel(at, got, tx, out):
    v = jnp.concatenate([got[i] for i in range(16)], axis=0)
    out[...] = table_dot(tx[at_x(at)], v)


def back_x_one_kernel(at, got, tx, out, weight):
    v = jnp.concatenate([got[i] for i in range(16)], axis=0)
    out[...] = table_dot(tx[at_x(at)], v[:, :256])
    weight[...] = jnp.concatenate([v[:32, 256:], v[32:, 256:]], axis=1)


def back_y_kernel(at, a, b, ty, out):
    v = jnp.concatenate([a[...], b[...]], axis=0)
    out[...] = table_dot_tn(ty[at_y(at)], v)


def back_y_one_kernel(at, a, b, ty, weight, out):
    v = jnp.concatenate([a[...], b[...]], axis=0)
    out[:ROWS] = table_dot_tn(ty[at_y(at)], v)
    out[ROWS:] = weight[...]


def stack_modes(refs, modes):
    for j, ref in enumerate(refs):
        modes[:, j * 256 : (j + 1) * 256] = ref[:ROWS].astype(bf16)


def middle_kernel(
    at, local_from, slope_from, a, b, c, d, mine, dz_to, p1, p2, p3,
    modes, total, dz, ka, local, slope, sems,
):
    def copies(i):
        cut = block(i)
        return (
            pltpu.make_async_copy(local_from.at[:, cut], local.at[:, cut], sems.at[i]),
            pltpu.make_async_copy(slope_from.at[:, cut], slope.at[:, cut], sems.at[8 + i]),
        )

    def leave(i):
        return pltpu.make_async_copy(dz.at[:, block(i)], dz_to.at[:, block(i)], sems.at[16 + i])

    for i in range(8):
        for copy in copies(i):
            copy.start()
    stack_modes((a, b, c, d), modes)
    total[...] = jnp.zeros_like(total)
    fill_table(ka, mine, 0)
    for i in range(9):
        if i < 8:
            if i < 7:
                fill_table(ka, mine, i + 1)
            for copy in copies(i):
                copy.wait()
            down = dot_nt(modes[...], ka[block(i), :]) + local[:, block(i)]
            dz[:, block(i)] = (down * slope[:, block(i)]).astype(bf16)
            leave(i).start()
        if i > 0:
            total[...] += dot(dz[:, block(i - 1)], ka[block(i - 1), 256:])
    store_parts(total[...], (p1, p2, p3))
    for i in range(8):
        leave(i).wait()


def end_kernel(
    at, local_from, a, b, c, d, mine, out_to, weight_two, weight_one,
    modes, out, ka, local, sems,
):
    def copy(i):
        return pltpu.make_async_copy(local_from.at[:, block(i)], local.at[:, block(i)], sems.at[i])

    def leave(i):
        return pltpu.make_async_copy(out.at[:, block(i)], out_to.at[:, block(i)], sems.at[8 + i])

    for i in range(8):
        copy(i).start()
    stack_modes((a, b, c, d), modes)
    fill_table(ka, mine, 0)
    for i in range(8):
        if i < 7:
            fill_table(ka, mine, i + 1)
        copy(i).wait()
        down = dot_nt(modes[...], ka[block(i), :]) + local[:, block(i)]
        out[:, block(i)] = down.astype(bf16)
        leave(i).start()
    w = (a[ROWS:] + b[ROWS:]) + (c[ROWS:] + d[ROWS:])
    w = jnp.concatenate([w[:, :128], w[:, 128:]], axis=0)
    weight_two[...] = w[:, :C]
    weight_one[...] = w[:, C:]
    for i in range(8):
        leave(i).wait()


def shift_pairs(kind, s):
    return kind, [(i, i ^ s if kind == "gy" else (i + s) % 4) for i in range(4)]


def shifted(v, kind, s):
    axis, pairs = shift_pairs(kind, s)
    return lax.ppermute(v, axis, pairs)


def exchange(parts, kind):
    return [parts[0]] + [shifted(parts[s], kind, s) for s in (1, 2, 3)]


def spread(v, kind):
    return [v] + [shifted(v, kind, s) for s in (3, 2, 1)]


def reduce_y(at, near, far, width):
    keep, send = call(
        keep_kernel, [((32, width), f32)] * 2, at, near, shifted(far, "gy", 1)
    )
    return keep, shifted(send, "gy", 2)


def spread_y(at, v):
    (pair,) = call(pair_kernel, [((64, 256), f32)], at, v, shifted(v, "gy", 2))
    return pair, shifted(pair, "gy", 1)


def over_x(v):
    return lax.all_to_all(v, "gz", 0, 0, tiled=True)


def on_device(
    grid_input, pre_one, pre_two, grad_output, spectral_one, spectral_two, point_one, point_two
):
    tz, ty, tx = [jnp.asarray(t) for t in build_tables()]
    at = lax.axis_index(("gz", "gy", "gx")).reshape(1)
    first, pre_one, pre_two, upstream = [
        t.reshape(ROWS, WIDE) for t in (grid_input, pre_one, pre_two, grad_output)
    ]
    big = (ROWS, WIDE)
    half = ((ROWS, 256), f32)
    table = ((WIDE, 16 * C), bf16)
    native = ((4, 4, C * C), f32)
    dma = pltpu.SemaphoreType.DMA

    dz_two, *parts, mine = call(
        start_kernel,
        [(big, bf16, "raw")] + [half] * 3 + [((CELLS_Z, 16 * C), f32)],
        at,
        pre_two,
        upstream,
        tz,
        raw=3,
        scratch=[
            table,
            ((ROWS, 12 * C), f32),
            (big, bf16),
            (big, bf16),
            (big, bf16),
            ((CELLS_Z, 16 * C), bf16),
            dma((25,)),
        ],
    )
    own, fold = call(
        own_kernel,
        [half, ((C * C, C), bf16)],
        at,
        mine,
        dz_two,
        scratch=[((WIDE, 256), bf16)],
    )
    got = exchange([own] + parts, "gx")
    near, far = call(along_y_kernel, [((64, 256), f32)] * 2, at, *got, ty)
    got = reduce_y(at, near, far, 256)
    (modes,) = call(along_x_kernel, [((16, 4, 256), f32)], at, *got, tx)
    modes, pre_one, dz_side = lax.optimization_barrier((modes, pre_one, dz_two))
    slope, local_two, weight_two, *ins = call(
        side_kernel,
        [(big, f32, "raw")] * 2 + [((C, C), f32, 0)] + [((ROWS, 512), f32)] * 4,
        at,
        pre_one,
        first,
        dz_side,
        mine,
        point_two,
        limit=14,
        scratch=[
            table,
            ((2 * ROWS, WIDE), bf16),
            ((2 * ROWS, 16 * C), f32),
            ((256, 256), f32),
            ((256, 256), bf16),
            (big, f32),
            (big, f32),
            dma((16,)),
        ],
    )
    got = over_x(modes)
    got, ins = lax.optimization_barrier((got, ins))
    got_in = exchange(ins, "gx")
    back, hat_two = call(
        mix_two_kernel,
        [((16, 4, 256), f32), ((4, 256), f32)],
        at,
        got,
        spectral_two,
        fold,
        scratch=[native],
    )
    got = over_x(back)
    got, got_in = lax.optimization_barrier((got, got_in))
    (tall,) = call(back_x_kernel, [((32, 256), f32)], at, got, tx)
    got = spread_y(at, tall)
    (tall,) = call(back_y_kernel, [half], at, *got, ty)
    got = spread(tall, "gx")
    ins = call(along_y_kernel, [((64, 512), f32)] * 2, at, *got_in, ty)
    dz_one, *parts = call(
        middle_kernel,
        [(big, bf16, "raw")] + [half] * 3,
        at,
        local_two,
        slope,
        *got,
        mine,
        raw=2,
        limit=12,
        scratch=[
            ((ROWS, 16 * C), bf16),
            ((ROWS, 12 * C), f32),
            (big, bf16),
            table,
            (big, f32),
            (big, f32),
            dma((24,)),
        ],
    )
    sent, own = call(
        side_one_kernel,
        [((32, 256), f32), half],
        at,
        first,
        dz_one,
        mine,
        weight_two,
        scratch=[((WIDE, 256), bf16)],
    )
    got = exchange([own] + parts, "gx")
    near, far = call(along_y_join_kernel, [((64, 1024), f32)] * 2, at, *got, ty, *ins, sent)
    got = reduce_y(at, near, far, 1024)
    (modes,) = call(along_x_kernel, [((16, 4, 896), f32)], at, *got, tx)
    back, hat_one, mid_hat, first_hat = call(
        mix_one_kernel,
        [((16, 4, 384), f32)] + [((4, 256), f32)] * 3,
        at,
        over_x(modes),
        spectral_one,
        fold,
        scratch=[native],
    )
    (spec_two,) = call(outer_kernel, [(*native, 0)], at, mid_hat, hat_two, fold)
    (spec_one,) = call(outer_kernel, [(*native, 0)], at, first_hat, hat_one, fold)
    back, dz_late = lax.optimization_barrier((back, dz_one))
    (local_one,) = call(
        local_kernel,
        [(big, f32, "raw")],
        at,
        dz_late,
        point_one,
        scratch=[((256, 256), bf16), (big, f32), dma((8,))],
    )
    got = over_x(back)
    got, local_one = lax.optimization_barrier((got, local_one))
    tall, weight = call(back_x_one_kernel, [((32, 256), f32)] * 2, at, got, tx)
    got = spread_y(at, tall)
    (tall,) = call(back_y_one_kernel, [((ROWS + 32, 256), f32)], at, *got, ty, weight)
    got = spread(tall, "gx")
    input_grad, weight_two, weight_one = call(
        end_kernel,
        [(big, bf16, "raw"), ((C, C), f32, 0), ((C, C), f32, 0)],
        at,
        local_one,
        *got,
        mine,
        raw=1,
        scratch=[((ROWS, 16 * C), bf16), (big, bf16), table, (big, f32), dma((16,))],
    )
    return (
        input_grad.reshape(CELLS_X, CELLS_Y, WIDE),
        spec_one[None],
        spec_two[None],
        weight_one,
        weight_two,
    )


def solution(mesh):
    grid = P("gz", "gy", "gx")
    modes = P("gz", "gy", "gx", None)
    return jax.shard_map(
        on_device,
        mesh=mesh,
        in_specs=(grid, grid, grid, grid, modes, modes, P(), P()),
        out_specs=(grid, modes, modes, P(), P()),
        check_vma=False,
    )
```

```python
import jax
import jax.numpy as jnp
import numpy as np
from jax import lax
from jax.experimental import pallas as pl
from jax.experimental.pallas import tpu as pltpu
from jax.sharding import PartitionSpec as P


INTERPRET = False

C = 64
CELLS_X, CELLS_Y, CELLS_Z = 8, 16, 32
DEV_X, DEV_Y, DEV_Z = 16, 4, 4
ROWS = CELLS_X * CELLS_Y
WIDE = CELLS_Z * C
TOTAL_CELLS = CELLS_X * DEV_X * CELLS_Y * DEV_Y * CELLS_Z * DEV_Z
TOTAL_MODES = 16**3
SCALE_A = (TOTAL_CELLS * TOTAL_MODES) ** (-0.25)
SCALE_B = TOTAL_CELLS ** (-0.5)

inv_root_two = 0.7071067811865476
inv_root_tau = 0.3989422804014327
bf16 = jnp.bfloat16
f32 = jnp.float32


def cas(mode, length, position):
    mode = np.asarray(mode)
    freq = np.where(mode < 8, mode, length - 16 + mode)
    phase = (freq * position % length) * (2.0 * np.pi / length)
    return (np.cos(phase) + np.sin(phase)).astype(np.float32)


def build_tables():
    four = np.arange(4)
    z = np.arange(CELLS_Z)
    tz = np.zeros((DEV_Z, CELLS_Z, 16), np.float32)
    for d in range(DEV_Z):
        modes = (((d + four) % 4)[:, None] * 4 + four[None, :]).reshape(-1)
        tz[d] = cas(modes[None, :], CELLS_Z * DEV_Z, z[:, None] * DEV_Z + d)
    tz_back = np.repeat(tz.transpose(0, 2, 1), C, axis=2)
    tz = np.repeat(tz, C, axis=2)
    y = np.arange(CELLS_Y)
    ty = np.zeros((DEV_Y, 4, CELLS_X, 4, CELLS_X, CELLS_Y), np.float32)
    for d in range(DEV_Y):
        modes = (d ^ np.array([0, 2, 1, 3]))[:, None] * 4 + four[None, :]
        small = cas(modes[:, :, None], CELLS_Y * DEV_Y, y * DEV_Y + d)
        for x in range(CELLS_X):
            ty[d, :, x, :, x, :] = small
    ty = ty.reshape(DEV_Y, ROWS, ROWS)
    x = np.arange(CELLS_X)
    tx = np.zeros((DEV_X, 16, 4, CELLS_X, 4), np.float32)
    for d in range(DEV_X):
        small = cas(np.arange(16)[:, None], CELLS_X * DEV_X, x * DEV_X + d)
        for l in range(4):
            tx[d, :, l, :, l] = small
    tx = tx.reshape(DEV_X, 64, CELLS_X * 4).transpose(0, 2, 1)
    return tuple(t.astype(bf16) for t in (tz, tz_back, ty, tx))


def dot(left, right):
    return jnp.dot(left, right, preferred_element_type=f32)


def dot_nt(left, right):
    return lax.dot_general(left, right, (((1,), (1,)), ((), ())), preferred_element_type=f32)


def dot_tn(left, right):
    return lax.dot_general(left, right, (((0,), (0,)), ((), ())), preferred_element_type=f32)


def split(v):
    high = v.astype(bf16)
    return high, (v - high.astype(f32)).astype(bf16)


def table_dot(table, v):
    high, low = split(v)
    return dot(table, high) + dot(table, low)


def table_dot_tn(table, v):
    high, low = split(v)
    return dot_tn(table, high) + dot_tn(table, low)


def slope_of(v, cdf):
    return cdf + v * jnp.exp(-0.5 * v * v) * inv_root_tau


def cdf_of(v):
    return 0.5 * (1.0 + lax.erf(v * inv_root_two))


def call(body, outs, *args, scratch=(), limit=8, raw=0):
    near = args[1 : 1 + raw]
    rest = args[1 + raw :]
    shapes = [pltpu.VMEM(*o) if len(o) == 2 else jax.ShapeDtypeStruct(*o[:2]) for o in outs]
    shapes = [pltpu.HBM(*o[:2]) if "raw" in o else v for o, v in zip(outs, shapes)]
    if INTERPRET:
        shapes = [jax.ShapeDtypeStruct(*o[:2]) for o in outs]
    else:
        near = [pltpu.with_memory_space_constraint(a, pltpu.HBM) for a in near]
        rest = [pltpu.with_memory_space_constraint(a, pltpu.VMEM) for a in rest]
    return pl.pallas_call(
        body,
        out_shape=shapes,
        in_specs=[pl.BlockSpec(memory_space=pltpu.SMEM)]
        + [pl.BlockSpec(memory_space=pl.ANY if INTERPRET else pltpu.HBM)] * raw
        + [pl.BlockSpec(memory_space=pltpu.VMEM)] * len(rest),
        out_specs=[
            pl.BlockSpec(memory_space=(pl.ANY if INTERPRET else pltpu.HBM) if "raw" in o else pltpu.VMEM)
            for o in outs
        ],
        scratch_shapes=[pltpu.VMEM(*s) if isinstance(s, tuple) else s for s in scratch],
        interpret=INTERPRET,
        compiler_params=pltpu.CompilerParams(vmem_limit_bytes=limit << 20),
    )(*args[:1], *near, *rest)


def at_x(at):
    return at[0] >> 4


def at_y(at):
    return (at[0] >> 2) & 3


def at_z(at):
    return at[0] & 3


def block(b):
    return slice(b * 256, (b + 1) * 256)


def store_parts(v, refs):
    for j, ref in enumerate(refs):
        ref[...] = v[:, j * 256 : (j + 1) * 256]


def fill_table(ka, mine, b, wide=16 * C):
    lane = lax.broadcasted_iota(jnp.int32, (C, wide), 1) & (C - 1)
    row = lax.broadcasted_iota(jnp.int32, (C, wide), 0)
    eye = jnp.where(lane == row, 1.0, 0.0)
    for z in range(4 * b, 4 * b + 4):
        ka[z * C : (z + 1) * C, :] = (eye * mine[z : z + 1, :wide]).astype(bf16)


def fill_back(ka, mine, b):
    lane = lax.broadcasted_iota(jnp.int32, (C, 256), 1) & (C - 1)
    row = lax.broadcasted_iota(jnp.int32, (C, 256), 0)
    eye = jnp.where(lane == row, 1.0, 0.0)
    for k in range(16):
        ka[k * C : (k + 1) * C, block(b)] = (eye * mine[k : k + 1, block(b)]).astype(bf16)


def start_kernel(
    at, pre_from, grad_from, tz, tz_back, dz_to, p1, p2, p3, mine, mine_back,
    ka, total, pre, grad, dz, short, short_back, sems,
):
    def copies(b):
        cut = block(b)
        return (
            pltpu.make_async_copy(pre_from.at[:, cut], pre.at[:, cut], sems.at[b]),
            pltpu.make_async_copy(grad_from.at[:, cut], grad.at[:, cut], sems.at[8 + b]),
        )

    def leave(b):
        return pltpu.make_async_copy(dz.at[:, block(b)], dz_to.at[:, block(b)], sems.at[17 + b])

    first = pltpu.make_async_copy(tz.at[at_z(at)], short, sems.at[16])
    first.start()
    for b in range(8):
        for copy in copies(b):
            copy.start()
    second = pltpu.make_async_copy(tz_back.at[at_z(at)], short_back, sems.at[25])
    second.start()
    first.wait()
    mine[...] = short[...].astype(f32)
    total[...] = jnp.zeros_like(total)
    for b in range(9):
        if b < 8:
            fill_table(ka, mine, b)
            for copy in copies(b):
                copy.wait()
            v = pre[:, block(b)].astype(f32)
            slope = slope_of(v, cdf_of(v))
            dz[:, block(b)] = (grad[:, block(b)].astype(f32) * slope).astype(bf16)
            leave(b).start()
        if b > 0:
            total[...] += dot(dz[:, block(b - 1)], ka[block(b - 1), 256:])
    store_parts(total[...], (p1, p2, p3))
    second.wait()
    mine_back[...] = short_back[...].astype(f32)
    for b in range(8):
        leave(b).wait()


def own_kernel(at, mine, dz, p0, fold, ka):
    for b in range(8):
        fill_table(ka, mine, b, 256)
    p0[...] = dot(dz[...], ka[...])
    row = lax.broadcasted_iota(jnp.int32, (256, C), 0) >> 6
    lane = lax.broadcasted_iota(jnp.int32, (256, C), 1)
    for r in range(16):
        fold[r * 256 : (r + 1) * 256, :] = jnp.where(lane == row + 4 * r, 1.0, 0.0).astype(bf16)


def fill_point(square, point):
    square[...] = jnp.zeros_like(square)
    for i in range(4):
        square[i * C : (i + 1) * C, i * C : (i + 1) * C] = point[...]


def diagonal_sum(total):
    return sum(total[i * C : (i + 1) * C, i * C : (i + 1) * C] for i in range(4))


def side_kernel(
    at, pre, first, dz, mine, point, slope_to, local_to, weight, q0, q1, q2, q3,
    ka, mid, own, squares, square, slope, local, sems,
):
    fill_point(square, point)

    def leave(b):
        cut = block(b)
        return (
            pltpu.make_async_copy(slope.at[:, cut], slope_to.at[:, cut], sems.at[b]),
            pltpu.make_async_copy(local.at[:, cut], local_to.at[:, cut], sems.at[8 + b]),
        )

    own[...] = jnp.zeros_like(own)
    squares[...] = jnp.zeros_like(squares)
    for b in range(9):
        if b < 8:
            cut = block(b)
            fill_table(ka, mine, b)
            v = pre[:, cut].astype(f32)
            cdf = cdf_of(v)
            slope[:, cut] = slope_of(v, cdf)
            mid[:ROWS, cut] = (v * cdf).astype(bf16)
            mid[ROWS:, cut] = first[:, cut]
            local[:, cut] = dot_nt(dz[:, cut], square[...])
            for copy in leave(b):
                copy.start()
        if b > 0:
            cut = block(b - 1)
            squares[...] += dot_tn(mid[:ROWS, cut], dz[:, cut])
            own[...] += dot(mid[:, cut], ka[cut, :])
    weight[...] = diagonal_sum(squares[...])
    for j, ref in enumerate((q0, q1, q2, q3)):
        ref[:, :256] = own[:ROWS, j * 256 : (j + 1) * 256]
        ref[:, 256:] = own[ROWS:, j * 256 : (j + 1) * 256]
    for b in range(8):
        for copy in leave(b):
            copy.wait()


def side_one_kernel(at, first, dz, mine, weight_two, sent, p0, ka):
    for b in range(8):
        fill_table(ka, mine, b, 256)
    squares = dot_tn(first[:, :256], dz[:, :256])
    for b in range(1, 8):
        squares = squares + dot_tn(first[:, block(b)], dz[:, block(b)])
    p0[...] = dot(dz[...], ka[...])
    both = jnp.concatenate([weight_two[...], diagonal_sum(squares)], axis=1) * SCALE_B
    sent[...] = jnp.concatenate([both[:32], both[32:]], axis=1)


def local_kernel(at, dz, point, local_to, square, local, sems):
    fill_point(square, point)

    def leave(b):
        return pltpu.make_async_copy(local.at[:, block(b)], local_to.at[:, block(b)], sems.at[b])

    for b in range(8):
        local[:, block(b)] = dot_nt(dz[:, block(b)], square[...])
        leave(b).start()
    for b in range(8):
        leave(b).wait()


def total_of(refs):
    return (refs[0][...] + refs[1][...]) + (refs[2][...] + refs[3][...])


def along_y_kernel(at, a, b, c, d, ty, near, far):
    out = table_dot(ty[at_y(at)], total_of((a, b, c, d)))
    near[...] = out[:64]
    far[...] = out[64:]


def along_y_join_kernel(at, a, b, c, d, ty, ins_near, ins_far, sent, near, far):
    out = table_dot(ty[at_y(at)], total_of((a, b, c, d)))
    for ref, ins, here in ((near, ins_near, out[:64]), (far, ins_far, out[64:])):
        ref[:, :256] = here
        ref[:, 256:768] = ins[...]
        ref[:32, 768:] = sent[...]
        ref[32:, 768:] = jnp.zeros((32, 256), f32)


def keep_kernel(at, near, got, keep, send):
    v = near[...] + got[...]
    keep[...] = v[:32]
    wide = min(v.shape[1], 768)
    send[:, :wide] = v[32:, :wide]
    if v.shape[1] > 768:
        send[:, 768:] = v[:32, 768:]


def pair_kernel(at, a, b, out):
    out[:32] = a[...]
    out[32:] = b[...]


def along_x_kernel(at, a, b, tx, out):
    v = a[...] + b[...]
    modes = table_dot_tn(tx[at_x(at)], v[:, : min(v.shape[1], 768)])
    for i in range(16):
        out[i, :, : modes.shape[1]] = modes[i * 4 : (i + 1) * 4]
    if v.shape[1] > 768:
        weight = jnp.concatenate([v[:, 768:896], v[:, 896:]], axis=0)
        for i in range(16):
            out[i, :, 768:] = weight[i * 4 : (i + 1) * 4]


def mixed(hat, spectral, wide, fold):
    wide[...] = spectral[0].astype(f32)
    products = []
    for k in range(4):
        h = hat[:, k * C : (k + 1) * C]
        h = jnp.concatenate([h, h], axis=1)
        products.append(wide[:, k, :] * jnp.concatenate([h] * 32, axis=1))
    high, low = split(jnp.concatenate(products, axis=0))
    out = dot(jnp.concatenate([high, low], axis=0), fold[...])
    out = (out[:16] + out[16:]) * SCALE_A
    return jnp.concatenate([out[k * 4 : (k + 1) * 4] for k in range(4)], axis=1)


def sixteen(got):
    v = [got[i] for i in range(16)]
    while len(v) > 1:
        v = [v[i] + v[i + 1] for i in range(0, len(v), 2)]
    return v[0]


def mix_two_kernel(at, got, spectral, fold, back, hat_out, wide):
    hat = sixteen(got) * SCALE_B
    hat_out[...] = hat
    out = mixed(hat, spectral, wide, fold)
    for i in range(16):
        back[i] = out


def mix_one_kernel(at, got, spectral, fold, back, hat_out, mid_out, first_out, wide):
    v = sixteen(got)
    hat = v[:, :256] * SCALE_B
    hat_out[...] = hat
    mid_out[...] = v[:, 256:512] * SCALE_A
    first_out[...] = v[:, 512:768] * SCALE_A
    out = mixed(hat, spectral, wide, fold)
    for i in range(16):
        back[i, :, :256] = out
        back[i, :, 256:] = v[:, 768:]


def outer_kernel(at, left, right, fold, out):
    lefts = []
    rights = []
    for k in range(4):
        cut = slice(k * C, (k + 1) * C)
        h = right[:, cut]
        lefts.append(left[:, cut])
        rights.append(jnp.concatenate([h, h], axis=1))
    v = jnp.concatenate(lefts, axis=0)
    high, rest = v.astype(bf16), v - v.astype(bf16).astype(f32)
    low, last = split(rest)
    spread_left = dot_nt(jnp.concatenate([high, low, last], axis=0), fold[...])
    tall = jnp.concatenate(rights, axis=0)
    whole = (spread_left[:16] + spread_left[16:32]) + spread_left[32:]
    whole = whole * jnp.concatenate([tall] * 32, axis=1)
    for k in range(4):
        out[:, k, :] = whole[k * 4 : (k + 1) * 4]


def back_x_kernel(at, got, tx, out):
    v = jnp.concatenate([got[i] for i in range(16)], axis=0)
    out[...] = table_dot(tx[at_x(at)], v)


def back_x_one_kernel(at, got, tx, out, weight):
    v = jnp.concatenate([got[i] for i in range(16)], axis=0)
    out[...] = table_dot(tx[at_x(at)], v[:, :256])
    weight[...] = jnp.concatenate([v[:32, 256:], v[32:, 256:]], axis=1)


def back_y_kernel(at, a, b, ty, out):
    v = jnp.concatenate([a[...], b[...]], axis=0)
    out[...] = table_dot_tn(ty[at_y(at)], v)


def back_y_one_kernel(at, a, b, ty, weight, out):
    v = jnp.concatenate([a[...], b[...]], axis=0)
    out[:ROWS] = table_dot_tn(ty[at_y(at)], v)
    out[ROWS:] = weight[...]


def stack_modes(refs, modes):
    for j, ref in enumerate(refs):
        modes[:, j * 256 : (j + 1) * 256] = ref[:ROWS].astype(bf16)


def middle_kernel(
    at, local_from, slope_from, a, b, c, d, mine, mine_back, dz_to, p1, p2, p3,
    modes, total, dz, ka, ka_back, local, slope, sems,
):
    def copies(i):
        cut = block(i)
        return (
            pltpu.make_async_copy(local_from.at[:, cut], local.at[:, cut], sems.at[i]),
            pltpu.make_async_copy(slope_from.at[:, cut], slope.at[:, cut], sems.at[8 + i]),
        )

    def leave(i):
        return pltpu.make_async_copy(dz.at[:, block(i)], dz_to.at[:, block(i)], sems.at[16 + i])

    for i in range(8):
        for copy in copies(i):
            copy.start()
    stack_modes((a, b, c, d), modes)
    total[...] = jnp.zeros_like(total)
    fill_back(ka_back, mine_back, 0)
    for i in range(9):
        if i < 8:
            if i < 7:
                fill_back(ka_back, mine_back, i + 1)
            fill_table(ka, mine, i)
            for copy in copies(i):
                copy.wait()
            down = dot(modes[...], ka_back[:, block(i)]) + local[:, block(i)]
            dz[:, block(i)] = (down * slope[:, block(i)]).astype(bf16)
            leave(i).start()
        if i > 0:
            total[...] += dot(dz[:, block(i - 1)], ka[block(i - 1), 256:])
    store_parts(total[...], (p1, p2, p3))
    for i in range(8):
        leave(i).wait()


def end_kernel(
    at, a, b, c, d, mine, local, out_to, weight_two, weight_one, modes, out, ka, sems
):
    def leave(i):
        return pltpu.make_async_copy(out.at[:, block(i)], out_to.at[:, block(i)], sems.at[i])

    stack_modes((a, b, c, d), modes)
    fill_back(ka, mine, 0)
    for i in range(8):
        if i < 7:
            fill_back(ka, mine, i + 1)
        down = dot(modes[...], ka[:, block(i)]) + local[:, block(i)]
        out[:, block(i)] = down.astype(bf16)
        leave(i).start()
    w = (a[ROWS:] + b[ROWS:]) + (c[ROWS:] + d[ROWS:])
    w = jnp.concatenate([w[:, :128], w[:, 128:]], axis=0)
    weight_two[...] = w[:, :C]
    weight_one[...] = w[:, C:]
    for i in range(8):
        leave(i).wait()


def shift_pairs(kind, s):
    return kind, [(i, i ^ s if kind == "gy" else (i + s) % 4) for i in range(4)]


def shifted(v, kind, s):
    axis, pairs = shift_pairs(kind, s)
    return lax.ppermute(v, axis, pairs)


def exchange(parts, kind):
    return [parts[0]] + [shifted(parts[s], kind, s) for s in (1, 2, 3)]


def spread(v, kind):
    return [v] + [shifted(v, kind, s) for s in (3, 2, 1)]


def reduce_y(at, near, far, width):
    keep, send = call(
        keep_kernel, [((32, width), f32)] * 2, at, near, shifted(far, "gy", 1)
    )
    return keep, shifted(send, "gy", 2)


def spread_y(at, v):
    (pair,) = call(pair_kernel, [((64, 256), f32)], at, v, shifted(v, "gy", 2))
    return pair, shifted(pair, "gy", 1)


def over_x(v):
    return lax.all_to_all(v, "gz", 0, 0, tiled=True)


def on_device(
    grid_input, pre_one, pre_two, grad_output, spectral_one, spectral_two, point_one, point_two
):
    tz, tz_back, ty, tx = [jnp.asarray(t) for t in build_tables()]
    at = lax.axis_index(("gz", "gy", "gx")).reshape(1)
    first, pre_one, pre_two, upstream = [
        t.reshape(ROWS, WIDE) for t in (grid_input, pre_one, pre_two, grad_output)
    ]
    big = (ROWS, WIDE)
    half = ((ROWS, 256), f32)
    table = ((WIDE, 16 * C), bf16)
    table_back = ((16 * C, WIDE), bf16)
    native = ((4, 4, C * C), f32)
    dma = pltpu.SemaphoreType.DMA

    dz_two, *parts, mine, mine_back = call(
        start_kernel,
        [(big, bf16, "raw")] + [half] * 3 + [((CELLS_Z, 16 * C), f32), ((16, WIDE), f32)],
        at,
        pre_two,
        upstream,
        tz,
        tz_back,
        raw=4,
        scratch=[
            table,
            ((ROWS, 12 * C), f32),
            (big, bf16),
            (big, bf16),
            (big, bf16),
            ((CELLS_Z, 16 * C), bf16),
            ((16, WIDE), bf16),
            dma((26,)),
        ],
    )
    own, fold = call(
        own_kernel,
        [half, ((C * C, C), bf16)],
        at,
        mine,
        dz_two,
        scratch=[((WIDE, 256), bf16)],
    )
    got = exchange([own] + parts, "gx")
    near, far = call(along_y_kernel, [((64, 256), f32)] * 2, at, *got, ty)
    got = reduce_y(at, near, far, 256)
    (modes,) = call(along_x_kernel, [((16, 4, 256), f32)], at, *got, tx)
    modes, pre_one, dz_side = lax.optimization_barrier((modes, pre_one, dz_two))
    slope, local_two, weight_two, *ins = call(
        side_kernel,
        [(big, f32, "raw")] * 2 + [((C, C), f32, 0)] + [((ROWS, 512), f32)] * 4,
        at,
        pre_one,
        first,
        dz_side,
        mine,
        point_two,
        limit=14,
        scratch=[
            table,
            ((2 * ROWS, WIDE), bf16),
            ((2 * ROWS, 16 * C), f32),
            ((256, 256), f32),
            ((256, 256), bf16),
            (big, f32),
            (big, f32),
            dma((16,)),
        ],
    )
    got = over_x(modes)
    got, ins = lax.optimization_barrier((got, ins))
    got_in = exchange(ins, "gx")
    back, hat_two = call(
        mix_two_kernel,
        [((16, 4, 256), f32), ((4, 256), f32)],
        at,
        got,
        spectral_two,
        fold,
        scratch=[native],
    )
    got = over_x(back)
    (tall,) = call(back_x_kernel, [((32, 256), f32)], at, got, tx)
    got = spread_y(at, tall)
    (tall,) = call(back_y_kernel, [half], at, *got, ty)
    got = spread(tall, "gx")
    ins = call(along_y_kernel, [((64, 512), f32)] * 2, at, *got_in, ty)
    dz_one, *parts = call(
        middle_kernel,
        [(big, bf16, "raw")] + [half] * 3,
        at,
        local_two,
        slope,
        *got,
        mine,
        mine_back,
        raw=2,
        limit=16,
        scratch=[
            ((ROWS, 16 * C), bf16),
            ((ROWS, 12 * C), f32),
            (big, bf16),
            table,
            table_back,
            (big, f32),
            (big, f32),
            dma((24,)),
        ],
    )
    sent, own = call(
        side_one_kernel,
        [((32, 256), f32), half],
        at,
        first,
        dz_one,
        mine,
        weight_two,
        scratch=[((WIDE, 256), bf16)],
    )
    got = exchange([own] + parts, "gx")
    near, far = call(along_y_join_kernel, [((64, 1024), f32)] * 2, at, *got, ty, *ins, sent)
    got = reduce_y(at, near, far, 1024)
    (modes,) = call(along_x_kernel, [((16, 4, 896), f32)], at, *got, tx)
    back, hat_one, mid_hat, first_hat = call(
        mix_one_kernel,
        [((16, 4, 384), f32)] + [((4, 256), f32)] * 3,
        at,
        over_x(modes),
        spectral_one,
        fold,
        scratch=[native],
    )
    (spec_two,) = call(outer_kernel, [(*native, 0)], at, mid_hat, hat_two, fold)
    (spec_one,) = call(outer_kernel, [(*native, 0)], at, first_hat, hat_one, fold)
    back, dz_late = lax.optimization_barrier((back, dz_one))
    (local_one,) = call(
        local_kernel,
        [(big, f32, "raw")],
        at,
        dz_late,
        point_one,
        scratch=[((256, 256), bf16), (big, f32), dma((8,))],
    )
    got = over_x(back)
    got, local_one = lax.optimization_barrier((got, local_one))
    tall, weight = call(back_x_one_kernel, [((32, 256), f32)] * 2, at, got, tx)
    got = spread_y(at, tall)
    (tall,) = call(back_y_one_kernel, [((ROWS + 32, 256), f32)], at, *got, ty, weight)
    got = spread(tall, "gx")
    input_grad, weight_two, weight_one = call(
        end_kernel,
        [(big, bf16, "raw"), ((C, C), f32, 0), ((C, C), f32, 0)],
        at,
        *got,
        mine_back,
        local_one,
        scratch=[((ROWS, 16 * C), bf16), (big, bf16), table_back, dma((8,))],
    )
    return (
        input_grad.reshape(CELLS_X, CELLS_Y, WIDE),
        spec_one[None],
        spec_two[None],
        weight_one,
        weight_two,
    )


def solution(mesh):
    grid = P("gz", "gy", "gx")
    modes = P("gz", "gy", "gx", None)
    return jax.shard_map(
        on_device,
        mesh=mesh,
        in_specs=(grid, grid, grid, grid, modes, modes, P(), P()),
        out_specs=(grid, modes, modes, P(), P()),
        check_vma=False,
    )
```

```python
import jax
import jax.numpy as jnp
import numpy as np
from jax import lax
from jax.experimental import pallas as pl
from jax.experimental.pallas import tpu as pltpu
from jax.sharding import PartitionSpec as P


INTERPRET = False

C = 64
CELLS_X, CELLS_Y, CELLS_Z = 8, 16, 32
DEV_X, DEV_Y, DEV_Z = 16, 4, 4
ROWS = CELLS_X * CELLS_Y
WIDE = CELLS_Z * C
TOTAL_CELLS = CELLS_X * DEV_X * CELLS_Y * DEV_Y * CELLS_Z * DEV_Z
TOTAL_MODES = 16**3
SCALE_A = (TOTAL_CELLS * TOTAL_MODES) ** (-0.25)
SCALE_B = TOTAL_CELLS ** (-0.5)

inv_root_two = 0.7071067811865476
inv_root_tau = 0.3989422804014327
bf16 = jnp.bfloat16
f32 = jnp.float32


def cas(mode, length, position):
    mode = np.asarray(mode)
    freq = np.where(mode < 8, mode, length - 16 + mode)
    phase = (freq * position % length) * (2.0 * np.pi / length)
    return (np.cos(phase) + np.sin(phase)).astype(np.float32)


def build_tables():
    four = np.arange(4)
    z = np.arange(CELLS_Z)
    tz = np.zeros((DEV_Z, CELLS_Z, 16), np.float32)
    for d in range(DEV_Z):
        modes = (((d + four) % 4)[:, None] * 4 + four[None, :]).reshape(-1)
        tz[d] = cas(modes[None, :], CELLS_Z * DEV_Z, z[:, None] * DEV_Z + d)
    tz_back = np.repeat(tz.transpose(0, 2, 1), C, axis=2)
    tz = np.repeat(tz, C, axis=2)
    y = np.arange(CELLS_Y)
    ty = np.zeros((DEV_Y, 4, CELLS_X, 4, CELLS_X, CELLS_Y), np.float32)
    for d in range(DEV_Y):
        modes = (d ^ np.array([0, 2, 1, 3]))[:, None] * 4 + four[None, :]
        small = cas(modes[:, :, None], CELLS_Y * DEV_Y, y * DEV_Y + d)
        for x in range(CELLS_X):
            ty[d, :, x, :, x, :] = small
    ty = ty.reshape(DEV_Y, ROWS, ROWS)
    flat = np.zeros((DEV_Y, CELLS_X, 16, CELLS_X, CELLS_Y), np.float32)
    for d in range(DEV_Y):
        for x in range(CELLS_X):
            flat[d, x, :, x] = cas(np.arange(16)[:, None], CELLS_Y * DEV_Y, y * DEV_Y + d)
    flat = flat.reshape(DEV_Y, ROWS, ROWS)
    x = np.arange(CELLS_X)
    tx = np.zeros((DEV_X, 16, 4, CELLS_X, 4), np.float32)
    few = np.zeros((DEV_X, 16, CELLS_X), np.float32)
    for d in range(DEV_X):
        small = cas(np.arange(16)[:, None], CELLS_X * DEV_X, x * DEV_X + d)
        few[d] = small
        for l in range(4):
            tx[d, :, l, :, l] = small
    tx = tx.reshape(DEV_X, 64, CELLS_X * 4).transpose(0, 2, 1)
    return tuple(t.astype(bf16) for t in (tz, tz_back, ty, flat, tx)) + (
        few.reshape(DEV_X, 128).astype(bf16).astype(np.float32),
    )


def dot(left, right):
    return jnp.dot(left, right, preferred_element_type=f32)


def dot_nt(left, right):
    return lax.dot_general(left, right, (((1,), (1,)), ((), ())), preferred_element_type=f32)


def dot_tn(left, right):
    return lax.dot_general(left, right, (((0,), (0,)), ((), ())), preferred_element_type=f32)


def split(v):
    high = v.astype(bf16)
    return high, (v - high.astype(f32)).astype(bf16)


def table_dot(table, v):
    high, low = split(v)
    return dot(table, high) + dot(table, low)


def table_dot_tn(table, v):
    high, low = split(v)
    return dot_tn(table, high) + dot_tn(table, low)


def slope_of(v, cdf):
    return cdf + v * jnp.exp(-0.5 * v * v) * inv_root_tau


def cdf_of(v):
    return 0.5 * (1.0 + lax.erf(v * inv_root_two))


def call(body, outs, *args, scratch=(), limit=8, raw=0):
    near = args[1 : 1 + raw]
    rest = args[1 + raw :]
    shapes = [pltpu.VMEM(*o) if len(o) == 2 else jax.ShapeDtypeStruct(*o[:2]) for o in outs]
    shapes = [pltpu.HBM(*o[:2]) if "raw" in o else v for o, v in zip(outs, shapes)]
    if INTERPRET:
        shapes = [jax.ShapeDtypeStruct(*o[:2]) for o in outs]
    else:
        near = [pltpu.with_memory_space_constraint(a, pltpu.HBM) for a in near]
        rest = [pltpu.with_memory_space_constraint(a, pltpu.VMEM) for a in rest]
    return pl.pallas_call(
        body,
        out_shape=shapes,
        in_specs=[pl.BlockSpec(memory_space=pltpu.SMEM)]
        + [pl.BlockSpec(memory_space=pl.ANY if INTERPRET else pltpu.HBM)] * raw
        + [pl.BlockSpec(memory_space=pltpu.VMEM)] * len(rest),
        out_specs=[
            pl.BlockSpec(memory_space=(pl.ANY if INTERPRET else pltpu.HBM) if "raw" in o else pltpu.VMEM)
            for o in outs
        ],
        scratch_shapes=[pltpu.VMEM(*s) if isinstance(s, tuple) else s for s in scratch],
        interpret=INTERPRET,
        compiler_params=pltpu.CompilerParams(vmem_limit_bytes=limit << 20),
    )(*args[:1], *near, *rest)


def at_x(at):
    return at[0] >> 4


def at_y(at):
    return (at[0] >> 2) & 3


def at_z(at):
    return at[0] & 3


def block(b):
    return slice(b * 256, (b + 1) * 256)


def store_parts(v, refs):
    for j, ref in enumerate(refs):
        ref[...] = v[:, j * 256 : (j + 1) * 256]


def fill_table(ka, mine, b, wide=16 * C):
    lane = lax.broadcasted_iota(jnp.int32, (C, wide), 1) & (C - 1)
    row = lax.broadcasted_iota(jnp.int32, (C, wide), 0)
    eye = jnp.where(lane == row, 1.0, 0.0)
    for z in range(4 * b, 4 * b + 4):
        ka[z * C : (z + 1) * C, :] = (eye * mine[z : z + 1, :wide]).astype(bf16)


def fill_back(ka, mine, b):
    lane = lax.broadcasted_iota(jnp.int32, (C, 256), 1) & (C - 1)
    row = lax.broadcasted_iota(jnp.int32, (C, 256), 0)
    eye = jnp.where(lane == row, 1.0, 0.0)
    for k in range(16):
        ka[k * C : (k + 1) * C, block(b)] = (eye * mine[k : k + 1, block(b)]).astype(bf16)


def start_kernel(
    at, pre_from, grad_from, tz, tz_back, dz_to, p1, p2, p3, mine, mine_back,
    ka, total, pre, grad, dz, short, short_back, sems,
):
    def copies(b):
        cut = block(b)
        return (
            pltpu.make_async_copy(pre_from.at[:, cut], pre.at[:, cut], sems.at[b]),
            pltpu.make_async_copy(grad_from.at[:, cut], grad.at[:, cut], sems.at[8 + b]),
        )

    def leave(b):
        return pltpu.make_async_copy(dz.at[:, block(b)], dz_to.at[:, block(b)], sems.at[17 + b])

    first = pltpu.make_async_copy(tz.at[at_z(at)], short, sems.at[16])
    first.start()
    for b in range(8):
        for copy in copies(b):
            copy.start()
    second = pltpu.make_async_copy(tz_back.at[at_z(at)], short_back, sems.at[25])
    second.start()
    first.wait()
    mine[...] = short[...].astype(f32)
    total[...] = jnp.zeros_like(total)
    for b in range(9):
        if b < 8:
            fill_table(ka, mine, b)
            for copy in copies(b):
                copy.wait()
            v = pre[:, block(b)].astype(f32)
            slope = slope_of(v, cdf_of(v))
            dz[:, block(b)] = (grad[:, block(b)].astype(f32) * slope).astype(bf16)
            leave(b).start()
        if b > 0:
            total[...] += dot(dz[:, block(b - 1)], ka[block(b - 1), 256:])
    store_parts(total[...], (p1, p2, p3))
    second.wait()
    mine_back[...] = short_back[...].astype(f32)
    for b in range(8):
        leave(b).wait()


def own_kernel(at, mine, dz, few, p0, fold, coef, ka):
    side = lax.broadcasted_iota(jnp.int32, (128, 128), 0)
    same = jnp.where(side == lax.broadcasted_iota(jnp.int32, (128, 128), 1), 1.0, 0.0)
    same = (same * few[pl.ds(at_x(at), 1), :]).astype(bf16)
    coef[...] = dot(same, jnp.ones((128, 128), bf16))
    for b in range(8):
        fill_table(ka, mine, b, 256)
    p0[...] = dot(dz[...], ka[...])
    row = lax.broadcasted_iota(jnp.int32, (256, C), 0) >> 6
    lane = lax.broadcasted_iota(jnp.int32, (256, C), 1)
    for r in range(16):
        fold[r * 256 : (r + 1) * 256, :] = jnp.where(lane == row + 4 * r, 1.0, 0.0).astype(bf16)


def fill_point(square, point):
    square[...] = jnp.zeros_like(square)
    for i in range(4):
        square[i * C : (i + 1) * C, i * C : (i + 1) * C] = point[...]


def diagonal_sum(total):
    return sum(total[i * C : (i + 1) * C, i * C : (i + 1) * C] for i in range(4))


def side_kernel(
    at, pre, first, dz, mine, point, slope_to, local_to, weight, q0, q1, q2, q3,
    ka, mid, own, squares, square, slope, local, sems,
):
    fill_point(square, point)

    def leave(b):
        cut = block(b)
        return (
            pltpu.make_async_copy(slope.at[:, cut], slope_to.at[:, cut], sems.at[b]),
            pltpu.make_async_copy(local.at[:, cut], local_to.at[:, cut], sems.at[8 + b]),
        )

    own[...] = jnp.zeros_like(own)
    squares[...] = jnp.zeros_like(squares)
    for b in range(9):
        if b < 8:
            cut = block(b)
            fill_table(ka, mine, b)
            v = pre[:, cut].astype(f32)
            cdf = cdf_of(v)
            slope[:, cut] = slope_of(v, cdf)
            mid[:ROWS, cut] = (v * cdf).astype(bf16)
            mid[ROWS:, cut] = first[:, cut]
            local[:, cut] = dot_nt(dz[:, cut], square[...])
            for copy in leave(b):
                copy.start()
        if b > 0:
            cut = block(b - 1)
            squares[...] += dot_tn(mid[:ROWS, cut], dz[:, cut])
            own[...] += dot(mid[:, cut], ka[cut, :])
    weight[...] = diagonal_sum(squares[...])
    for j, ref in enumerate((q0, q1, q2, q3)):
        ref[:, :256] = own[:ROWS, j * 256 : (j + 1) * 256]
        ref[:, 256:] = own[ROWS:, j * 256 : (j + 1) * 256]
    for b in range(8):
        for copy in leave(b):
            copy.wait()


def side_one_kernel(at, first, dz, mine, weight_two, sent, p0, ka):
    for b in range(8):
        fill_table(ka, mine, b, 256)
    squares = dot_tn(first[:, :256], dz[:, :256])
    for b in range(1, 8):
        squares = squares + dot_tn(first[:, block(b)], dz[:, block(b)])
    p0[...] = dot(dz[...], ka[...])
    both = jnp.concatenate([weight_two[...], diagonal_sum(squares)], axis=1) * SCALE_B
    sent[...] = jnp.concatenate([both[:32], both[32:]], axis=1)


def local_kernel(at, dz, point, local_to, square, local, sems):
    fill_point(square, point)

    def leave(b):
        return pltpu.make_async_copy(local.at[:, block(b)], local_to.at[:, block(b)], sems.at[b])

    for b in range(8):
        local[:, block(b)] = dot_nt(dz[:, block(b)], square[...])
        leave(b).start()
    for b in range(8):
        leave(b).wait()


def total_of(refs):
    return (refs[0][...] + refs[1][...]) + (refs[2][...] + refs[3][...])


def factor(coef, k, x):
    c = coef[k * 8 + x : k * 8 + x + 1, :]
    return jnp.concatenate([c, c], axis=1)


def along_yx_kernel(at, a, b, c, d, flat, coef, out):
    v = table_dot(flat[at_y(at)], total_of((a, b, c, d)))
    for k in range(16):
        here = factor(coef, k, 0) * v[:16]
        for x in range(1, 8):
            here = here + factor(coef, k, x) * v[x * 16 : (x + 1) * 16]
        for g in range(4):
            out[k * 4 + g] = here[g * 4 : (g + 1) * 4]


def back_xy(at, got, flat, coef, tall):
    for k in range(16):
        here = jnp.concatenate([got[k * 4 + g, :, :256] for g in range(4)], axis=0)
        for x in range(8):
            rows = slice(x * 16, (x + 1) * 16)
            more = factor(coef, k, x) * here
            tall[rows] = more if k == 0 else tall[rows] + more
    return table_dot_tn(flat[at_y(at)], tall[...])


def back_xy_kernel(at, got, flat, coef, out, tall):
    out[...] = back_xy(at, got, flat, coef, tall)


def back_xy_one_kernel(at, got, flat, coef, out, tall):
    out[:ROWS] = back_xy(at, got, flat, coef, tall)
    weight = jnp.concatenate([got[k * 4, :, 256:] for k in range(16)], axis=0)
    out[ROWS:] = jnp.concatenate([weight[:32], weight[32:]], axis=1)


def along_y_kernel(at, a, b, c, d, ty, near, far):
    out = table_dot(ty[at_y(at)], total_of((a, b, c, d)))
    near[...] = out[:64]
    far[...] = out[64:]


def along_y_join_kernel(at, a, b, c, d, ty, ins_near, ins_far, sent, near, far):
    out = table_dot(ty[at_y(at)], total_of((a, b, c, d)))
    for ref, ins, here in ((near, ins_near, out[:64]), (far, ins_far, out[64:])):
        ref[:, :256] = here
        ref[:, 256:768] = ins[...]
        ref[:32, 768:] = sent[...]
        ref[32:, 768:] = jnp.zeros((32, 256), f32)


def keep_kernel(at, near, got, keep, send):
    v = near[...] + got[...]
    keep[...] = v[:32]
    wide = min(v.shape[1], 768)
    send[:, :wide] = v[32:, :wide]
    if v.shape[1] > 768:
        send[:, 768:] = v[:32, 768:]


def along_x_kernel(at, a, b, tx, out):
    v = a[...] + b[...]
    modes = table_dot_tn(tx[at_x(at)], v[:, : min(v.shape[1], 768)])
    for i in range(16):
        out[i, :, : modes.shape[1]] = modes[i * 4 : (i + 1) * 4]
    if v.shape[1] > 768:
        weight = jnp.concatenate([v[:, 768:896], v[:, 896:]], axis=0)
        for i in range(16):
            out[i, :, 768:] = weight[i * 4 : (i + 1) * 4]


def mixed(hat, spectral, wide, fold):
    wide[...] = spectral[0].astype(f32)
    products = []
    for k in range(4):
        h = hat[:, k * C : (k + 1) * C]
        h = jnp.concatenate([h, h], axis=1)
        products.append(wide[:, k, :] * jnp.concatenate([h] * 32, axis=1))
    high, low = split(jnp.concatenate(products, axis=0))
    out = dot(jnp.concatenate([high, low], axis=0), fold[...])
    out = (out[:16] + out[16:]) * SCALE_A
    return jnp.concatenate([out[k * 4 : (k + 1) * 4] for k in range(4)], axis=1)


def sum_of(got):
    v = [got[i] for i in range(got.shape[0])]
    while len(v) > 1:
        v = [v[i] + v[i + 1] for i in range(0, len(v), 2)]
    return v[0]


def mix_two_kernel(at, got, spectral, fold, back, hat_out, wide):
    hat = sum_of(got) * SCALE_B
    hat_out[...] = hat
    out = mixed(hat, spectral, wide, fold)
    for i in range(64):
        back[i] = out


def mix_one_kernel(at, got, spectral, fold, back, hat_out, mid_out, first_out, wide):
    v = sum_of(got)
    hat = v[:, :256] * SCALE_B
    hat_out[...] = hat
    mid_out[...] = v[:, 256:512] * SCALE_A
    first_out[...] = v[:, 512:768] * SCALE_A
    out = mixed(hat, spectral, wide, fold)
    for i in range(64):
        back[i, :, :256] = out
        back[i, :, 256:] = v[:, 768:]


def outer_kernel(at, left, right, fold, out):
    lefts = []
    rights = []
    for k in range(4):
        cut = slice(k * C, (k + 1) * C)
        h = right[:, cut]
        lefts.append(left[:, cut])
        rights.append(jnp.concatenate([h, h], axis=1))
    v = jnp.concatenate(lefts, axis=0)
    high, rest = v.astype(bf16), v - v.astype(bf16).astype(f32)
    low, last = split(rest)
    spread_left = dot_nt(jnp.concatenate([high, low, last], axis=0), fold[...])
    tall = jnp.concatenate(rights, axis=0)
    whole = (spread_left[:16] + spread_left[16:32]) + spread_left[32:]
    whole = whole * jnp.concatenate([tall] * 32, axis=1)
    for k in range(4):
        out[:, k, :] = whole[k * 4 : (k + 1) * 4]


def stack_modes(refs, modes):
    for j, ref in enumerate(refs):
        modes[:, j * 256 : (j + 1) * 256] = ref[:ROWS].astype(bf16)


def middle_kernel(
    at, local_from, slope_from, a, b, c, d, mine, mine_back, dz_to, p1, p2, p3,
    modes, total, dz, ka, ka_back, local, slope, sems,
):
    def copies(i):
        cut = block(i)
        return (
            pltpu.make_async_copy(local_from.at[:, cut], local.at[:, cut], sems.at[i]),
            pltpu.make_async_copy(slope_from.at[:, cut], slope.at[:, cut], sems.at[8 + i]),
        )

    def leave(i):
        return pltpu.make_async_copy(dz.at[:, block(i)], dz_to.at[:, block(i)], sems.at[16 + i])

    for i in range(8):
        for copy in copies(i):
            copy.start()
    stack_modes((a, b, c, d), modes)
    total[...] = jnp.zeros_like(total)
    fill_back(ka_back, mine_back, 0)
    for i in range(9):
        if i < 8:
            if i < 7:
                fill_back(ka_back, mine_back, i + 1)
            fill_table(ka, mine, i)
            for copy in copies(i):
                copy.wait()
            down = dot(modes[...], ka_back[:, block(i)]) + local[:, block(i)]
            dz[:, block(i)] = (down * slope[:, block(i)]).astype(bf16)
            leave(i).start()
        if i > 0:
            total[...] += dot(dz[:, block(i - 1)], ka[block(i - 1), 256:])
    store_parts(total[...], (p1, p2, p3))
    for i in range(8):
        leave(i).wait()


def end_kernel(
    at, a, b, c, d, mine, local, out_to, weight_two, weight_one, modes, out, ka, sems
):
    def leave(i):
        return pltpu.make_async_copy(out.at[:, block(i)], out_to.at[:, block(i)], sems.at[i])

    stack_modes((a, b, c, d), modes)
    fill_back(ka, mine, 0)
    for i in range(8):
        if i < 7:
            fill_back(ka, mine, i + 1)
        down = dot(modes[...], ka[:, block(i)]) + local[:, block(i)]
        out[:, block(i)] = down.astype(bf16)
        leave(i).start()
    w = (a[ROWS:] + b[ROWS:]) + (c[ROWS:] + d[ROWS:])
    w = jnp.concatenate([w[:, :128], w[:, 128:]], axis=0)
    weight_two[...] = w[:, :C]
    weight_one[...] = w[:, C:]
    for i in range(8):
        leave(i).wait()


def shift_pairs(kind, s):
    return kind, [(i, i ^ s if kind == "gy" else (i + s) % 4) for i in range(4)]


def shifted(v, kind, s):
    axis, pairs = shift_pairs(kind, s)
    return lax.ppermute(v, axis, pairs)


def exchange(parts, kind):
    return [parts[0]] + [shifted(parts[s], kind, s) for s in (1, 2, 3)]


def spread(v, kind):
    return [v] + [shifted(v, kind, s) for s in (3, 2, 1)]


def reduce_y(at, near, far, width):
    keep, send = call(
        keep_kernel, [((32, width), f32)] * 2, at, near, shifted(far, "gy", 1)
    )
    return keep, shifted(send, "gy", 2)


def over(v, axes):
    return lax.all_to_all(v, axes, 0, 0, tiled=True)


def on_device(
    grid_input, pre_one, pre_two, grad_output, spectral_one, spectral_two, point_one, point_two
):
    tz, tz_back, ty, flat, tx, few = [jnp.asarray(t) for t in build_tables()]
    at = lax.axis_index(("gz", "gy", "gx")).reshape(1)
    first, pre_one, pre_two, upstream = [
        t.reshape(ROWS, WIDE) for t in (grid_input, pre_one, pre_two, grad_output)
    ]
    big = (ROWS, WIDE)
    half = ((ROWS, 256), f32)
    table = ((WIDE, 16 * C), bf16)
    table_back = ((16 * C, WIDE), bf16)
    native = ((4, 4, C * C), f32)
    dma = pltpu.SemaphoreType.DMA

    dz_two, *parts, mine, mine_back = call(
        start_kernel,
        [(big, bf16, "raw")] + [half] * 3 + [((CELLS_Z, 16 * C), f32), ((16, WIDE), f32)],
        at,
        pre_two,
        upstream,
        tz,
        tz_back,
        raw=4,
        scratch=[
            table,
            ((ROWS, 12 * C), f32),
            (big, bf16),
            (big, bf16),
            (big, bf16),
            ((CELLS_Z, 16 * C), bf16),
            ((16, WIDE), bf16),
            dma((26,)),
        ],
    )
    own, fold, coef = call(
        own_kernel,
        [half, ((C * C, C), bf16), ((128, 128), f32)],
        at,
        mine,
        dz_two,
        few,
        scratch=[((WIDE, 256), bf16)],
    )
    got = exchange([own] + parts, "gx")
    (modes,) = call(along_yx_kernel, [((64, 4, 256), f32)], at, *got, flat, coef)
    modes, pre_one, dz_side = lax.optimization_barrier((modes, pre_one, dz_two))
    slope, local_two, weight_two, *ins = call(
        side_kernel,
        [(big, f32, "raw")] * 2 + [((C, C), f32, 0)] + [((ROWS, 512), f32)] * 4,
        at,
        pre_one,
        first,
        dz_side,
        mine,
        point_two,
        limit=14,
        scratch=[
            table,
            ((2 * ROWS, WIDE), bf16),
            ((2 * ROWS, 16 * C), f32),
            ((256, 256), f32),
            ((256, 256), bf16),
            (big, f32),
            (big, f32),
            dma((16,)),
        ],
    )
    got = over(modes, ("gz", "gy"))
    got, ins = lax.optimization_barrier((got, ins))
    got_in = exchange(ins, "gx")
    back, hat_two = call(
        mix_two_kernel,
        [((64, 4, 256), f32), ((4, 256), f32)],
        at,
        got,
        spectral_two,
        fold,
        scratch=[native],
    )
    got = over(back, ("gz", "gy"))
    (tall,) = call(back_xy_kernel, [half], at, got, flat, coef, scratch=[half])
    got = spread(tall, "gx")
    ins = call(along_y_kernel, [((64, 512), f32)] * 2, at, *got_in, ty)
    dz_one, *parts = call(
        middle_kernel,
        [(big, bf16, "raw")] + [half] * 3,
        at,
        local_two,
        slope,
        *got,
        mine,
        mine_back,
        raw=2,
        limit=16,
        scratch=[
            ((ROWS, 16 * C), bf16),
            ((ROWS, 12 * C), f32),
            (big, bf16),
            table,
            table_back,
            (big, f32),
            (big, f32),
            dma((24,)),
        ],
    )
    sent, own = call(
        side_one_kernel,
        [((32, 256), f32), half],
        at,
        first,
        dz_one,
        mine,
        weight_two,
        scratch=[((WIDE, 256), bf16)],
    )
    got = exchange([own] + parts, "gx")
    near, far = call(along_y_join_kernel, [((64, 1024), f32)] * 2, at, *got, ty, *ins, sent)
    got = reduce_y(at, near, far, 1024)
    (modes,) = call(along_x_kernel, [((16, 4, 896), f32)], at, *got, tx)
    back, hat_one, mid_hat, first_hat = call(
        mix_one_kernel,
        [((64, 4, 384), f32)] + [((4, 256), f32)] * 3,
        at,
        over(modes, "gz"),
        spectral_one,
        fold,
        scratch=[native],
    )
    (spec_two,) = call(outer_kernel, [(*native, 0)], at, mid_hat, hat_two, fold)
    (spec_one,) = call(outer_kernel, [(*native, 0)], at, first_hat, hat_one, fold)
    back, dz_late = lax.optimization_barrier((back, dz_one))
    (local_one,) = call(
        local_kernel,
        [(big, f32, "raw")],
        at,
        dz_late,
        point_one,
        scratch=[((256, 256), bf16), (big, f32), dma((8,))],
    )
    got = over(back, ("gz", "gy"))
    got, local_one = lax.optimization_barrier((got, local_one))
    (tall,) = call(
        back_xy_one_kernel, [((ROWS + 32, 256), f32)], at, got, flat, coef, scratch=[half]
    )
    got = spread(tall, "gx")
    input_grad, weight_two, weight_one = call(
        end_kernel,
        [(big, bf16, "raw"), ((C, C), f32, 0), ((C, C), f32, 0)],
        at,
        *got,
        mine_back,
        local_one,
        scratch=[((ROWS, 16 * C), bf16), (big, bf16), table_back, dma((8,))],
    )
    return (
        input_grad.reshape(CELLS_X, CELLS_Y, WIDE),
        spec_one[None],
        spec_two[None],
        weight_one,
        weight_two,
    )


def solution(mesh):
    grid = P("gz", "gy", "gx")
    modes = P("gz", "gy", "gx", None)
    return jax.shard_map(
        on_device,
        mesh=mesh,
        in_specs=(grid, grid, grid, grid, modes, modes, P(), P()),
        out_specs=(grid, modes, modes, P(), P()),
        check_vma=False,
    )
```

```python
import jax
import jax.numpy as jnp
import numpy as np
from jax import lax
from jax.experimental import pallas as pl
from jax.experimental.pallas import tpu as pltpu
from jax.sharding import PartitionSpec as P


INTERPRET = False

C = 64
CELLS_X, CELLS_Y, CELLS_Z = 8, 16, 32
DEV_X, DEV_Y, DEV_Z = 16, 4, 4
ROWS = CELLS_X * CELLS_Y
WIDE = CELLS_Z * C
TOTAL_CELLS = CELLS_X * DEV_X * CELLS_Y * DEV_Y * CELLS_Z * DEV_Z
TOTAL_MODES = 16**3
SCALE_A = (TOTAL_CELLS * TOTAL_MODES) ** (-0.25)
SCALE_B = TOTAL_CELLS ** (-0.5)

inv_root_two = 0.7071067811865476
inv_root_tau = 0.3989422804014327
bf16 = jnp.bfloat16
f32 = jnp.float32


def cas(mode, length, position):
    mode = np.asarray(mode)
    freq = np.where(mode < 8, mode, length - 16 + mode)
    phase = (freq * position % length) * (2.0 * np.pi / length)
    return (np.cos(phase) + np.sin(phase)).astype(np.float32)


def build_tables():
    four = np.arange(4)
    z = np.arange(CELLS_Z)
    tz = np.zeros((DEV_Z, CELLS_Z, 16), np.float32)
    for d in range(DEV_Z):
        modes = (((d + four) % 4)[:, None] * 4 + four[None, :]).reshape(-1)
        tz[d] = cas(modes[None, :], CELLS_Z * DEV_Z, z[:, None] * DEV_Z + d)
    tz_back = np.repeat(tz.transpose(0, 2, 1), C, axis=2)
    tz = np.repeat(tz, C, axis=2)
    y = np.arange(CELLS_Y)
    ty = np.zeros((DEV_Y, 4, CELLS_X, 4, CELLS_X, CELLS_Y), np.float32)
    for d in range(DEV_Y):
        modes = (d ^ np.array([0, 2, 1, 3]))[:, None] * 4 + four[None, :]
        small = cas(modes[:, :, None], CELLS_Y * DEV_Y, y * DEV_Y + d)
        for x in range(CELLS_X):
            ty[d, :, x, :, x, :] = small
    ty = ty.reshape(DEV_Y, ROWS, ROWS)
    flat = np.zeros((DEV_Y, CELLS_X, 16, CELLS_X, CELLS_Y), np.float32)
    for d in range(DEV_Y):
        for x in range(CELLS_X):
            flat[d, x, :, x] = cas(np.arange(16)[:, None], CELLS_Y * DEV_Y, y * DEV_Y + d)
    flat = flat.reshape(DEV_Y, ROWS, ROWS)
    x = np.arange(CELLS_X)
    tx = np.zeros((DEV_X, 16, 4, CELLS_X, 4), np.float32)
    few = np.zeros((DEV_X, 16, CELLS_X), np.float32)
    for d in range(DEV_X):
        small = cas(np.arange(16)[:, None], CELLS_X * DEV_X, x * DEV_X + d)
        few[d] = small
        for l in range(4):
            tx[d, :, l, :, l] = small
    tx = tx.reshape(DEV_X, 64, CELLS_X * 4).transpose(0, 2, 1)
    return tuple(t.astype(bf16) for t in (tz, tz_back, ty, flat, tx)) + (
        few.reshape(DEV_X, 128).astype(bf16).astype(np.float32),
    )


def dot(left, right):
    return jnp.dot(left, right, preferred_element_type=f32)


def dot_nt(left, right):
    return lax.dot_general(left, right, (((1,), (1,)), ((), ())), preferred_element_type=f32)


def dot_tn(left, right):
    return lax.dot_general(left, right, (((0,), (0,)), ((), ())), preferred_element_type=f32)


def split(v):
    high = v.astype(bf16)
    return high, (v - high.astype(f32)).astype(bf16)


def table_dot(table, v):
    high, low = split(v)
    return dot(table, high) + dot(table, low)


def table_dot_tn(table, v):
    high, low = split(v)
    return dot_tn(table, high) + dot_tn(table, low)


def slope_of(v, cdf):
    return cdf + v * jnp.exp(-0.5 * v * v) * inv_root_tau


def cdf_of(v):
    return 0.5 * (1.0 + lax.erf(v * inv_root_two))


def call(body, outs, *args, scratch=(), limit=8, raw=0):
    near = args[1 : 1 + raw]
    rest = args[1 + raw :]
    shapes = [pltpu.VMEM(*o) if len(o) == 2 else jax.ShapeDtypeStruct(*o[:2]) for o in outs]
    shapes = [pltpu.HBM(*o[:2]) if "raw" in o else v for o, v in zip(outs, shapes)]
    if INTERPRET:
        shapes = [jax.ShapeDtypeStruct(*o[:2]) for o in outs]
    else:
        near = [pltpu.with_memory_space_constraint(a, pltpu.HBM) for a in near]
        rest = [pltpu.with_memory_space_constraint(a, pltpu.VMEM) for a in rest]
    return pl.pallas_call(
        body,
        out_shape=shapes,
        in_specs=[pl.BlockSpec(memory_space=pltpu.SMEM)]
        + [pl.BlockSpec(memory_space=pl.ANY if INTERPRET else pltpu.HBM)] * raw
        + [pl.BlockSpec(memory_space=pltpu.VMEM)] * len(rest),
        out_specs=[
            pl.BlockSpec(memory_space=(pl.ANY if INTERPRET else pltpu.HBM) if "raw" in o else pltpu.VMEM)
            for o in outs
        ],
        scratch_shapes=[pltpu.VMEM(*s) if isinstance(s, tuple) else s for s in scratch],
        interpret=INTERPRET,
        compiler_params=pltpu.CompilerParams(vmem_limit_bytes=limit << 20),
    )(*args[:1], *near, *rest)


def at_x(at):
    return at[0] >> 4


def at_y(at):
    return (at[0] >> 2) & 3


def at_z(at):
    return at[0] & 3


def block(b):
    return slice(b * 256, (b + 1) * 256)


def store_parts(v, refs):
    for j, ref in enumerate(refs):
        ref[...] = v[:, j * 256 : (j + 1) * 256]


def fill_table(ka, mine, b, wide=16 * C):
    lane = lax.broadcasted_iota(jnp.int32, (C, wide), 1) & (C - 1)
    row = lax.broadcasted_iota(jnp.int32, (C, wide), 0)
    eye = jnp.where(lane == row, 1.0, 0.0)
    for z in range(4 * b, 4 * b + 4):
        ka[z * C : (z + 1) * C, :] = (eye * mine[z : z + 1, :wide]).astype(bf16)


def fill_back(ka, mine, b):
    lane = lax.broadcasted_iota(jnp.int32, (C, 256), 1) & (C - 1)
    row = lax.broadcasted_iota(jnp.int32, (C, 256), 0)
    eye = jnp.where(lane == row, 1.0, 0.0)
    for k in range(16):
        ka[k * C : (k + 1) * C, block(b)] = (eye * mine[k : k + 1, block(b)]).astype(bf16)


def start_kernel(
    at, pre_from, grad_from, tz, tz_back, dz_to, p1, p2, p3, mine, mine_back,
    ka, total, pre, grad, dz, short, short_back, sems,
):
    def copies(b):
        cut = block(b)
        return (
            pltpu.make_async_copy(pre_from.at[:, cut], pre.at[:, cut], sems.at[b]),
            pltpu.make_async_copy(grad_from.at[:, cut], grad.at[:, cut], sems.at[8 + b]),
        )

    def leave(b):
        return pltpu.make_async_copy(dz.at[:, block(b)], dz_to.at[:, block(b)], sems.at[17 + b])

    first = pltpu.make_async_copy(tz.at[at_z(at)], short, sems.at[16])
    first.start()
    for b in range(8):
        for copy in copies(b):
            copy.start()
    second = pltpu.make_async_copy(tz_back.at[at_z(at)], short_back, sems.at[25])
    second.start()
    first.wait()
    mine[...] = short[...].astype(f32)
    total[...] = jnp.zeros_like(total)
    for b in range(9):
        if b < 8:
            fill_table(ka, mine, b)
            for copy in copies(b):
                copy.wait()
            v = pre[:, block(b)].astype(f32)
            slope = slope_of(v, cdf_of(v))
            dz[:, block(b)] = (grad[:, block(b)].astype(f32) * slope).astype(bf16)
            leave(b).start()
        if b > 0:
            total[...] += dot(dz[:, block(b - 1)], ka[block(b - 1), 256:])
    store_parts(total[...], (p1, p2, p3))
    second.wait()
    mine_back[...] = short_back[...].astype(f32)
    for b in range(8):
        leave(b).wait()


def own_kernel(at, mine, dz, few, p0, fold, coef, ka):
    side = lax.broadcasted_iota(jnp.int32, (128, 128), 0)
    same = jnp.where(side == lax.broadcasted_iota(jnp.int32, (128, 128), 1), 1.0, 0.0)
    same = (same * few[pl.ds(at_x(at), 1), :]).astype(bf16)
    coef[...] = dot(same, jnp.ones((128, 128), bf16))
    for b in range(8):
        fill_table(ka, mine, b, 256)
    p0[...] = dot(dz[...], ka[...])
    row = lax.broadcasted_iota(jnp.int32, (256, C), 0) >> 6
    lane = lax.broadcasted_iota(jnp.int32, (256, C), 1)
    for r in range(16):
        fold[r * 256 : (r + 1) * 256, :] = jnp.where(lane == row + 4 * r, 1.0, 0.0).astype(bf16)


def fill_point(square, point):
    square[...] = jnp.zeros_like(square)
    for i in range(4):
        square[i * C : (i + 1) * C, i * C : (i + 1) * C] = point[...]


def diagonal_sum(total):
    return sum(total[i * C : (i + 1) * C, i * C : (i + 1) * C] for i in range(4))


def side_kernel(
    at, pre, first, dz, mine, point, slope_to, local_to, weight, q0, q1, q2, q3,
    ka, mid, own, squares, square, slope, local, sems,
):
    fill_point(square, point)

    def leave(b):
        cut = block(b)
        return (
            pltpu.make_async_copy(slope.at[:, cut], slope_to.at[:, cut], sems.at[b]),
            pltpu.make_async_copy(local.at[:, cut], local_to.at[:, cut], sems.at[8 + b]),
        )

    own[...] = jnp.zeros_like(own)
    squares[...] = jnp.zeros_like(squares)
    for b in range(9):
        if b < 8:
            cut = block(b)
            fill_table(ka, mine, b)
            v = pre[:, cut].astype(f32)
            cdf = cdf_of(v)
            slope[:, cut] = slope_of(v, cdf)
            mid[:ROWS, cut] = (v * cdf).astype(bf16)
            mid[ROWS:, cut] = first[:, cut]
            local[:, cut] = dot_nt(dz[:, cut], square[...])
            for copy in leave(b):
                copy.start()
        if b > 0:
            cut = block(b - 1)
            squares[...] += dot_tn(mid[:ROWS, cut], dz[:, cut])
            own[...] += dot(mid[:, cut], ka[cut, :])
    weight[...] = diagonal_sum(squares[...])
    for j, ref in enumerate((q0, q1, q2, q3)):
        ref[:, :256] = own[:ROWS, j * 256 : (j + 1) * 256]
        ref[:, 256:] = own[ROWS:, j * 256 : (j + 1) * 256]
    for b in range(8):
        for copy in leave(b):
            copy.wait()


def side_one_kernel(at, first, dz, mine, weight_two, sent, p0, ka):
    for b in range(8):
        fill_table(ka, mine, b, 256)
    squares = dot_tn(first[:, :256], dz[:, :256])
    for b in range(1, 8):
        squares = squares + dot_tn(first[:, block(b)], dz[:, block(b)])
    p0[...] = dot(dz[...], ka[...])
    both = jnp.concatenate([weight_two[...], diagonal_sum(squares)], axis=1) * SCALE_B
    sent[...] = jnp.concatenate([both[:32], both[32:]], axis=1)


def local_kernel(at, dz, point, local_to, square, local, sems):
    fill_point(square, point)

    def leave(b):
        return pltpu.make_async_copy(local.at[:, block(b)], local_to.at[:, block(b)], sems.at[b])

    for b in range(8):
        local[:, block(b)] = dot_nt(dz[:, block(b)], square[...])
        leave(b).start()
    for b in range(8):
        leave(b).wait()


def total_of(refs):
    return (refs[0][...] + refs[1][...]) + (refs[2][...] + refs[3][...])


def factor(coef, k, x):
    c = coef[k * 8 + x : k * 8 + x + 1, :]
    return jnp.concatenate([c, c], axis=1)


def along_yx_kernel(at, a, b, c, d, flat, coef, out):
    v = table_dot(flat[at_y(at)], total_of((a, b, c, d)))
    for k in range(16):
        here = factor(coef, k, 0) * v[:16]
        for x in range(1, 8):
            here = here + factor(coef, k, x) * v[x * 16 : (x + 1) * 16]
        for g in range(4):
            out[k * 4 + g] = here[g * 4 : (g + 1) * 4]


def back_xy(at, got, flat, coef, tall):
    for k in range(16):
        here = jnp.concatenate([got[k * 4 + g, :, :256] for g in range(4)], axis=0)
        for x in range(8):
            rows = slice(x * 16, (x + 1) * 16)
            more = factor(coef, k, x) * here
            tall[rows] = more if k == 0 else tall[rows] + more
    return table_dot_tn(flat[at_y(at)], tall[...])


def back_xy_kernel(at, got, flat, coef, out, tall):
    out[...] = back_xy(at, got, flat, coef, tall)


def back_xy_one_kernel(at, got, flat, coef, out, tall):
    out[:ROWS] = back_xy(at, got, flat, coef, tall)
    weight = jnp.concatenate([got[k * 4, :, 256:] for k in range(16)], axis=0)
    out[ROWS:] = jnp.concatenate([weight[:32], weight[32:]], axis=1)


def along_y_kernel(at, a, b, c, d, ty, near, far):
    out = table_dot(ty[at_y(at)], total_of((a, b, c, d)))
    near[...] = out[:64]
    far[...] = out[64:]


def along_y_join_kernel(at, a, b, c, d, ty, ins_near, ins_far, sent, near, far):
    out = table_dot(ty[at_y(at)], total_of((a, b, c, d)))
    for ref, ins, here in ((near, ins_near, out[:64]), (far, ins_far, out[64:])):
        ref[:, :256] = here
        ref[:, 256:768] = ins[...]
        ref[:32, 768:] = sent[...]
        ref[32:, 768:] = jnp.zeros((32, 256), f32)


def keep_kernel(at, near, got, keep, send):
    v = near[...] + got[...]
    keep[...] = v[:32]
    wide = min(v.shape[1], 768)
    send[:, :wide] = v[32:, :wide]
    if v.shape[1] > 768:
        send[:, 768:] = v[:32, 768:]


def along_x_kernel(at, a, b, tx, out):
    v = a[...] + b[...]
    modes = table_dot_tn(tx[at_x(at)], v[:, : min(v.shape[1], 768)])
    for i in range(16):
        out[i, :, : modes.shape[1]] = modes[i * 4 : (i + 1) * 4]
    if v.shape[1] > 768:
        weight = jnp.concatenate([v[:, 768:896], v[:, 896:]], axis=0)
        for i in range(16):
            out[i, :, 768:] = weight[i * 4 : (i + 1) * 4]


def mixed(hat, spectral, wide, fold):
    wide[...] = spectral[0].astype(f32)
    products = []
    for k in range(4):
        h = hat[:, k * C : (k + 1) * C]
        h = jnp.concatenate([h, h], axis=1)
        products.append(wide[:, k, :] * jnp.concatenate([h] * 32, axis=1))
    high, low = split(jnp.concatenate(products, axis=0))
    out = dot(jnp.concatenate([high, low], axis=0), fold[...])
    out = (out[:16] + out[16:]) * SCALE_A
    return jnp.concatenate([out[k * 4 : (k + 1) * 4] for k in range(4)], axis=1)


def sum_of(got):
    v = [got[i] for i in range(got.shape[0])]
    while len(v) > 1:
        v = [v[i] + v[i + 1] for i in range(0, len(v), 2)]
    return v[0]


def mix_two_kernel(at, got, spectral, fold, back, hat_out, wide):
    hat = sum_of(got) * SCALE_B
    hat_out[...] = hat
    out = mixed(hat, spectral, wide, fold)
    for i in range(64):
        back[i] = out


def mix_one_kernel(at, got, spectral, fold, back, hat_out, mid_out, first_out, wide):
    v = sum_of(got)
    hat = v[:, :256] * SCALE_B
    hat_out[...] = hat
    mid_out[...] = v[:, 256:512] * SCALE_A
    first_out[...] = v[:, 512:768] * SCALE_A
    out = mixed(hat, spectral, wide, fold)
    for i in range(64):
        back[i, :, :256] = out
        back[i, :, 256:] = v[:, 768:]


def outer_kernel(at, left, right, fold, out):
    lefts = []
    rights = []
    for k in range(4):
        cut = slice(k * C, (k + 1) * C)
        h = right[:, cut]
        lefts.append(left[:, cut])
        rights.append(jnp.concatenate([h, h], axis=1))
    v = jnp.concatenate(lefts, axis=0)
    high, rest = v.astype(bf16), v - v.astype(bf16).astype(f32)
    low, last = split(rest)
    spread_left = dot_nt(jnp.concatenate([high, low, last], axis=0), fold[...])
    tall = jnp.concatenate(rights, axis=0)
    whole = (spread_left[:16] + spread_left[16:32]) + spread_left[32:]
    whole = whole * jnp.concatenate([tall] * 32, axis=1)
    for k in range(4):
        out[:, k, :] = whole[k * 4 : (k + 1) * 4]


def stack_modes(refs, modes):
    for j, ref in enumerate(refs):
        modes[:, j * 256 : (j + 1) * 256] = ref[:ROWS].astype(bf16)


def middle_kernel(
    at, local_from, slope_from, a, b, c, d, mine, mine_back, dz_to, p1, p2, p3,
    modes, total, dz, ka, ka_back, local, slope, sems,
):
    def copies(i):
        cut = block(i)
        return (
            pltpu.make_async_copy(local_from.at[:, cut], local.at[:, cut], sems.at[i]),
            pltpu.make_async_copy(slope_from.at[:, cut], slope.at[:, cut], sems.at[8 + i]),
        )

    def leave(i):
        return pltpu.make_async_copy(dz.at[:, block(i)], dz_to.at[:, block(i)], sems.at[16 + i])

    for i in range(8):
        for copy in copies(i):
            copy.start()
    stack_modes((a, b, c, d), modes)
    total[...] = jnp.zeros_like(total)
    fill_back(ka_back, mine_back, 0)
    for i in range(9):
        if i < 8:
            if i < 7:
                fill_back(ka_back, mine_back, i + 1)
            fill_table(ka, mine, i)
            for copy in copies(i):
                copy.wait()
            down = dot(modes[...], ka_back[:, block(i)]) + local[:, block(i)]
            dz[:, block(i)] = (down * slope[:, block(i)]).astype(bf16)
            leave(i).start()
        if i > 0:
            total[...] += dot(dz[:, block(i - 1)], ka[block(i - 1), 256:])
    store_parts(total[...], (p1, p2, p3))
    for i in range(8):
        leave(i).wait()


def end_kernel(
    at, a, b, c, d, mine, local, out_to, weight_two, weight_one, modes, out, ka, sems
):
    def leave(i):
        return pltpu.make_async_copy(out.at[:, block(i)], out_to.at[:, block(i)], sems.at[i])

    stack_modes((a, b, c, d), modes)
    fill_back(ka, mine, 0)
    for i in range(8):
        if i < 7:
            fill_back(ka, mine, i + 1)
        down = dot(modes[...], ka[:, block(i)]) + local[:, block(i)]
        out[:, block(i)] = down.astype(bf16)
        leave(i).start()
    w = (a[ROWS:] + b[ROWS:]) + (c[ROWS:] + d[ROWS:])
    w = jnp.concatenate([w[:, :128], w[:, 128:]], axis=0)
    weight_two[...] = w[:, :C]
    weight_one[...] = w[:, C:]
    for i in range(8):
        leave(i).wait()


def shift_pairs(kind, s):
    return kind, [(i, i ^ s if kind == "gy" else (i + s) % 4) for i in range(4)]


def shifted(v, kind, s):
    axis, pairs = shift_pairs(kind, s)
    return lax.ppermute(v, axis, pairs)


def exchange(parts, kind):
    return [parts[0]] + [shifted(parts[s], kind, s) for s in (1, 2, 3)]


def spread(v, kind):
    return [v] + [shifted(v, kind, s) for s in (3, 2, 1)]


def reduce_y(at, near, far, width):
    keep, send = call(
        keep_kernel, [((32, width), f32)] * 2, at, near, shifted(far, "gy", 1)
    )
    return keep, shifted(send, "gy", 2)


def over(v, axes):
    return lax.all_to_all(v, axes, 0, 0, tiled=True)


def on_device(
    grid_input, pre_one, pre_two, grad_output, spectral_one, spectral_two, point_one, point_two
):
    tz, tz_back, ty, flat, tx, few = [jnp.asarray(t) for t in build_tables()]
    at = lax.axis_index(("gz", "gy", "gx")).reshape(1)
    first, pre_one, pre_two, upstream = [
        t.reshape(ROWS, WIDE) for t in (grid_input, pre_one, pre_two, grad_output)
    ]
    big = (ROWS, WIDE)
    half = ((ROWS, 256), f32)
    table = ((WIDE, 16 * C), bf16)
    table_back = ((16 * C, WIDE), bf16)
    native = ((4, 4, C * C), f32)
    dma = pltpu.SemaphoreType.DMA

    dz_two, *parts, mine, mine_back = call(
        start_kernel,
        [(big, bf16, "raw")] + [half] * 3 + [((CELLS_Z, 16 * C), f32), ((16, WIDE), f32)],
        at,
        pre_two,
        upstream,
        tz,
        tz_back,
        raw=4,
        scratch=[
            table,
            ((ROWS, 12 * C), f32),
            (big, bf16),
            (big, bf16),
            (big, bf16),
            ((CELLS_Z, 16 * C), bf16),
            ((16, WIDE), bf16),
            dma((26,)),
        ],
    )
    own, fold, coef = call(
        own_kernel,
        [half, ((C * C, C), bf16), ((128, 128), f32)],
        at,
        mine,
        dz_two,
        few,
        scratch=[((WIDE, 256), bf16)],
    )
    got = exchange([own] + parts, "gx")
    slope, local_two, weight_two, *ins = call(
        side_kernel,
        [(big, f32, "raw")] * 2 + [((C, C), f32, 0)] + [((ROWS, 512), f32)] * 4,
        at,
        pre_one,
        first,
        dz_two,
        mine,
        point_two,
        limit=14,
        scratch=[
            table,
            ((2 * ROWS, WIDE), bf16),
            ((2 * ROWS, 16 * C), f32),
            ((256, 256), f32),
            ((256, 256), bf16),
            (big, f32),
            (big, f32),
            dma((16,)),
        ],
    )
    got, ins, slope, local_two = lax.optimization_barrier((got, ins, slope, local_two))
    (modes,) = call(along_yx_kernel, [((64, 4, 256), f32)], at, *got, flat, coef)
    got = over(modes, ("gz", "gy"))
    got_in = exchange(ins, "gx")
    back, hat_two = call(
        mix_two_kernel,
        [((64, 4, 256), f32), ((4, 256), f32)],
        at,
        got,
        spectral_two,
        fold,
        scratch=[native],
    )
    got = over(back, ("gz", "gy"))
    (tall,) = call(back_xy_kernel, [half], at, got, flat, coef, scratch=[half])
    got = spread(tall, "gx")
    ins = call(along_y_kernel, [((64, 512), f32)] * 2, at, *got_in, ty)
    dz_one, *parts = call(
        middle_kernel,
        [(big, bf16, "raw")] + [half] * 3,
        at,
        local_two,
        slope,
        *got,
        mine,
        mine_back,
        raw=2,
        limit=16,
        scratch=[
            ((ROWS, 16 * C), bf16),
            ((ROWS, 12 * C), f32),
            (big, bf16),
            table,
            table_back,
            (big, f32),
            (big, f32),
            dma((24,)),
        ],
    )
    sent, own = call(
        side_one_kernel,
        [((32, 256), f32), half],
        at,
        first,
        dz_one,
        mine,
        weight_two,
        scratch=[((WIDE, 256), bf16)],
    )
    got = exchange([own] + parts, "gx")
    near, far = call(along_y_join_kernel, [((64, 1024), f32)] * 2, at, *got, ty, *ins, sent)
    got = reduce_y(at, near, far, 1024)
    (modes,) = call(along_x_kernel, [((16, 4, 896), f32)], at, *got, tx)
    back, hat_one, mid_hat, first_hat = call(
        mix_one_kernel,
        [((64, 4, 384), f32)] + [((4, 256), f32)] * 3,
        at,
        over(modes, "gz"),
        spectral_one,
        fold,
        scratch=[native],
    )
    (spec_two,) = call(outer_kernel, [(*native, 0)], at, mid_hat, hat_two, fold)
    (spec_one,) = call(outer_kernel, [(*native, 0)], at, first_hat, hat_one, fold)
    back, dz_late = lax.optimization_barrier((back, dz_one))
    (local_one,) = call(
        local_kernel,
        [(big, f32, "raw")],
        at,
        dz_late,
        point_one,
        scratch=[((256, 256), bf16), (big, f32), dma((8,))],
    )
    got = over(back, ("gz", "gy"))
    got, local_one = lax.optimization_barrier((got, local_one))
    (tall,) = call(
        back_xy_one_kernel, [((ROWS + 32, 256), f32)], at, got, flat, coef, scratch=[half]
    )
    got = spread(tall, "gx")
    input_grad, weight_two, weight_one = call(
        end_kernel,
        [(big, bf16, "raw"), ((C, C), f32, 0), ((C, C), f32, 0)],
        at,
        *got,
        mine_back,
        local_one,
        scratch=[((ROWS, 16 * C), bf16), (big, bf16), table_back, dma((8,))],
    )
    return (
        input_grad.reshape(CELLS_X, CELLS_Y, WIDE),
        spec_one[None],
        spec_two[None],
        weight_one,
        weight_two,
    )


def solution(mesh):
    grid = P("gz", "gy", "gx")
    modes = P("gz", "gy", "gx", None)
    return jax.shard_map(
        on_device,
        mesh=mesh,
        in_specs=(grid, grid, grid, grid, modes, modes, P(), P()),
        out_specs=(grid, modes, modes, P(), P()),
        check_vma=False,
    )
```

```python
import jax
import jax.numpy as jnp
import numpy as np
from jax import lax
from jax.experimental import pallas as pl
from jax.experimental.pallas import tpu as pltpu
from jax.sharding import PartitionSpec as P


INTERPRET = False

C = 64
CELLS_X, CELLS_Y, CELLS_Z = 8, 16, 32
DEV_X, DEV_Y, DEV_Z = 16, 4, 4
ROWS = CELLS_X * CELLS_Y
WIDE = CELLS_Z * C
TOTAL_CELLS = CELLS_X * DEV_X * CELLS_Y * DEV_Y * CELLS_Z * DEV_Z
TOTAL_MODES = 16**3
SCALE_A = (TOTAL_CELLS * TOTAL_MODES) ** (-0.25)
SCALE_B = TOTAL_CELLS ** (-0.5)

inv_root_two = 0.7071067811865476
inv_root_tau = 0.3989422804014327
bf16 = jnp.bfloat16
f32 = jnp.float32


def cas(mode, length, position):
    mode = np.asarray(mode)
    freq = np.where(mode < 8, mode, length - 16 + mode)
    phase = (freq * position % length) * (2.0 * np.pi / length)
    return (np.cos(phase) + np.sin(phase)).astype(np.float32)


def build_tables():
    four = np.arange(4)
    z = np.arange(CELLS_Z)
    tz = np.zeros((DEV_Z, CELLS_Z, 16), np.float32)
    for d in range(DEV_Z):
        modes = (((d + four) % 4)[:, None] * 4 + four[None, :]).reshape(-1)
        tz[d] = cas(modes[None, :], CELLS_Z * DEV_Z, z[:, None] * DEV_Z + d)
    tz_back = np.repeat(tz.transpose(0, 2, 1), C, axis=2)
    tz = np.repeat(tz, C, axis=2)
    y = np.arange(CELLS_Y)
    ty = np.zeros((DEV_Y, 4, CELLS_X, 4, CELLS_X, CELLS_Y), np.float32)
    for d in range(DEV_Y):
        modes = (d ^ np.array([0, 2, 1, 3]))[:, None] * 4 + four[None, :]
        small = cas(modes[:, :, None], CELLS_Y * DEV_Y, y * DEV_Y + d)
        for x in range(CELLS_X):
            ty[d, :, x, :, x, :] = small
    ty = ty.reshape(DEV_Y, ROWS, ROWS)
    flat = np.zeros((DEV_Y, CELLS_X, 16, CELLS_X, CELLS_Y), np.float32)
    for d in range(DEV_Y):
        for x in range(CELLS_X):
            flat[d, x, :, x] = cas(np.arange(16)[:, None], CELLS_Y * DEV_Y, y * DEV_Y + d)
    flat = flat.reshape(DEV_Y, ROWS, ROWS)
    x = np.arange(CELLS_X)
    tx = np.zeros((DEV_X, 16, 4, CELLS_X, 4), np.float32)
    few = np.zeros((DEV_X, 16, CELLS_X), np.float32)
    for d in range(DEV_X):
        small = cas(np.arange(16)[:, None], CELLS_X * DEV_X, x * DEV_X + d)
        few[d] = small
        for l in range(4):
            tx[d, :, l, :, l] = small
    tx = tx.reshape(DEV_X, 64, CELLS_X * 4).transpose(0, 2, 1)
    return tuple(t.astype(bf16) for t in (tz, tz_back, ty, flat, tx)) + (
        few.reshape(DEV_X, 128).astype(bf16).astype(np.float32),
    )


def dot(left, right):
    return jnp.dot(left, right, preferred_element_type=f32)


def dot_nt(left, right):
    return lax.dot_general(left, right, (((1,), (1,)), ((), ())), preferred_element_type=f32)


def dot_tn(left, right):
    return lax.dot_general(left, right, (((0,), (0,)), ((), ())), preferred_element_type=f32)


def split(v):
    high = v.astype(bf16)
    return high, (v - high.astype(f32)).astype(bf16)


def table_dot(table, v):
    high, low = split(v)
    return dot(table, high) + dot(table, low)


def table_dot_tn(table, v):
    high, low = split(v)
    return dot_tn(table, high) + dot_tn(table, low)


def slope_of(v, cdf):
    return cdf + v * jnp.exp(-0.5 * v * v) * inv_root_tau


def cdf_of(v):
    return 0.5 * (1.0 + lax.erf(v * inv_root_two))


def call(body, outs, *args, scratch=(), limit=8, raw=0):
    near = args[1 : 1 + raw]
    rest = args[1 + raw :]
    shapes = [pltpu.VMEM(*o) if len(o) == 2 else jax.ShapeDtypeStruct(*o[:2]) for o in outs]
    shapes = [pltpu.HBM(*o[:2]) if "raw" in o else v for o, v in zip(outs, shapes)]
    if INTERPRET:
        shapes = [jax.ShapeDtypeStruct(*o[:2]) for o in outs]
    else:
        near = [pltpu.with_memory_space_constraint(a, pltpu.HBM) for a in near]
        rest = [pltpu.with_memory_space_constraint(a, pltpu.VMEM) for a in rest]
    return pl.pallas_call(
        body,
        out_shape=shapes,
        in_specs=[pl.BlockSpec(memory_space=pltpu.SMEM)]
        + [pl.BlockSpec(memory_space=pl.ANY if INTERPRET else pltpu.HBM)] * raw
        + [pl.BlockSpec(memory_space=pltpu.VMEM)] * len(rest),
        out_specs=[
            pl.BlockSpec(memory_space=(pl.ANY if INTERPRET else pltpu.HBM) if "raw" in o else pltpu.VMEM)
            for o in outs
        ],
        scratch_shapes=[pltpu.VMEM(*s) if isinstance(s, tuple) else s for s in scratch],
        interpret=INTERPRET,
        compiler_params=pltpu.CompilerParams(vmem_limit_bytes=limit << 20),
    )(*args[:1], *near, *rest)


def at_x(at):
    return at[0] >> 4


def at_y(at):
    return (at[0] >> 2) & 3


def at_z(at):
    return at[0] & 3


def block(b):
    return slice(b * 256, (b + 1) * 256)


def store_parts(v, refs):
    for j, ref in enumerate(refs):
        ref[...] = v[:, j * 256 : (j + 1) * 256]


def fill_table(ka, mine, b, wide=16 * C):
    lane = lax.broadcasted_iota(jnp.int32, (C, wide), 1) & (C - 1)
    row = lax.broadcasted_iota(jnp.int32, (C, wide), 0)
    eye = jnp.where(lane == row, 1.0, 0.0)
    for z in range(4 * b, 4 * b + 4):
        ka[z * C : (z + 1) * C, :] = (eye * mine[z : z + 1, :wide]).astype(bf16)


def fill_back(ka, mine, b):
    lane = lax.broadcasted_iota(jnp.int32, (C, 256), 1) & (C - 1)
    row = lax.broadcasted_iota(jnp.int32, (C, 256), 0)
    eye = jnp.where(lane == row, 1.0, 0.0)
    for k in range(16):
        ka[k * C : (k + 1) * C, block(b)] = (eye * mine[k : k + 1, block(b)]).astype(bf16)


def start_kernel(
    at, pre_from, grad_from, tz, tz_back, dz_to, p1, p2, p3, mine, mine_back,
    ka, total, pre, grad, dz, short, short_back, sems,
):
    def copies(b):
        cut = block(b)
        return (
            pltpu.make_async_copy(pre_from.at[:, cut], pre.at[:, cut], sems.at[b]),
            pltpu.make_async_copy(grad_from.at[:, cut], grad.at[:, cut], sems.at[8 + b]),
        )

    def leave(b):
        return pltpu.make_async_copy(dz.at[:, block(b)], dz_to.at[:, block(b)], sems.at[17 + b])

    first = pltpu.make_async_copy(tz.at[at_z(at)], short, sems.at[16])
    first.start()
    for b in range(8):
        for copy in copies(b):
            copy.start()
    second = pltpu.make_async_copy(tz_back.at[at_z(at)], short_back, sems.at[25])
    second.start()
    first.wait()
    mine[...] = short[...].astype(f32)
    total[...] = jnp.zeros_like(total)
    for b in range(9):
        if b < 8:
            fill_table(ka, mine, b)
            for copy in copies(b):
                copy.wait()
            v = pre[:, block(b)].astype(f32)
            slope = slope_of(v, cdf_of(v))
            dz[:, block(b)] = (grad[:, block(b)].astype(f32) * slope).astype(bf16)
            leave(b).start()
        if b > 0:
            total[...] += dot(dz[:, block(b - 1)], ka[block(b - 1), 256:])
    store_parts(total[...], (p1, p2, p3))
    second.wait()
    mine_back[...] = short_back[...].astype(f32)
    for b in range(8):
        leave(b).wait()


def own_kernel(at, mine, dz, few, p0, fold, coef, ka):
    side = lax.broadcasted_iota(jnp.int32, (128, 128), 0)
    same = jnp.where(side == lax.broadcasted_iota(jnp.int32, (128, 128), 1), 1.0, 0.0)
    same = (same * few[pl.ds(at_x(at), 1), :]).astype(bf16)
    coef[...] = dot(same, jnp.ones((128, 128), bf16))
    for b in range(8):
        fill_table(ka, mine, b, 256)
    p0[...] = dot(dz[...], ka[...])
    row = lax.broadcasted_iota(jnp.int32, (256, C), 0) >> 6
    lane = lax.broadcasted_iota(jnp.int32, (256, C), 1)
    for r in range(16):
        fold[r * 256 : (r + 1) * 256, :] = jnp.where(lane == row + 4 * r, 1.0, 0.0).astype(bf16)


def fill_point(square, point):
    square[...] = jnp.zeros_like(square)
    for i in range(4):
        square[i * C : (i + 1) * C, i * C : (i + 1) * C] = point[...]


def diagonal_sum(total):
    return sum(total[i * C : (i + 1) * C, i * C : (i + 1) * C] for i in range(4))


def side_kernel(
    at, pre, first, dz, mine, point, slope_to, local_to, weight, q0, q1, q2, q3,
    ka, mid, own, squares, square, slope, local, sems,
):
    fill_point(square, point)

    def leave(b):
        cut = block(b)
        return (
            pltpu.make_async_copy(slope.at[:, cut], slope_to.at[:, cut], sems.at[b]),
            pltpu.make_async_copy(local.at[:, cut], local_to.at[:, cut], sems.at[8 + b]),
        )

    own[...] = jnp.zeros_like(own)
    squares[...] = jnp.zeros_like(squares)
    for b in range(9):
        if b < 8:
            cut = block(b)
            fill_table(ka, mine, b)
            v = pre[:, cut].astype(f32)
            cdf = cdf_of(v)
            slope[:, cut] = slope_of(v, cdf)
            mid[:ROWS, cut] = (v * cdf).astype(bf16)
            mid[ROWS:, cut] = first[:, cut]
            local[:, cut] = dot_nt(dz[:, cut], square[...])
            for copy in leave(b):
                copy.start()
        if b > 0:
            cut = block(b - 1)
            squares[...] += dot_tn(mid[:ROWS, cut], dz[:, cut])
            own[...] += dot(mid[:, cut], ka[cut, :])
    weight[...] = diagonal_sum(squares[...])
    for j, ref in enumerate((q0, q1, q2, q3)):
        ref[:, :256] = own[:ROWS, j * 256 : (j + 1) * 256]
        ref[:, 256:] = own[ROWS:, j * 256 : (j + 1) * 256]
    for b in range(8):
        for copy in leave(b):
            copy.wait()


def side_one_kernel(at, first, dz, mine, weight_two, sent, p0, ka):
    for b in range(8):
        fill_table(ka, mine, b, 256)
    squares = dot_tn(first[:, :256], dz[:, :256])
    for b in range(1, 8):
        squares = squares + dot_tn(first[:, block(b)], dz[:, block(b)])
    p0[...] = dot(dz[...], ka[...])
    both = jnp.concatenate([weight_two[...], diagonal_sum(squares)], axis=1) * SCALE_B
    sent[...] = jnp.concatenate([both[:32], both[32:]], axis=1)


def local_kernel(at, dz, point, local_to, square, local, sems):
    fill_point(square, point)

    def leave(b):
        return pltpu.make_async_copy(local.at[:, block(b)], local_to.at[:, block(b)], sems.at[b])

    for b in range(8):
        local[:, block(b)] = dot_nt(dz[:, block(b)], square[...])
        leave(b).start()
    for b in range(8):
        leave(b).wait()


def total_of(refs):
    return (refs[0][...] + refs[1][...]) + (refs[2][...] + refs[3][...])


def factor(coef, k, x):
    c = coef[k * 8 + x : k * 8 + x + 1, :]
    return jnp.concatenate([c, c], axis=1)


def along_yx_kernel(at, a, b, c, d, flat, coef, out):
    v = table_dot(flat[at_y(at)], total_of((a, b, c, d)))
    for k in range(16):
        here = factor(coef, k, 0) * v[:16]
        for x in range(1, 8):
            here = here + factor(coef, k, x) * v[x * 16 : (x + 1) * 16]
        for g in range(4):
            out[k * 4 + g] = here[g * 4 : (g + 1) * 4]


def back_xy(at, got, flat, coef, tall):
    for k in range(16):
        here = jnp.concatenate([got[k * 4 + g, :, :256] for g in range(4)], axis=0)
        for x in range(8):
            rows = slice(x * 16, (x + 1) * 16)
            more = factor(coef, k, x) * here
            tall[rows] = more if k == 0 else tall[rows] + more
    return table_dot_tn(flat[at_y(at)], tall[...])


def back_xy_kernel(at, got, flat, coef, out, tall):
    out[...] = back_xy(at, got, flat, coef, tall)


def back_xy_one_kernel(at, got, flat, coef, out, tall):
    out[:ROWS] = back_xy(at, got, flat, coef, tall)
    weight = jnp.concatenate([got[k * 4, :, 256:] for k in range(16)], axis=0)
    out[ROWS:] = jnp.concatenate([weight[:32], weight[32:]], axis=1)


def along_y_kernel(at, a, b, c, d, ty, near, far):
    out = table_dot(ty[at_y(at)], total_of((a, b, c, d)))
    near[...] = out[:64]
    far[...] = out[64:]


def along_y_join_kernel(at, a, b, c, d, ty, ins_near, ins_far, sent, near, far):
    out = table_dot(ty[at_y(at)], total_of((a, b, c, d)))
    for ref, ins, here in ((near, ins_near, out[:64]), (far, ins_far, out[64:])):
        ref[:, :256] = here
        ref[:, 256:768] = ins[...]
        ref[:32, 768:] = sent[...]
        ref[32:, 768:] = jnp.zeros((32, 256), f32)


def keep_kernel(at, near, got, keep, send):
    v = near[...] + got[...]
    keep[...] = v[:32]
    wide = min(v.shape[1], 768)
    send[:, :wide] = v[32:, :wide]
    if v.shape[1] > 768:
        send[:, 768:] = v[:32, 768:]


def along_x_kernel(at, a, b, tx, out):
    v = a[...] + b[...]
    modes = table_dot_tn(tx[at_x(at)], v[:, : min(v.shape[1], 768)])
    for i in range(16):
        out[i, :, : modes.shape[1]] = modes[i * 4 : (i + 1) * 4]
    if v.shape[1] > 768:
        weight = jnp.concatenate([v[:, 768:896], v[:, 896:]], axis=0)
        for i in range(16):
            out[i, :, 768:] = weight[i * 4 : (i + 1) * 4]


def mixed(hat, spectral, wide, fold):
    wide[...] = spectral[0].astype(f32)
    products = []
    for k in range(4):
        h = hat[:, k * C : (k + 1) * C]
        h = jnp.concatenate([h, h], axis=1)
        products.append(wide[:, k, :] * jnp.concatenate([h] * 32, axis=1))
    high, low = split(jnp.concatenate(products, axis=0))
    out = dot(jnp.concatenate([high, low], axis=0), fold[...])
    out = (out[:16] + out[16:]) * SCALE_A
    return jnp.concatenate([out[k * 4 : (k + 1) * 4] for k in range(4)], axis=1)


def sum_of(got):
    v = [got[i] for i in range(got.shape[0])]
    while len(v) > 1:
        v = [v[i] + v[i + 1] for i in range(0, len(v), 2)]
    return v[0]


def mix_two_kernel(at, got, spectral, fold, back, hat_out, wide):
    hat = sum_of(got) * SCALE_B
    hat_out[...] = hat
    out = mixed(hat, spectral, wide, fold)
    for i in range(64):
        back[i] = out


def mix_one_kernel(at, got, spectral, fold, back, hat_out, mid_out, first_out, wide):
    v = sum_of(got)
    hat = v[:, :256] * SCALE_B
    hat_out[...] = hat
    mid_out[...] = v[:, 256:512] * SCALE_A
    first_out[...] = v[:, 512:768] * SCALE_A
    out = mixed(hat, spectral, wide, fold)
    for i in range(64):
        back[i, :, :256] = out
        back[i, :, 256:] = v[:, 768:]


def outer_kernel(at, left, right, fold, out):
    lefts = []
    rights = []
    for k in range(4):
        cut = slice(k * C, (k + 1) * C)
        h = right[:, cut]
        lefts.append(left[:, cut])
        rights.append(jnp.concatenate([h, h], axis=1))
    v = jnp.concatenate(lefts, axis=0)
    high, rest = v.astype(bf16), v - v.astype(bf16).astype(f32)
    low, last = split(rest)
    spread_left = dot_nt(jnp.concatenate([high, low, last], axis=0), fold[...])
    tall = jnp.concatenate(rights, axis=0)
    whole = (spread_left[:16] + spread_left[16:32]) + spread_left[32:]
    whole = whole * jnp.concatenate([tall] * 32, axis=1)
    for k in range(4):
        out[:, k, :] = whole[k * 4 : (k + 1) * 4]


def stack_modes(refs, modes):
    for j, ref in enumerate(refs):
        modes[:, j * 256 : (j + 1) * 256] = ref[:ROWS].astype(bf16)


def middle_kernel(
    at, local_from, slope_from, a, b, c, d, mine, mine_back, dz_to, p1, p2, p3,
    modes, total, dz, ka, ka_back, local, slope, sems,
):
    def copies(i):
        cut = block(i)
        return (
            pltpu.make_async_copy(local_from.at[:, cut], local.at[:, cut], sems.at[i]),
            pltpu.make_async_copy(slope_from.at[:, cut], slope.at[:, cut], sems.at[8 + i]),
        )

    def leave(i):
        return pltpu.make_async_copy(dz.at[:, block(i)], dz_to.at[:, block(i)], sems.at[16 + i])

    for i in range(8):
        for copy in copies(i):
            copy.start()
    stack_modes((a, b, c, d), modes)
    total[...] = jnp.zeros_like(total)
    fill_back(ka_back, mine_back, 0)
    for i in range(9):
        if i < 8:
            if i < 7:
                fill_back(ka_back, mine_back, i + 1)
            fill_table(ka, mine, i)
            for copy in copies(i):
                copy.wait()
            down = dot(modes[...], ka_back[:, block(i)]) + local[:, block(i)]
            dz[:, block(i)] = (down * slope[:, block(i)]).astype(bf16)
            leave(i).start()
        if i > 0:
            total[...] += dot(dz[:, block(i - 1)], ka[block(i - 1), 256:])
    store_parts(total[...], (p1, p2, p3))
    for i in range(8):
        leave(i).wait()


def end_kernel(
    at, a, b, c, d, mine, local, out_to, weight_two, weight_one, modes, out, ka, sems
):
    def leave(i):
        return pltpu.make_async_copy(out.at[:, block(i)], out_to.at[:, block(i)], sems.at[i])

    stack_modes((a, b, c, d), modes)
    fill_back(ka, mine, 0)
    for i in range(8):
        if i < 7:
            fill_back(ka, mine, i + 1)
        down = dot(modes[...], ka[:, block(i)]) + local[:, block(i)]
        out[:, block(i)] = down.astype(bf16)
        leave(i).start()
    w = (a[ROWS:] + b[ROWS:]) + (c[ROWS:] + d[ROWS:])
    w = jnp.concatenate([w[:, :128], w[:, 128:]], axis=0)
    weight_two[...] = w[:, :C]
    weight_one[...] = w[:, C:]
    for i in range(8):
        leave(i).wait()


def shift_pairs(kind, s):
    return kind, [(i, i ^ s if kind == "gy" else (i + s) % 4) for i in range(4)]


def shifted(v, kind, s):
    axis, pairs = shift_pairs(kind, s)
    return lax.ppermute(v, axis, pairs)


def exchange(parts, kind):
    far = shifted(parts[2], kind, 2)
    return [parts[0], shifted(parts[1], kind, 1), far, shifted(parts[3], kind, 3)]


def spread(v, kind):
    far = shifted(v, kind, 2)
    return [v, shifted(v, kind, 3), far, shifted(v, kind, 1)]


def reduce_y(at, near, far, width):
    keep, send = call(
        keep_kernel, [((32, width), f32)] * 2, at, near, shifted(far, "gy", 1)
    )
    return keep, shifted(send, "gy", 2)


def over(v, axes):
    return lax.all_to_all(v, axes, 0, 0, tiled=True)


def on_device(
    grid_input, pre_one, pre_two, grad_output, spectral_one, spectral_two, point_one, point_two
):
    tz, tz_back, ty, flat, tx, few = [jnp.asarray(t) for t in build_tables()]
    at = lax.axis_index(("gz", "gy", "gx")).reshape(1)
    first, pre_one, pre_two, upstream = [
        t.reshape(ROWS, WIDE) for t in (grid_input, pre_one, pre_two, grad_output)
    ]
    big = (ROWS, WIDE)
    half = ((ROWS, 256), f32)
    table = ((WIDE, 16 * C), bf16)
    table_back = ((16 * C, WIDE), bf16)
    native = ((4, 4, C * C), f32)
    dma = pltpu.SemaphoreType.DMA

    dz_two, *parts, mine, mine_back = call(
        start_kernel,
        [(big, bf16, "raw")] + [half] * 3 + [((CELLS_Z, 16 * C), f32), ((16, WIDE), f32)],
        at,
        pre_two,
        upstream,
        tz,
        tz_back,
        raw=4,
        scratch=[
            table,
            ((ROWS, 12 * C), f32),
            (big, bf16),
            (big, bf16),
            (big, bf16),
            ((CELLS_Z, 16 * C), bf16),
            ((16, WIDE), bf16),
            dma((26,)),
        ],
    )
    own, fold, coef = call(
        own_kernel,
        [half, ((C * C, C), bf16), ((128, 128), f32)],
        at,
        mine,
        dz_two,
        few,
        scratch=[((WIDE, 256), bf16)],
    )
    got = exchange([own] + parts, "gx")
    (modes,) = call(along_yx_kernel, [((64, 4, 256), f32)], at, *got, flat, coef)
    modes, pre_one, dz_side = lax.optimization_barrier((modes, pre_one, dz_two))
    slope, local_two, weight_two, *ins = call(
        side_kernel,
        [(big, f32, "raw")] * 2 + [((C, C), f32, 0)] + [((ROWS, 512), f32)] * 4,
        at,
        pre_one,
        first,
        dz_side,
        mine,
        point_two,
        limit=14,
        scratch=[
            table,
            ((2 * ROWS, WIDE), bf16),
            ((2 * ROWS, 16 * C), f32),
            ((256, 256), f32),
            ((256, 256), bf16),
            (big, f32),
            (big, f32),
            dma((16,)),
        ],
    )
    got = over(modes, ("gz", "gy"))
    got, ins = lax.optimization_barrier((got, ins))
    got_in = exchange(ins, "gx")
    back, hat_two = call(
        mix_two_kernel,
        [((64, 4, 256), f32), ((4, 256), f32)],
        at,
        got,
        spectral_two,
        fold,
        scratch=[native],
    )
    got = over(back, ("gz", "gy"))
    (tall,) = call(back_xy_kernel, [half], at, got, flat, coef, scratch=[half])
    got = spread(tall, "gx")
    ins = call(along_y_kernel, [((64, 512), f32)] * 2, at, *got_in, ty)
    dz_one, *parts = call(
        middle_kernel,
        [(big, bf16, "raw")] + [half] * 3,
        at,
        local_two,
        slope,
        *got,
        mine,
        mine_back,
        raw=2,
        limit=16,
        scratch=[
            ((ROWS, 16 * C), bf16),
            ((ROWS, 12 * C), f32),
            (big, bf16),
            table,
            table_back,
            (big, f32),
            (big, f32),
            dma((24,)),
        ],
    )
    sent, own = call(
        side_one_kernel,
        [((32, 256), f32), half],
        at,
        first,
        dz_one,
        mine,
        weight_two,
        scratch=[((WIDE, 256), bf16)],
    )
    got = exchange([own] + parts, "gx")
    near, far = call(along_y_join_kernel, [((64, 1024), f32)] * 2, at, *got, ty, *ins, sent)
    got = reduce_y(at, near, far, 1024)
    (modes,) = call(along_x_kernel, [((16, 4, 896), f32)], at, *got, tx)
    back, hat_one, mid_hat, first_hat = call(
        mix_one_kernel,
        [((64, 4, 384), f32)] + [((4, 256), f32)] * 3,
        at,
        over(modes, "gz"),
        spectral_one,
        fold,
        scratch=[native],
    )
    (spec_two,) = call(outer_kernel, [(*native, 0)], at, mid_hat, hat_two, fold)
    (spec_one,) = call(outer_kernel, [(*native, 0)], at, first_hat, hat_one, fold)
    back, dz_late = lax.optimization_barrier((back, dz_one))
    (local_one,) = call(
        local_kernel,
        [(big, f32, "raw")],
        at,
        dz_late,
        point_one,
        scratch=[((256, 256), bf16), (big, f32), dma((8,))],
    )
    got = over(back, ("gz", "gy"))
    got, local_one = lax.optimization_barrier((got, local_one))
    (tall,) = call(
        back_xy_one_kernel, [((ROWS + 32, 256), f32)], at, got, flat, coef, scratch=[half]
    )
    got = spread(tall, "gx")
    input_grad, weight_two, weight_one = call(
        end_kernel,
        [(big, bf16, "raw"), ((C, C), f32, 0), ((C, C), f32, 0)],
        at,
        *got,
        mine_back,
        local_one,
        scratch=[((ROWS, 16 * C), bf16), (big, bf16), table_back, dma((8,))],
    )
    return (
        input_grad.reshape(CELLS_X, CELLS_Y, WIDE),
        spec_one[None],
        spec_two[None],
        weight_one,
        weight_two,
    )


def solution(mesh):
    grid = P("gz", "gy", "gx")
    modes = P("gz", "gy", "gx", None)
    return jax.shard_map(
        on_device,
        mesh=mesh,
        in_specs=(grid, grid, grid, grid, modes, modes, P(), P()),
        out_specs=(grid, modes, modes, P(), P()),
        check_vma=False,
    )
```
